32 devices in a mesh: axial: 8 (over y, x, core), azim: 4 (over z).
Axes of the slice: x: 2, y: 2, z: 4, core: 2. Of those that a mesh axis runs over, the one named last changes fastest.
Arguments:
- state: float32 [5, 16, 1024, 96], P(None, 'axial', 'azim'), as said below
- start: float32 [5, 16, 1024, 96], P(None, 'axial', 'azim'), as said below
- modes: int32 [64], replicated, may hold values from 1 to 512, as said below
Outputs:
- section: float32 [5, 16, 1024, 96], P(None, 'axial', 'azim')
The draws below stay inside these ranges and needn't reach their ends.
Inputs may be any that keep to these rules, and one draw needn't show every extreme that they name: Cycle j keeps the modes 0 to modes[j] - 1; modes[j] lies between 8 * (j + 1) and 2 * 8 * (j + 1), capped at 512, which the last cycle reaches. `state`: the density (field 0) lies between 0.85 and 1.15. `start`: the density (field 0) lies between 0.85 and 1.15.
All inputs are finite; a program needn't handle non-finite values.
Results may differ from the reference program's by a relative error of at most 0.00005.
Values sent between devices are 32-bit elements; how exact they have to be, the bound alone decides.
A program may use at most 64 MiB of HBM per device.

```python
import math
import jax
import jax.numpy as jnp
from jax import lax

NTH = 1024
NR = 96
NIN = 64
X_DEV = 2
NA = 16
MSTEP = 8
N_AXIAL = 8


GAMMA = 1.4


def make_state(key):
    keys = jax.random.split(key, 5)
    shape = (NA, NTH, NR)
    density = 1.0 + jax.random.uniform(keys[0], shape, jnp.float32, -0.15, 0.15)
    axial_speed = 1.5 + 0.3 * jnp.clip(jax.random.normal(keys[1], shape, jnp.float32), -4.0, 4.0)
    radial_speed = 0.3 * jnp.clip(jax.random.normal(keys[2], shape, jnp.float32), -4.0, 4.0)
    swirl_speed = 0.3 * jnp.clip(jax.random.normal(keys[3], shape, jnp.float32), -4.0, 4.0)
    pressure = jax.random.uniform(keys[4], shape, jnp.float32, 0.6, 0.85)
    kinetic = axial_speed * axial_speed + radial_speed * radial_speed + swirl_speed * swirl_speed
    energy = pressure / (GAMMA - 1.0) + 0.5 * density * kinetic
    fields = jnp.stack([density, density * axial_speed, density * radial_speed, density * swirl_speed, energy])
    return fields.astype(jnp.float32)


def draw_state(key, part):
    return make_state(jax.random.fold_in(key, 11))


def draw_start(key, part):
    return make_state(jax.random.fold_in(key, 23))


def draw_modes(key, part):
    own_key = jax.random.fold_in(key, 37)
    lower = MSTEP * (jnp.arange(NIN, dtype=jnp.int32) + 1)
    extra = jax.random.randint(own_key, (NIN,), 0, lower + 1, dtype=jnp.int32)
    return jnp.minimum(lower + extra, NTH // 2).astype(jnp.int32)


def setup_inputs(seed: int = 0) -> dict:
    arg_keys = jax.random.split(jax.random.key(seed), 4)
    return {
        "state": draw_state(jax.random.fold_in(arg_keys[3], 71), 0),
        "start": draw_start(jax.random.fold_in(arg_keys[3], 71), 0),
        "modes": draw_modes(jax.random.fold_in(arg_keys[3], 71), 0),
    }


GAMMA = 1.4
STEP_DT = 0.05


def central_diff(values, dimension):
    length = values.shape[dimension] - 4

    def part_at(offset):
        return lax.slice_in_dim(values, offset, offset + length, axis=dimension)

    return (8.0 * (part_at(3) - part_at(1)) - (part_at(4) - part_at(0))) / 12.0


def pressure_of(values, inverse):
    kinetic = (values[1] * values[1] + values[2] * values[2] + values[3] * values[3]) * inverse
    return (GAMMA - 1.0) * (values[4] - 0.5 * kinetic)


def flux_along(values, direction):
    inverse = 1.0 / values[0]
    velocity = values[direction] * inverse
    pressure = pressure_of(values, inverse)
    components = [values[direction], values[1] * velocity, values[2] * velocity, values[3] * velocity, (values[4] + pressure) * velocity]
    components[direction] = components[direction] + pressure
    return jnp.stack(components)


def rates_of(padded, dtheta):
    axial_cells = padded[:, :, 2:-2, 2:-2]
    azimuth_cells = padded[:, 2:-2, :, 2:-2]
    radial_cells = padded[:, 2:-2, 2:-2, :]
    centre = padded[:, 2:-2, 2:-2, 2:-2]
    radius_all = jnp.arange(padded.shape[3], dtype=jnp.float32) - 1.5
    inv_radius = 1.0 / radius_all[2:-2]
    axial_term = central_diff(flux_along(axial_cells, 1), 1)
    radial_term = central_diff(flux_along(radial_cells, 2) * radius_all, 3) * inv_radius
    azimuth_term = central_diff(flux_along(azimuth_cells, 3), 2) * (inv_radius / dtheta)
    inverse = 1.0 / centre[0]
    pressure = pressure_of(centre, inverse)
    source_radial = (centre[3] * centre[3] * inverse + pressure) * inv_radius
    source_azimuth = -(centre[2] * centre[3] * inverse) * inv_radius
    totals = -(axial_term + radial_term + azimuth_term)
    return jnp.stack([totals[0], totals[1], totals[2] + source_radial, totals[3] + source_azimuth, totals[4]])


def radial_extend(haloed, partner):
    signs = jnp.array([1.0, 1.0, -1.0, -1.0, 1.0], dtype=jnp.float32).reshape(5, 1, 1, 1)
    ghost = jnp.flip(partner, 3) * signs
    rim_axial = (haloed.shape[1] - ghost.shape[1]) // 2
    rim_theta = (haloed.shape[2] - ghost.shape[2]) // 2
    ghost = jnp.pad(ghost, ((0, 0), (rim_axial, rim_axial), (rim_theta, rim_theta), (0, 0)))
    outer_cycles = jnp.repeat(haloed[..., -1:], 2, axis=3)
    return jnp.concatenate([ghost.astype(haloed.dtype), haloed, outer_cycles], axis=3)


def reference(state, start, modes):
    half_modes = NTH // 2
    inner = state[..., :NIN]
    spectrum = jnp.fft.rfft(inner, axis=2)
    wavenumbers = jnp.arange(half_modes + 1, dtype=jnp.int32)
    keep_mask = wavenumbers[:, None] < modes[None, :]
    spectrum = jnp.where(keep_mask, spectrum, jnp.zeros_like(spectrum))
    smooth_inner = jnp.fft.irfft(spectrum, n=NTH, axis=2).astype(state.dtype)
    smoothed = jnp.concatenate([smooth_inner, state[..., NIN:]], axis=3)
    partner = jnp.roll(smoothed[..., :2], half_modes, axis=2)
    extended = radial_extend(smoothed, partner)
    extended = jnp.concatenate([extended[:, :, -2:], extended, extended[:, :, :2]], axis=2)
    extended = jnp.concatenate([extended[:, -2:], extended, extended[:, :2]], axis=1)
    dtheta = 2.0 * math.pi / NTH

    def one_slab(slab_index):
        piece = lax.dynamic_slice_in_dim(extended, slab_index * X_DEV, X_DEV + 4, axis=1)
        return rates_of(piece, dtheta)

    slab_rates = lax.map(one_slab, jnp.arange(N_AXIAL, dtype=jnp.int32))
    rate = jnp.moveaxis(slab_rates, 0, 1).reshape(state.shape)
    return start + STEP_DT * rate
```

```python
import functools
import math

import jax
import jax.numpy as jnp
import numpy as np
from jax import lax
from jax.experimental import pallas as pl
from jax.experimental.pallas import tpu as pltpu
from jax.sharding import PartitionSpec as P

STEP_DT = 0.05
LANES = 128
CHUNKS = 2
BLOCK = 16
FLOOR = 1e-9
F32 = jnp.float32
BF16 = jnp.bfloat16
MESH = pl.DeviceIdType.MESH


def split_np(values):
    high = values.astype(np.float32).astype(jnp.bfloat16)
    low = (values - high.astype(np.float64)).astype(np.float32).astype(jnp.bfloat16)
    return high, low


def round_up(value, multiple):
    return -(-value // multiple) * multiple


@functools.lru_cache(None)
def plan(cells, count):
    total = cells * count
    width = round_up(cells, LANES)
    where = np.arange(cells)

    def coupling(offset):
        distance = offset * cells + where[:, None] - where[None, :]
        sine = np.sin(np.pi * distance / total)
        return np.where(distance == 0, 0.0, 1.0 / (total * np.where(distance == 0, 1.0, sine)))

    def wide(rows):
        return np.concatenate([rows] * (width // cells), axis=1)

    def padded(rows):
        return np.pad(rows, ((0, 0), (0, width - cells)))

    local = np.zeros((width, width))
    local[:cells] = wide(coupling(0).T)
    starts, ranks, outgoing, incoming = [], [], [], []
    for offset in range(1, count):
        left, values, right = np.linalg.svd(coupling(offset))
        rank = round_up(max(int(np.sum(values > FLOOR)), 1), 8)
        starts.append(sum(ranks))
        ranks.append(rank)
        outgoing.append(padded(right[:rank]))
        incoming.append(wide((left[:, :rank] * values[:rank]).T))
    depth = sum(ranks)
    out_high, out_low = split_np(np.concatenate(outgoing))
    in_high, in_low = split_np(np.concatenate(incoming))
    stacked = round_up(3 * depth, LANES)
    blank = np.zeros((stacked - 3 * depth, width), jnp.bfloat16)
    table = np.concatenate([*split_np(local), out_high, out_low, in_high, in_high, in_low, blank])
    return dict(width=width, depth=depth, stacked=stacked, starts=starts, ranks=ranks, table=table)


def split(values):
    high = values.astype(BF16)
    return high, (values - high.astype(F32)).astype(BF16)


def mm(a, b):
    return jnp.dot(a, b, preferred_element_type=F32)


def pressure_of(values, inverse):
    kinetic = (values[1] * values[1] + values[2] * values[2] + values[3] * values[3]) * inverse
    return 0.4 * (values[4] - 0.5 * kinetic)


def fluxes(values, direction, inverse, pressure):
    velocity = values[direction] * inverse
    parts = [
        values[direction],
        values[1] * velocity,
        values[2] * velocity,
        values[3] * velocity,
        (values[4] + pressure) * velocity,
    ]
    parts[direction] = parts[direction] + pressure
    return parts


def turns(steps, total):
    quarter = total // 2
    quadrant = (steps + quarter // 2) // quarter
    angle = (steps - quadrant * quarter).astype(F32) * (math.pi / total)
    square = angle * angle
    sine = angle + angle * square * (
        -1.0 / 6 + square * (1.0 / 120 + square * (-1.0 / 5040 + square * (1.0 / 362880)))
    )
    cosine = 1.0 + square * (
        -0.5
        + square * (1.0 / 24 + square * (-1.0 / 720 + square * (1.0 / 40320 - square * (1.0 / 3628800))))
    )
    odd = (quadrant & 1) == 1
    first, second = jnp.where(odd, cosine, sine), jnp.where(odd, sine, cosine)
    return (
        jnp.where((quadrant & 2) == 2, -first, first),
        jnp.where(((quadrant + 1) & 2) == 2, -second, second),
    )


def kernel(
    cfg,
    state_hbm, modes_hbm, table_hbm, out,
    state, modes, table, cosines, sines,
    x_high, x_low, near, mom_own, mom_in,
    fx_own, fx_left, fx_right, g_turn, g_out, rate,
    edge_right, edge_left, edge_from_left, edge_from_right, ghost,
    load_sem, mom_send, mom_recv, fx_send, fx_recv, edge_send, edge_recv,
):
    fields, axial, cycles, width = state.shape
    cells, inner = cfg["cells"], modes.shape[1]
    depth, stacked = cfg["depth"], cfg["stacked"]
    starts, ranks = cfg["starts"], cfg["ranks"]
    count, ring = lax.axis_size("azim"), lax.axis_size("axial")
    d, a = lax.axis_index("azim"), lax.axis_index("axial")
    total = cells * count
    planes = [(f, x) for f in range(fields) for x in range(axial)]
    span = inner // CHUNKS

    def z_at(offset):
        return {"azim": lax.rem(d + offset, count)}

    x_right = {"axial": lax.rem(a + 1, ring)}
    x_left = {"axial": lax.rem(a + ring - 1, ring)}

    def remote(src, dst, send, recv, device):
        return pltpu.make_async_remote_copy(
            src_ref=src, dst_ref=dst, send_sem=send, recv_sem=recv,
            device_id=device, device_id_type=MESH,
        )

    outer_rows, inner_rows = pl.ds(inner, cycles - inner), pl.ds(0, inner)
    loads = [
        pltpu.make_async_copy(modes_hbm, modes, load_sem.at[0]),
        pltpu.make_async_copy(
            state_hbm.at[:, :, outer_rows], state.at[:, :, outer_rows], load_sem.at[1]
        ),
        pltpu.make_async_copy(
            state_hbm.at[:, :, inner_rows], state.at[:, :, inner_rows], load_sem.at[2]
        ),
        pltpu.make_async_copy(table_hbm, table, load_sem.at[3]),
    ]
    for copy in loads:
        copy.start()

    barrier = pltpu.get_barrier_semaphore()
    peers = [z_at(offset) for offset in range(1, count)] + [x_right, x_left]
    for device in peers:
        pl.semaphore_signal(barrier, inc=1, device_id=device, device_id_type=MESH)

    moments = [
        [
            remote(
                mom_own.at[c, pl.ds(starts[k], ranks[k])], mom_in.at[c, pl.ds(starts[k], ranks[k])],
                mom_send.at[c, k], mom_recv.at[c, k], z_at(k + 1),
            )
            for k in range(len(ranks))
        ]
        for c in range(CHUNKS)
    ]
    pieces = [pl.ds(c * span, span) for c in range(CHUNKS)] + [outer_rows]
    crossings = [
        [
            remote(
                fx_own.at[:, :, rows], fx_left.at[:, :, rows], fx_send.at[0, k], fx_recv.at[0, k], x_right
            ),
            remote(
                fx_own.at[:, :, rows], fx_right.at[:, :, rows], fx_send.at[1, k], fx_recv.at[1, k], x_left
            ),
        ]
        for k, rows in enumerate(pieces)
    ]
    edges = [
        remote(edge_right, edge_from_left, edge_send.at[0], edge_recv.at[0], z_at(1)),
        remote(edge_left, edge_from_right, edge_send.at[1], edge_recv.at[1], z_at(count - 1)),
        remote(
            g_out.at[:, :, pl.ds(0, 8)], ghost, edge_send.at[2], edge_recv.at[2], z_at(count // 2)
        ),
    ]

    loads[0].wait()
    kept = jnp.broadcast_to(modes[...], (inner, inner)).astype(F32)
    same = lax.broadcasted_iota(jnp.int32, (inner, inner), 0) == lax.broadcasted_iota(
        jnp.int32, (inner, inner), 1
    )
    odd_count = 2.0 * jnp.sum(jnp.where(same, kept, 0.0), axis=1, keepdims=True) - 1.0
    share = odd_count * (1.0 / total)
    lane = lax.broadcasted_iota(jnp.int32, (inner, width), 1)
    place = (lax.rem(lane, cells) + d * cells).astype(F32)
    steps = (odd_count * place).astype(jnp.int32) & (2 * total - 1)
    sine, cosine = turns(steps, total)
    sines[...] = sine
    cosines[...] = cosine

    def axial_flux(values, x, rows):
        inverse = 1.0 / values[0]
        for f, part in enumerate(fluxes(values, 1, inverse, pressure_of(values, inverse))):
            fx_own[f, x, rows, :] = part

    loads[1].wait()
    for first in range(inner, cycles, BLOCK):
        rows = pl.ds(first, BLOCK)
        for x in range(axial):
            axial_flux([state[f, x, rows, :] for f in range(fields)], x, rows)
    pl.semaphore_wait(barrier, len(peers))
    for copy in crossings[CHUNKS]:
        copy.start()

    loads[2].wait()
    loads[3].wait()
    out_table = table[pl.ds(2 * width, 2 * depth), :]
    contract_lanes = (((1,), (1,)), ((), ()))
    for c in range(CHUNKS):
        rows = pl.ds(c * span, span)
        for p, (f, x) in enumerate(planes):
            value = state[f, x, rows, :]
            for part, wave in enumerate((cosines, sines)):
                high, low = split(value * wave[rows, :])
                slot = pl.ds((2 * p + part) * span, span)
                x_high[c, slot, :] = high
                x_low[c, slot, :] = low
        sums = lax.dot_general(
            out_table, x_high[c], contract_lanes, preferred_element_type=F32
        ) + lax.dot_general(out_table, x_low[c], contract_lanes, preferred_element_type=F32)
        sums = sums[:depth] + sums[depth:]
        for k in range(len(ranks)):
            wrapped = (1 - 2 * ((d + k + 1) // count)).astype(F32)
            mom_own[c, pl.ds(starts[k], ranks[k]), :] = (
                sums[starts[k] : starts[k] + ranks[k]] * wrapped
            )
        for copy in moments[c]:
            copy.start()

    local_high, local_low = table[pl.ds(0, width), :], table[pl.ds(width, width), :]
    for c in range(CHUNKS):
        near[c] = mm(x_high[c], local_high) + mm(x_low[c], local_high) + mm(x_high[c], local_low)

    in_table = table[pl.ds(2 * width + 2 * depth, stacked), :]
    for c in range(CHUNKS):
        for copy in moments[c]:
            copy.wait_recv()
        high = mom_in[c].astype(BF16).astype(F32)
        low = (mom_in[c] - high).astype(BF16).astype(F32)
        parts = [high, low, high]
        if stacked > 3 * depth:
            parts.append(jnp.zeros((stacked - 3 * depth, high.shape[1]), F32))
        stack = jnp.concatenate(parts, axis=0).T.astype(BF16)
        near[c] = near[c] + mm(stack, in_table)
        for first in range(0, span, BLOCK):
            rows = pl.ds(c * span + first, BLOCK)
            wave_sine, wave_cosine = sines[rows, :], cosines[rows, :]
            weight = share[c * span + first : c * span + first + BLOCK]
            for x in range(axial):
                values = []
                for f in range(fields):
                    slot = 2 * (f * axial + x) * span + first
                    kept_value = (
                        wave_sine * near[c, pl.ds(slot, BLOCK), :]
                        - wave_cosine * near[c, pl.ds(slot + span, BLOCK), :]
                        + weight * state[f, x, rows, :]
                    )
                    state[f, x, rows, :] = kept_value
                    values.append(kept_value)
                axial_flux(values, x, rows)
        for copy in crossings[c]:
            copy.start()

    radius_of = lambda first, size: (
        lax.broadcasted_iota(jnp.int32, (size, width), 0) + first
    ).astype(F32) + 0.5
    for first in range(0, cycles, BLOCK):
        rows = pl.ds(first, BLOCK)
        radius = radius_of(first, BLOCK)
        inv_radius = 1.0 / radius
        for x in range(axial):
            values = [state[f, x, rows, :] for f in range(fields)]
            inverse = 1.0 / values[0]
            pressure = pressure_of(values, inverse)
            for f, part in enumerate(fluxes(values, 3, inverse, pressure)):
                g_turn[f, x, rows, :] = part
            for f, part in enumerate(fluxes(values, 2, inverse, pressure)):
                g_out[f, x, rows, :] = part * radius
            rate[2, x, rows, :] = (values[3] * values[3] * inverse + pressure) * inv_radius
            rate[3, x, rows, :] = -(values[2] * values[3] * inverse) * inv_radius

    edge_lane = lax.broadcasted_iota(jnp.int32, (cycles, LANES), 1)
    pack_right = jnp.zeros((cycles, LANES), F32)
    pack_left = jnp.zeros((cycles, LANES), F32)
    for p, (f, x) in enumerate(planes):
        mine = (edge_lane >> 1) == p
        ends = g_turn[f, x, :, pl.ds(width - LANES, LANES)]
        pack_right = jnp.where(mine, pltpu.roll(ends, 2 * p + 2, 1), pack_right)
        heads = g_turn[f, x, :, pl.ds(0, LANES)]
        pack_left = jnp.where(mine, pltpu.roll(heads, 2 * p, 1) if p else heads, pack_left)
    edge_right[...] = pack_right
    edge_left[...] = pack_left
    for copy in edges:
        copy.start()

    inv_radius = 1.0 / radius_of(0, cycles)
    angular = inv_radius * (1.0 / (12.0 * (2.0 * math.pi / total)))
    radial = inv_radius * (1.0 / 12.0)
    tail_row = lax.broadcasted_iota(jnp.int32, (8, width), 0)
    beyond = jnp.where(
        tail_row < 2, (tail_row.astype(F32) + (cycles + 0.5)) * (1.0 / (cycles - 0.5)), 0.0
    )
    for f, x in planes:
        g = g_turn[f, x]
        turn_term = 8.0 * (pltpu.roll(g, width - 1, 1) - pltpu.roll(g, 1, 1)) - (
            pltpu.roll(g, width - 2, 1) - pltpu.roll(g, 2, 1)
        )
        g = g_out[f, x]
        tall = cycles + 8
        g = jnp.concatenate([g, beyond * g[cycles - 1 :]], axis=0)
        out_term = (
            8.0 * (pltpu.roll(g, tall - 1, 0) - pltpu.roll(g, 1, 0))
            - (pltpu.roll(g, tall - 2, 0) - pltpu.roll(g, 2, 0))
        )[:cycles]
        change = -(turn_term * angular + out_term * radial)
        if f in (2, 3):
            change = change + rate[f, x]
        rate[f, x] = STEP_DT * change

    for copy in edges:
        copy.wait_recv()
    from_left = edge_from_left[...] - edge_right[...]
    from_right = edge_from_right[...] - edge_left[...]
    even = (edge_lane & 1) == 0
    scale = -STEP_DT * angular[:, :LANES]
    from_left = scale * jnp.where(
        even, from_left - 8.0 * pltpu.roll(from_left, LANES - 1, 1), from_left
    )
    from_right = scale * jnp.where(
        even, -from_right, 8.0 * pltpu.roll(from_right, 1, 1) - from_right
    )
    head, end = pl.ds(0, LANES), pl.ds((cells - 1) // LANES * LANES, LANES)
    end_lane = (cells - 2) % LANES
    ghost_row = lax.broadcasted_iota(jnp.int32, (8, width), 0)
    ghost_scale = -STEP_DT * radial[:8]
    for p, (f, x) in enumerate(planes):
        value = pltpu.roll(from_left, (LANES - 2 * p) % LANES, 1) if p else from_left
        rate[f, x, :, head] = rate[f, x, :, head] + jnp.where(edge_lane < 2, value, 0.0)
        value = pltpu.roll(from_right, (end_lane - 2 * p) % LANES, 1)
        mine = (edge_lane >= end_lane) & (edge_lane < end_lane + 2)
        rate[f, x, :, end] = rate[f, x, :, end] + jnp.where(mine, value, 0.0)
        tile = -ghost[f, x] if f in (2, 3) else ghost[f, x]
        inside = jnp.where(
            ghost_row == 0,
            pltpu.roll(tile, 7, 0) - 8.0 * tile,
            jnp.where(ghost_row == 1, pltpu.roll(tile, 1, 0), 0.0),
        )
        rate[f, x, pl.ds(0, 8), :] = rate[f, x, pl.ds(0, 8), :] + ghost_scale * inside

    for k in [CHUNKS] + list(range(CHUNKS)):
        for copy in crossings[k]:
            copy.wait_recv()
        rows = pieces[k]
        for f in range(fields):
            own = [fx_own[f, x, rows, :] for x in range(axial)]
            left = [fx_left[f, x, rows, :] for x in range(axial)]
            right = [fx_right[f, x, rows, :] for x in range(axial)]
            terms = (
                8.0 * (own[1] - left[1]) - (right[0] - left[0]),
                8.0 * (right[0] - own[0]) - (right[1] - left[1]),
            )
            for x, term in enumerate(terms):
                out[f, x, rows, :] = rate[f, x, rows, :] - (STEP_DT / 12.0) * term

    for pair in crossings:
        for copy in pair:
            copy.wait_send()
    for group in moments:
        for copy in group:
            copy.wait_send()
    for copy in edges:
        copy.wait_send()


def shards(state, start, modes):
    fields, axial, cells, cycles = state.shape
    inner = modes.shape[0]
    cfg = dict(plan(cells, lax.axis_size("azim")), cells=cells)
    width, depth = cfg["width"], cfg["depth"]
    turned = state.transpose(0, 1, 3, 2)
    if width != cells:
        turned = jnp.concatenate([turned] * (width // cells), axis=3)
    table = jnp.asarray(cfg["table"])
    full = (fields, axial, cycles, width)
    columns = 2 * fields * axial * inner // CHUNKS
    hbm = pl.BlockSpec(memory_space=pltpu.HBM)
    vmem = pl.BlockSpec(memory_space=pltpu.VMEM)
    peers = len(cfg["ranks"])
    step = pl.pallas_call(
        functools.partial(kernel, cfg),
        out_shape=jax.ShapeDtypeStruct(full, F32),
        in_specs=[hbm, hbm, hbm],
        out_specs=vmem,
        scratch_shapes=[
            pltpu.VMEM(full, F32),
            pltpu.VMEM((1, inner), jnp.int32),
            pltpu.VMEM(table.shape, BF16),
            pltpu.VMEM((inner, width), F32),
            pltpu.VMEM((inner, width), F32),
            pltpu.VMEM((CHUNKS, columns, width), BF16),
            pltpu.VMEM((CHUNKS, columns, width), BF16),
            pltpu.VMEM((CHUNKS, columns, width), F32),
            pltpu.VMEM((CHUNKS, depth, columns), F32),
            pltpu.VMEM((CHUNKS, depth, columns), F32),
        ]
        + [pltpu.VMEM(full, F32)] * 6
        + [pltpu.VMEM((cycles, LANES), F32)] * 4
        + [
            pltpu.VMEM((fields, axial, 8, width), F32),
            pltpu.SemaphoreType.DMA((4,)),
            pltpu.SemaphoreType.DMA((CHUNKS, peers)),
            pltpu.SemaphoreType.DMA((CHUNKS, peers)),
            pltpu.SemaphoreType.DMA((2, CHUNKS + 1)),
            pltpu.SemaphoreType.DMA((2, CHUNKS + 1)),
            pltpu.SemaphoreType.DMA((3,)),
            pltpu.SemaphoreType.DMA((3,)),
        ],
        compiler_params=pltpu.CompilerParams(
            collective_id=0, has_side_effects=True, vmem_limit_bytes=48 * 1024 * 1024
        ),
        name="jet_section",
    )(turned, modes.reshape(1, inner), table)
    if width != cells:
        step = step[..., :cells]
    return start + step.transpose(0, 1, 3, 2)


def solution(mesh):
    in_specs = (P(None, "axial", "azim", None), P(None, "axial", "azim", None), P())
    out_specs = P(None, "axial", "azim", None)
    return jax.shard_map(shards, mesh=mesh, in_specs=in_specs, out_specs=out_specs, check_vma=False)
```

```python
import functools
import math

import jax
import jax.numpy as jnp
import numpy as np
from jax import lax
from jax.experimental import pallas as pl
from jax.experimental.pallas import tpu as pltpu
from jax.sharding import PartitionSpec as P

STEP_DT = 0.05
LANES = 128
CHUNKS = 2
BLOCK = 16
FLOOR = 1e-9
F32 = jnp.float32
BF16 = jnp.bfloat16
MESH = pl.DeviceIdType.MESH


def split_np(values):
    high = values.astype(np.float32).astype(jnp.bfloat16)
    low = (values - high.astype(np.float64)).astype(np.float32).astype(jnp.bfloat16)
    return high, low


def round_up(value, multiple):
    return -(-value // multiple) * multiple


@functools.lru_cache(None)
def plan(cells, count):
    total = cells * count
    width = round_up(cells, LANES)
    where = np.arange(cells)

    def coupling(offset):
        distance = offset * cells + where[:, None] - where[None, :]
        sine = np.sin(np.pi * distance / total)
        return np.where(distance == 0, 0.0, 1.0 / (total * np.where(distance == 0, 1.0, sine)))

    def wide(rows):
        return np.concatenate([rows] * (width // cells), axis=1)

    def padded(rows):
        return np.pad(rows, ((0, 0), (0, width - cells)))

    local = np.zeros((width, width))
    local[:cells] = wide(coupling(0).T)
    starts, ranks, outgoing, incoming = [], [], [], []
    for offset in range(1, count):
        left, values, right = np.linalg.svd(coupling(offset))
        rank = round_up(max(int(np.sum(values > FLOOR)), 1), 8)
        starts.append(sum(ranks))
        ranks.append(rank)
        outgoing.append(padded(right[:rank]))
        incoming.append(wide((left[:, :rank] * values[:rank]).T))
    depth = sum(ranks)
    out_high, out_low = split_np(np.concatenate(outgoing))
    in_high, in_low = split_np(np.concatenate(incoming))
    stacked = round_up(3 * depth, LANES)
    blank = np.zeros((stacked - 3 * depth, width), jnp.bfloat16)
    table = np.concatenate([*split_np(local), out_high, out_low, in_high, in_high, in_low, blank])
    return dict(width=width, depth=depth, stacked=stacked, starts=starts, ranks=ranks, table=table)


def pieces_of(inner, cycles):
    span = inner // CHUNKS
    pieces = [(inner, cycles - inner)]
    pieces += [(c * span, span) for c in range(CHUNKS - 1)]
    half = span // 2
    return pieces + [(inner - span, half), (inner - half, half // 2), (inner - half // 2, half // 2)]


def split(values):
    high = values.astype(BF16)
    return high, (values - high.astype(F32)).astype(BF16)


def mm(a, b):
    return jnp.dot(a, b, preferred_element_type=F32)


def pressure_of(values, inverse):
    kinetic = (values[1] * values[1] + values[2] * values[2] + values[3] * values[3]) * inverse
    return 0.4 * (values[4] - 0.5 * kinetic)


def fluxes(values, direction, inverse, pressure):
    velocity = values[direction] * inverse
    parts = [
        values[direction],
        values[1] * velocity,
        values[2] * velocity,
        values[3] * velocity,
        (values[4] + pressure) * velocity,
    ]
    parts[direction] = parts[direction] + pressure
    return parts


def turns(steps, total):
    quarter = total // 2
    quadrant = (steps + quarter // 2) // quarter
    angle = (steps - quadrant * quarter).astype(F32) * (math.pi / total)
    square = angle * angle
    sine = angle + angle * square * (
        -1.0 / 6 + square * (1.0 / 120 + square * (-1.0 / 5040 + square * (1.0 / 362880)))
    )
    cosine = 1.0 + square * (
        -0.5
        + square * (1.0 / 24 + square * (-1.0 / 720 + square * (1.0 / 40320 - square * (1.0 / 3628800))))
    )
    odd = (quadrant & 1) == 1
    first, second = jnp.where(odd, cosine, sine), jnp.where(odd, sine, cosine)
    return (
        jnp.where((quadrant & 2) == 2, -first, first),
        jnp.where(((quadrant + 1) & 2) == 2, -second, second),
    )


def kernel(
    cfg,
    state_hbm, modes_hbm, table_hbm, out,
    state, modes, table, cosines, sines,
    x_high, x_low, near, mom_own, mom_in,
    fx_own, fx_left, fx_right, g_turn, g_out, rate,
    edge_right, edge_left, edge_from_left, edge_from_right, ghost,
    load_sem, mom_send, mom_recv, fx_send, fx_recv, edge_send, edge_recv,
):
    fields, axial, cycles, width = state.shape
    cells, inner = cfg["cells"], modes.shape[1]
    depth, stacked = cfg["depth"], cfg["stacked"]
    starts, ranks = cfg["starts"], cfg["ranks"]
    count, ring = lax.axis_size("azim"), lax.axis_size("axial")
    d, a = lax.axis_index("azim"), lax.axis_index("axial")
    total = cells * count
    planes = [(f, x) for f in range(fields) for x in range(axial)]
    span = inner // CHUNKS

    def z_at(offset):
        return {"azim": lax.rem(d + offset, count)}

    x_right = {"axial": lax.rem(a + 1, ring)}
    x_left = {"axial": lax.rem(a + ring - 1, ring)}

    def remote(src, dst, send, recv, device):
        return pltpu.make_async_remote_copy(
            src_ref=src, dst_ref=dst, send_sem=send, recv_sem=recv,
            device_id=device, device_id_type=MESH,
        )

    outer_rows, inner_rows = pl.ds(inner, cycles - inner), pl.ds(0, inner)
    barrier = pltpu.get_barrier_semaphore()
    peers = [x_right, x_left] + [z_at(offset) for offset in range(1, count)]
    for device in peers:
        pl.semaphore_signal(barrier, inc=1, device_id=device, device_id_type=MESH)
    loads = [
        pltpu.make_async_copy(modes_hbm, modes, load_sem.at[0]),
        pltpu.make_async_copy(
            state_hbm.at[:, :, inner_rows], state.at[:, :, inner_rows], load_sem.at[1]
        ),
        pltpu.make_async_copy(
            state_hbm.at[:, :, outer_rows], state.at[:, :, outer_rows], load_sem.at[2]
        ),
        pltpu.make_async_copy(table_hbm, table, load_sem.at[3]),
    ]
    for copy in loads:
        copy.start()

    moments = [
        [
            remote(
                mom_own.at[c, pl.ds(starts[k], ranks[k])], mom_in.at[c, pl.ds(starts[k], ranks[k])],
                mom_send.at[c, k], mom_recv.at[c, k], z_at(k + 1),
            )
            for k in range(len(ranks))
        ]
        for c in range(CHUNKS)
    ]
    pieces = pieces_of(inner, cycles)
    crossings = []
    for k, (first, size) in enumerate(pieces):
        rows = pl.ds(first, size)
        source = state_hbm if first == inner else fx_own
        crossings.append(
            [
                remote(
                    source.at[:, :, rows], far_side.at[:, :, rows], fx_send.at[side, k],
                    fx_recv.at[side, k], device,
                )
                for side, (far_side, device) in enumerate(((fx_left, x_right), (fx_right, x_left)))
            ]
        )
    edges = [
        remote(edge_right, edge_from_left, edge_send.at[0], edge_recv.at[0], z_at(1)),
        remote(edge_left, edge_from_right, edge_send.at[1], edge_recv.at[1], z_at(count - 1)),
        remote(
            g_out.at[:, :, pl.ds(0, 8)], ghost, edge_send.at[2], edge_recv.at[2], z_at(count // 2)
        ),
    ]

    pl.semaphore_wait(barrier, len(peers))
    for copy in crossings[0]:
        copy.start()

    loads[0].wait()
    kept = jnp.broadcast_to(modes[...], (inner, inner)).astype(F32)
    same = lax.broadcasted_iota(jnp.int32, (inner, inner), 0) == lax.broadcasted_iota(
        jnp.int32, (inner, inner), 1
    )
    odd_count = 2.0 * jnp.sum(jnp.where(same, kept, 0.0), axis=1, keepdims=True) - 1.0
    share = odd_count * (1.0 / total)
    lane = lax.broadcasted_iota(jnp.int32, (inner, width), 1)
    place = (lax.rem(lane, cells) + d * cells).astype(F32)
    steps = (odd_count * place).astype(jnp.int32) & (2 * total - 1)
    sine, cosine = turns(steps, total)
    sines[...] = sine
    cosines[...] = cosine

    def axial_flux(values, x, rows):
        inverse = 1.0 / values[0]
        for f, part in enumerate(fluxes(values, 1, inverse, pressure_of(values, inverse))):
            fx_own[f, x, rows, :] = part

    loads[1].wait()
    loads[3].wait()
    out_table = table[pl.ds(2 * width, 2 * depth), :]
    contract_lanes = (((1,), (1,)), ((), ()))
    for c in range(CHUNKS):
        rows = pl.ds(c * span, span)
        for p, (f, x) in enumerate(planes):
            value = state[f, x, rows, :]
            for part, wave in enumerate((cosines, sines)):
                high, low = split(value * wave[rows, :])
                slot = pl.ds((2 * p + part) * span, span)
                x_high[c, slot, :] = high
                x_low[c, slot, :] = low
        sums = lax.dot_general(
            out_table, x_high[c], contract_lanes, preferred_element_type=F32
        ) + lax.dot_general(out_table, x_low[c], contract_lanes, preferred_element_type=F32)
        sums = sums[:depth] + sums[depth:]
        for k in range(len(ranks)):
            wrapped = (1 - 2 * ((d + k + 1) // count)).astype(F32)
            mom_own[c, pl.ds(starts[k], ranks[k]), :] = (
                sums[starts[k] : starts[k] + ranks[k]] * wrapped
            )
        for copy in moments[c]:
            copy.start()

    local_high, local_low = table[pl.ds(0, width), :], table[pl.ds(width, width), :]
    for c in range(CHUNKS):
        near[c] = mm(x_high[c], local_high) + mm(x_low[c], local_high) + mm(x_high[c], local_low)

    ends = [(first + size, pair) for (first, size), pair in zip(pieces, crossings) if first != inner]
    in_table = table[pl.ds(2 * width + 2 * depth, stacked), :]
    for c in range(CHUNKS):
        for copy in moments[c]:
            copy.wait_recv()
        high = mom_in[c].astype(BF16).astype(F32)
        low = (mom_in[c] - high).astype(BF16).astype(F32)
        parts = [high, low, high]
        if stacked > 3 * depth:
            parts.append(jnp.zeros((stacked - 3 * depth, high.shape[1]), F32))
        stack = jnp.concatenate(parts, axis=0).T.astype(BF16)
        near[c] = near[c] + mm(stack, in_table)
        for first in range(0, span, BLOCK):
            rows = pl.ds(c * span + first, BLOCK)
            wave_sine, wave_cosine = sines[rows, :], cosines[rows, :]
            weight = share[c * span + first : c * span + first + BLOCK]
            for x in range(axial):
                values = []
                for f in range(fields):
                    slot = 2 * (f * axial + x) * span + first
                    kept_value = (
                        wave_sine * near[c, pl.ds(slot, BLOCK), :]
                        - wave_cosine * near[c, pl.ds(slot + span, BLOCK), :]
                        + weight * state[f, x, rows, :]
                    )
                    state[f, x, rows, :] = kept_value
                    values.append(kept_value)
                axial_flux(values, x, rows)
            for end, pair in ends:
                if 0 < end - (c * span + first) <= BLOCK:
                    for copy in pair:
                        copy.start()

    radius_of = lambda first, size: (
        lax.broadcasted_iota(jnp.int32, (size, width), 0) + first
    ).astype(F32) + 0.5
    loads[2].wait()
    for first in range(0, cycles, BLOCK):
        rows = pl.ds(first, BLOCK)
        radius = radius_of(first, BLOCK)
        inv_radius = 1.0 / radius
        for x in range(axial):
            values = [state[f, x, rows, :] for f in range(fields)]
            inverse = 1.0 / values[0]
            pressure = pressure_of(values, inverse)
            for f, part in enumerate(fluxes(values, 3, inverse, pressure)):
                g_turn[f, x, rows, :] = part
            for f, part in enumerate(fluxes(values, 2, inverse, pressure)):
                g_out[f, x, rows, :] = part * radius
            rate[2, x, rows, :] = (values[3] * values[3] * inverse + pressure) * inv_radius
            rate[3, x, rows, :] = -(values[2] * values[3] * inverse) * inv_radius

    edge_lane = lax.broadcasted_iota(jnp.int32, (cycles, LANES), 1)
    pack_right = jnp.zeros((cycles, LANES), F32)
    pack_left = jnp.zeros((cycles, LANES), F32)
    for p, (f, x) in enumerate(planes):
        mine = (edge_lane >> 1) == p
        ends = g_turn[f, x, :, pl.ds(width - LANES, LANES)]
        pack_right = jnp.where(mine, pltpu.roll(ends, 2 * p + 2, 1), pack_right)
        heads = g_turn[f, x, :, pl.ds(0, LANES)]
        pack_left = jnp.where(mine, pltpu.roll(heads, 2 * p, 1) if p else heads, pack_left)
    edge_right[...] = pack_right
    edge_left[...] = pack_left
    for copy in edges:
        copy.start()

    inv_radius = 1.0 / radius_of(0, cycles)
    angular = inv_radius * (1.0 / (12.0 * (2.0 * math.pi / total)))
    radial = inv_radius * (1.0 / 12.0)
    tail_row = lax.broadcasted_iota(jnp.int32, (8, width), 0)
    beyond = jnp.where(
        tail_row < 2, (tail_row.astype(F32) + (cycles + 0.5)) * (1.0 / (cycles - 0.5)), 0.0
    )
    for f, x in planes:
        g = g_turn[f, x]
        turn_term = 8.0 * (pltpu.roll(g, width - 1, 1) - pltpu.roll(g, 1, 1)) - (
            pltpu.roll(g, width - 2, 1) - pltpu.roll(g, 2, 1)
        )
        g = g_out[f, x]
        tall = cycles + 8
        g = jnp.concatenate([g, beyond * g[cycles - 1 :]], axis=0)
        out_term = (
            8.0 * (pltpu.roll(g, tall - 1, 0) - pltpu.roll(g, 1, 0))
            - (pltpu.roll(g, tall - 2, 0) - pltpu.roll(g, 2, 0))
        )[:cycles]
        change = -(turn_term * angular + out_term * radial)
        if f in (2, 3):
            change = change + rate[f, x]
        rate[f, x] = STEP_DT * change

    for copy in edges:
        copy.wait_recv()
    from_left = edge_from_left[...] - edge_right[...]
    from_right = edge_from_right[...] - edge_left[...]
    even = (edge_lane & 1) == 0
    scale = -STEP_DT * angular[:, :LANES]
    from_left = scale * jnp.where(
        even, from_left - 8.0 * pltpu.roll(from_left, LANES - 1, 1), from_left
    )
    from_right = scale * jnp.where(
        even, -from_right, 8.0 * pltpu.roll(from_right, 1, 1) - from_right
    )
    head, end = pl.ds(0, LANES), pl.ds((cells - 1) // LANES * LANES, LANES)
    end_lane = (cells - 2) % LANES
    ghost_row = lax.broadcasted_iota(jnp.int32, (8, width), 0)
    ghost_scale = -STEP_DT * radial[:8]
    for p, (f, x) in enumerate(planes):
        value = pltpu.roll(from_left, (LANES - 2 * p) % LANES, 1) if p else from_left
        rate[f, x, :, head] = rate[f, x, :, head] + jnp.where(edge_lane < 2, value, 0.0)
        value = pltpu.roll(from_right, (end_lane - 2 * p) % LANES, 1)
        mine = (edge_lane >= end_lane) & (edge_lane < end_lane + 2)
        rate[f, x, :, end] = rate[f, x, :, end] + jnp.where(mine, value, 0.0)
        tile = -ghost[f, x] if f in (2, 3) else ghost[f, x]
        inside = jnp.where(
            ghost_row == 0,
            pltpu.roll(tile, 7, 0) - 8.0 * tile,
            jnp.where(ghost_row == 1, pltpu.roll(tile, 1, 0), 0.0),
        )
        rate[f, x, pl.ds(0, 8), :] = rate[f, x, pl.ds(0, 8), :] + ghost_scale * inside

    def raw_flux(ref, x, rows):
        values = [ref[f, x, rows, :] for f in range(fields)]
        inverse = 1.0 / values[0]
        return fluxes(values, 1, inverse, pressure_of(values, inverse))

    for (begin, size), pair in zip(pieces, crossings):
        for copy in pair:
            copy.wait_recv()
        for first in range(begin, begin + size, 8):
            rows = pl.ds(first, 8)
            if begin == inner:
                own, left, right = [
                    [raw_flux(ref, x, rows) for x in range(axial)] for ref in (state, fx_left, fx_right)
                ]
            else:
                own, left, right = [
                    [[ref[f, x, rows, :] for f in range(fields)] for x in range(axial)]
                    for ref in (fx_own, fx_left, fx_right)
                ]
            for f in range(fields):
                terms = (
                    8.0 * (own[1][f] - left[1][f]) - (right[0][f] - left[0][f]),
                    8.0 * (right[0][f] - own[0][f]) - (right[1][f] - left[1][f]),
                )
                for x, term in enumerate(terms):
                    out[f, x, rows, :] = rate[f, x, rows, :] - (STEP_DT / 12.0) * term

    for pair in crossings:
        for copy in pair:
            copy.wait_send()
    for group in moments:
        for copy in group:
            copy.wait_send()
    for copy in edges:
        copy.wait_send()


def shards(state, start, modes):
    fields, axial, cells, cycles = state.shape
    inner = modes.shape[0]
    cfg = dict(plan(cells, lax.axis_size("azim")), cells=cells)
    width, depth = cfg["width"], cfg["depth"]
    turned = state.transpose(0, 1, 3, 2)
    if width != cells:
        turned = jnp.concatenate([turned] * (width // cells), axis=3)
    full = (fields, axial, cycles, width)
    columns = 2 * fields * axial * inner // CHUNKS
    hbm = pl.BlockSpec(memory_space=pltpu.HBM)
    vmem = pl.BlockSpec(memory_space=pltpu.VMEM)
    peers, pieces = len(cfg["ranks"]), len(pieces_of(inner, cycles))
    operands = (turned, modes.reshape(1, inner), jnp.asarray(cfg["table"]))
    step = pl.pallas_call(
        functools.partial(kernel, cfg),
        out_shape=jax.ShapeDtypeStruct(full, F32),
        in_specs=[hbm, hbm, hbm],
        out_specs=vmem,
        scratch_shapes=[
            pltpu.VMEM(full, F32),
            pltpu.VMEM((1, inner), jnp.int32),
            pltpu.VMEM(cfg["table"].shape, BF16),
            pltpu.VMEM((inner, width), F32),
            pltpu.VMEM((inner, width), F32),
            pltpu.VMEM((CHUNKS, columns, width), BF16),
            pltpu.VMEM((CHUNKS, columns, width), BF16),
            pltpu.VMEM((CHUNKS, columns, width), F32),
            pltpu.VMEM((CHUNKS, depth, columns), F32),
            pltpu.VMEM((CHUNKS, depth, columns), F32),
        ]
        + [pltpu.VMEM(full, F32)] * 6
        + [pltpu.VMEM((cycles, LANES), F32)] * 4
        + [
            pltpu.VMEM((fields, axial, 8, width), F32),
            pltpu.SemaphoreType.DMA((4,)),
            pltpu.SemaphoreType.DMA((CHUNKS, peers)),
            pltpu.SemaphoreType.DMA((CHUNKS, peers)),
            pltpu.SemaphoreType.DMA((2, pieces)),
            pltpu.SemaphoreType.DMA((2, pieces)),
            pltpu.SemaphoreType.DMA((3,)),
            pltpu.SemaphoreType.DMA((3,)),
        ],
        compiler_params=pltpu.CompilerParams(
            collective_id=0, has_side_effects=True, vmem_limit_bytes=48 * 1024 * 1024
        ),
        name="jet_section",
    )(*[pltpu.with_memory_space_constraint(operand, pltpu.HBM) for operand in operands])
    if width != cells:
        step = step[..., :cells]
    return start + step.transpose(0, 1, 3, 2)


def solution(mesh):
    in_specs = (P(None, "axial", "azim", None), P(None, "axial", "azim", None), P())
    out_specs = P(None, "axial", "azim", None)
    return jax.shard_map(shards, mesh=mesh, in_specs=in_specs, out_specs=out_specs, check_vma=False)
```

```python
import functools
import math

import jax
import jax.numpy as jnp
import numpy as np
from jax import lax
from jax.experimental import pallas as pl
from jax.experimental.pallas import tpu as pltpu
from jax.sharding import PartitionSpec as P

STEP_DT = 0.05
LANES = 128
CHUNKS = 2
BLOCK = 16
MSTEP = 8
TILE = 8
FLOOR = 1e-9
F32 = jnp.float32
BF16 = jnp.bfloat16
MESH = pl.DeviceIdType.MESH


def split_np(values):
    high = values.astype(np.float32).astype(jnp.bfloat16)
    low = (values - high.astype(np.float64)).astype(np.float32).astype(jnp.bfloat16)
    return high, low


def round_up(value, multiple):
    return -(-value // multiple) * multiple


@functools.lru_cache(None)
def plan(cells, count):
    total = cells * count
    width = round_up(cells, LANES)
    where = np.arange(cells)

    def coupling(offset):
        distance = offset * cells + where[:, None] - where[None, :]
        sine = np.sin(np.pi * distance / total)
        return np.where(distance == 0, 0.0, 1.0 / (total * np.where(distance == 0, 1.0, sine)))

    def wide(rows):
        return np.concatenate([rows] * (width // cells), axis=1)

    def padded(rows):
        return np.pad(rows, ((0, 0), (0, width - cells)))

    local = np.zeros((width, width))
    local[:cells] = wide(coupling(0).T)
    starts, ranks, outgoing, incoming = [], [], [], []
    for offset in range(1, count):
        left, values, right = np.linalg.svd(coupling(offset))
        rank = round_up(max(int(np.sum(values > FLOOR)), 1), 8)
        starts.append(sum(ranks))
        ranks.append(rank)
        outgoing.append(padded(right[:rank]))
        incoming.append(wide((left[:, :rank] * values[:rank]).T))
    depth = sum(ranks)
    out_high, out_low = split_np(np.concatenate(outgoing))
    in_high, in_low = split_np(np.concatenate(incoming))
    stacked = round_up(3 * depth, LANES)
    blank = np.zeros((stacked - 3 * depth, width), jnp.bfloat16)
    table = np.concatenate([*split_np(local), out_high, out_low, in_high, in_high, in_low, blank])

    def band(tile):
        bound = min(2 * MSTEP * TILE * (tile + 1), total // 2)
        waves = np.arange(1, bound)
        phase = 2 * np.pi * ((where[:, None] * waves) % total) / total
        scale = np.sqrt(2.0 / total)
        columns = [np.full((cells, 1), 1.0 / np.sqrt(total)), scale * np.cos(phase), scale * np.sin(phase)]
        left, values, _ = np.linalg.svd(np.concatenate(columns, axis=1))
        return left, int(np.sum(values > FLOOR))

    (first, low), (second, high) = band(0), band(1)
    assert low + high <= width
    low = min(cells, low + (width - low - high) // 2)
    high = min(cells, width - low)
    pack, unpack = [], []
    for base, lanes in ((first[:, :low], (0, low)), (second[:, :high], (low, low + high))):
        into = np.zeros((width, width))
        into[:cells, lanes[0] : lanes[1]] = base
        out_of = np.zeros((width, width))
        out_of[lanes[0] : lanes[1]] = wide(base.T)
        pack.append(split_np(into))
        unpack.append(split_np(out_of))
    bases = np.concatenate(
        [pair[part] for pairs in (pack, unpack) for part in range(2) for pair in pairs]
    )
    return dict(
        width=width, depth=depth, stacked=stacked, starts=starts, ranks=ranks, table=table, bases=bases
    )


def pieces_of(inner, cycles):
    span = inner // CHUNKS
    half = span // 2
    pieces = [(inner, cycles - inner), (2 * TILE, span - 2 * TILE), (0, 2 * TILE)]
    pieces += [(c * span, span) for c in range(1, CHUNKS - 1)]
    return pieces + [(inner - span, half), (inner - half, half // 2), (inner - half // 2, half // 2)]


def split(values):
    high = values.astype(BF16)
    return high, (values - high.astype(F32)).astype(BF16)


def mm(a, b):
    return jnp.dot(a, b, preferred_element_type=F32)


def pressure_of(values, inverse):
    kinetic = (values[1] * values[1] + values[2] * values[2] + values[3] * values[3]) * inverse
    return 0.4 * (values[4] - 0.5 * kinetic)


def fluxes(values, direction, inverse, pressure):
    velocity = values[direction] * inverse
    parts = [
        values[direction],
        values[1] * velocity,
        values[2] * velocity,
        values[3] * velocity,
        (values[4] + pressure) * velocity,
    ]
    parts[direction] = parts[direction] + pressure
    return parts


def turns(steps, total):
    quarter = total // 2
    quadrant = (steps + quarter // 2) // quarter
    angle = (steps - quadrant * quarter).astype(F32) * (math.pi / total)
    square = angle * angle
    sine = angle + angle * square * (
        -1.0 / 6 + square * (1.0 / 120 + square * (-1.0 / 5040 + square * (1.0 / 362880)))
    )
    cosine = 1.0 + square * (
        -0.5
        + square * (1.0 / 24 + square * (-1.0 / 720 + square * (1.0 / 40320 - square * (1.0 / 3628800))))
    )
    odd = (quadrant & 1) == 1
    first, second = jnp.where(odd, cosine, sine), jnp.where(odd, sine, cosine)
    return (
        jnp.where((quadrant & 2) == 2, -first, first),
        jnp.where(((quadrant + 1) & 2) == 2, -second, second),
    )


def kernel(
    cfg,
    state_hbm, modes_hbm, table_hbm, bases_hbm, out,
    state, modes, table, bases, cosines, sines,
    x_high, x_low, near, mom_own, mom_in,
    fx_own, fx_left, fx_right, g_turn, g_out, rate, low_own, low_left, low_right,
    edge_right, edge_left, edge_from_left, edge_from_right, ghost,
    load_sem, mom_send, mom_recv, fx_send, fx_recv, edge_send, edge_recv,
):
    fields, axial, cycles, width = state.shape
    cells, inner = cfg["cells"], modes.shape[1]
    depth, stacked = cfg["depth"], cfg["stacked"]
    starts, ranks = cfg["starts"], cfg["ranks"]
    count, ring = lax.axis_size("azim"), lax.axis_size("axial")
    d, a = lax.axis_index("azim"), lax.axis_index("axial")
    total = cells * count
    planes = [(f, x) for f in range(fields) for x in range(axial)]
    span = inner // CHUNKS

    def z_at(offset):
        return {"azim": lax.rem(d + offset, count)}

    x_right = {"axial": lax.rem(a + 1, ring)}
    x_left = {"axial": lax.rem(a + ring - 1, ring)}

    def remote(src, dst, send, recv, device):
        return pltpu.make_async_remote_copy(
            src_ref=src, dst_ref=dst, send_sem=send, recv_sem=recv,
            device_id=device, device_id_type=MESH,
        )

    outer_rows, inner_rows = pl.ds(inner, cycles - inner), pl.ds(0, inner)
    barrier = pltpu.get_barrier_semaphore()
    peers = [x_right, x_left] + [z_at(offset) for offset in range(1, count)]
    for device in peers:
        pl.semaphore_signal(barrier, inc=1, device_id=device, device_id_type=MESH)
    loads = [
        pltpu.make_async_copy(modes_hbm, modes, load_sem.at[0]),
        pltpu.make_async_copy(
            state_hbm.at[:, :, inner_rows], state.at[:, :, inner_rows], load_sem.at[1]
        ),
        pltpu.make_async_copy(
            state_hbm.at[:, :, outer_rows], state.at[:, :, outer_rows], load_sem.at[2]
        ),
        pltpu.make_async_copy(table_hbm, table, load_sem.at[3]),
        pltpu.make_async_copy(bases_hbm, bases, load_sem.at[4]),
    ]
    for copy in loads:
        copy.start()

    moments = [
        [
            remote(
                mom_own.at[c, pl.ds(starts[k], ranks[k])], mom_in.at[c, pl.ds(starts[k], ranks[k])],
                mom_send.at[c, k], mom_recv.at[c, k], z_at(k + 1),
            )
            for k in range(len(ranks))
        ]
        for c in range(CHUNKS)
    ]
    pieces = pieces_of(inner, cycles)
    crossings = []
    for k, (first, size) in enumerate(pieces):
        rows = pl.ds(first, size)
        source = (state_hbm if first == inner else fx_own).at[:, :, rows]
        targets = fx_left.at[:, :, rows], fx_right.at[:, :, rows]
        if first == 0:
            source, targets = low_own, (low_left, low_right)
        crossings.append(
            [
                remote(source, target, fx_send.at[side, k], fx_recv.at[side, k], device)
                for side, (target, device) in enumerate(zip(targets, (x_right, x_left)))
            ]
        )
    edges = [
        remote(edge_right, edge_from_left, edge_send.at[0], edge_recv.at[0], z_at(1)),
        remote(edge_left, edge_from_right, edge_send.at[1], edge_recv.at[1], z_at(count - 1)),
        remote(
            g_out.at[:, :, pl.ds(0, 8)], ghost, edge_send.at[2], edge_recv.at[2], z_at(count // 2)
        ),
    ]

    pl.semaphore_wait(barrier, len(peers))
    for copy in crossings[0]:
        copy.start()

    loads[0].wait()
    kept = jnp.broadcast_to(modes[...], (inner, inner)).astype(F32)
    same = lax.broadcasted_iota(jnp.int32, (inner, inner), 0) == lax.broadcasted_iota(
        jnp.int32, (inner, inner), 1
    )
    odd_count = 2.0 * jnp.sum(jnp.where(same, kept, 0.0), axis=1, keepdims=True) - 1.0
    share = odd_count * (1.0 / total)
    lane = lax.broadcasted_iota(jnp.int32, (inner, width), 1)
    place = (lax.rem(lane, cells) + d * cells).astype(F32)
    steps = (odd_count * place).astype(jnp.int32) & (2 * total - 1)
    sine, cosine = turns(steps, total)
    sines[...] = sine
    cosines[...] = cosine

    def axial_flux(values, x, rows):
        inverse = 1.0 / values[0]
        for f, part in enumerate(fluxes(values, 1, inverse, pressure_of(values, inverse))):
            fx_own[f, x, rows, :] = part

    loads[1].wait()
    loads[3].wait()
    out_table = table[pl.ds(2 * width, 2 * depth), :]
    contract_lanes = (((1,), (1,)), ((), ()))
    for c in range(CHUNKS):
        rows = pl.ds(c * span, span)
        for p, (f, x) in enumerate(planes):
            value = state[f, x, rows, :]
            for part, wave in enumerate((cosines, sines)):
                high, low = split(value * wave[rows, :])
                slot = pl.ds((2 * p + part) * span, span)
                x_high[c, slot, :] = high
                x_low[c, slot, :] = low
        sums = lax.dot_general(
            out_table, x_high[c], contract_lanes, preferred_element_type=F32
        ) + lax.dot_general(out_table, x_low[c], contract_lanes, preferred_element_type=F32)
        sums = sums[:depth] + sums[depth:]
        for k in range(len(ranks)):
            wrapped = (1 - 2 * ((d + k + 1) // count)).astype(F32)
            mom_own[c, pl.ds(starts[k], ranks[k]), :] = (
                sums[starts[k] : starts[k] + ranks[k]] * wrapped
            )
        for copy in moments[c]:
            copy.start()

    local_high, local_low = table[pl.ds(0, width), :], table[pl.ds(width, width), :]
    for c in range(CHUNKS):
        near[c] = mm(x_high[c], local_high) + mm(x_low[c], local_high) + mm(x_high[c], local_low)

    ends = [
        (first + size, pair) for (first, size), pair in zip(pieces, crossings) if first not in (0, inner)
    ]

    def base(which, part, tile):
        return bases[pl.ds((4 * which + 2 * part + tile) * width, width), :]

    def change_basis(which, tile, high, low):
        rows = high.shape[0]
        both = mm(jnp.concatenate([high, low], axis=0), base(which, 0, tile))
        return both[:rows] + both[rows:] + mm(high, base(which, 1, tile))

    in_table = table[pl.ds(2 * width + 2 * depth, stacked), :]
    for c in range(CHUNKS):
        for copy in moments[c]:
            copy.wait_recv()
        high = mom_in[c].astype(BF16).astype(F32)
        low = (mom_in[c] - high).astype(BF16).astype(F32)
        parts = [high, low, high]
        if stacked > 3 * depth:
            parts.append(jnp.zeros((stacked - 3 * depth, high.shape[1]), F32))
        stack = jnp.concatenate(parts, axis=0).T.astype(BF16)
        near[c] = near[c] + mm(stack, in_table)
        for first in reversed(range(0, span, BLOCK)) if c == 0 else range(0, span, BLOCK):
            rows = pl.ds(c * span + first, BLOCK)
            wave_sine, wave_cosine = sines[rows, :], cosines[rows, :]
            weight = share[c * span + first : c * span + first + BLOCK]
            for x in range(axial):
                values = []
                for f in range(fields):
                    slot = 2 * (f * axial + x) * span + first
                    kept_value = (
                        wave_sine * near[c, pl.ds(slot, BLOCK), :]
                        - wave_cosine * near[c, pl.ds(slot + span, BLOCK), :]
                        + weight * state[f, x, rows, :]
                    )
                    state[f, x, rows, :] = kept_value
                    values.append(kept_value)
                axial_flux(values, x, rows)
            for end, pair in ends:
                if 0 < end - (c * span + first) <= BLOCK:
                    for copy in pair:
                        copy.start()
        if c == 0:
            loads[4].wait()
            packed = 0.0
            for tile in range(2):
                rows = pl.ds(tile * TILE, TILE)
                value = jnp.concatenate([state[f, x, rows, :] for f, x in planes], axis=0)
                packed = packed + change_basis(0, tile, *split(value))
            for p, (f, x) in enumerate(planes):
                low_own[f, x] = packed[p * TILE : (p + 1) * TILE]
            for copy in crossings[2]:
                copy.start()

    radius_of = lambda first, size: (
        lax.broadcasted_iota(jnp.int32, (size, width), 0) + first
    ).astype(F32) + 0.5
    loads[2].wait()
    for first in range(0, cycles, BLOCK):
        rows = pl.ds(first, BLOCK)
        radius = radius_of(first, BLOCK)
        inv_radius = 1.0 / radius
        for x in range(axial):
            values = [state[f, x, rows, :] for f in range(fields)]
            inverse = 1.0 / values[0]
            pressure = pressure_of(values, inverse)
            for f, part in enumerate(fluxes(values, 3, inverse, pressure)):
                g_turn[f, x, rows, :] = part
            for f, part in enumerate(fluxes(values, 2, inverse, pressure)):
                g_out[f, x, rows, :] = part * radius
            rate[2, x, rows, :] = (values[3] * values[3] * inverse + pressure) * inv_radius
            rate[3, x, rows, :] = -(values[2] * values[3] * inverse) * inv_radius

    edge_lane = lax.broadcasted_iota(jnp.int32, (cycles, LANES), 1)
    pack_right = jnp.zeros((cycles, LANES), F32)
    pack_left = jnp.zeros((cycles, LANES), F32)
    for p, (f, x) in enumerate(planes):
        mine = (edge_lane >> 1) == p
        ends = g_turn[f, x, :, pl.ds(width - LANES, LANES)]
        pack_right = jnp.where(mine, pltpu.roll(ends, 2 * p + 2, 1), pack_right)
        heads = g_turn[f, x, :, pl.ds(0, LANES)]
        pack_left = jnp.where(mine, pltpu.roll(heads, 2 * p, 1) if p else heads, pack_left)
    edge_right[...] = pack_right
    edge_left[...] = pack_left
    for copy in edges:
        copy.start()

    inv_radius = 1.0 / radius_of(0, cycles)
    angular = inv_radius * (1.0 / (12.0 * (2.0 * math.pi / total)))
    radial = inv_radius * (1.0 / 12.0)
    tail_row = lax.broadcasted_iota(jnp.int32, (8, width), 0)
    beyond = jnp.where(
        tail_row < 2, (tail_row.astype(F32) + (cycles + 0.5)) * (1.0 / (cycles - 0.5)), 0.0
    )
    for f, x in planes:
        g = g_turn[f, x]
        turn_term = 8.0 * (pltpu.roll(g, width - 1, 1) - pltpu.roll(g, 1, 1)) - (
            pltpu.roll(g, width - 2, 1) - pltpu.roll(g, 2, 1)
        )
        g = g_out[f, x]
        tall = cycles + 8
        g = jnp.concatenate([g, beyond * g[cycles - 1 :]], axis=0)
        out_term = (
            8.0 * (pltpu.roll(g, tall - 1, 0) - pltpu.roll(g, 1, 0))
            - (pltpu.roll(g, tall - 2, 0) - pltpu.roll(g, 2, 0))
        )[:cycles]
        change = -(turn_term * angular + out_term * radial)
        if f in (2, 3):
            change = change + rate[f, x]
        rate[f, x] = STEP_DT * change

    for copy in edges:
        copy.wait_recv()
    from_left = edge_from_left[...] - edge_right[...]
    from_right = edge_from_right[...] - edge_left[...]
    even = (edge_lane & 1) == 0
    scale = -STEP_DT * angular[:, :LANES]
    from_left = scale * jnp.where(
        even, from_left - 8.0 * pltpu.roll(from_left, LANES - 1, 1), from_left
    )
    from_right = scale * jnp.where(
        even, -from_right, 8.0 * pltpu.roll(from_right, 1, 1) - from_right
    )
    head, end = pl.ds(0, LANES), pl.ds((cells - 1) // LANES * LANES, LANES)
    end_lane = (cells - 2) % LANES
    ghost_row = lax.broadcasted_iota(jnp.int32, (8, width), 0)
    ghost_scale = -STEP_DT * radial[:8]
    for p, (f, x) in enumerate(planes):
        value = pltpu.roll(from_left, (LANES - 2 * p) % LANES, 1) if p else from_left
        rate[f, x, :, head] = rate[f, x, :, head] + jnp.where(edge_lane < 2, value, 0.0)
        value = pltpu.roll(from_right, (end_lane - 2 * p) % LANES, 1)
        mine = (edge_lane >= end_lane) & (edge_lane < end_lane + 2)
        rate[f, x, :, end] = rate[f, x, :, end] + jnp.where(mine, value, 0.0)
        tile = -ghost[f, x] if f in (2, 3) else ghost[f, x]
        inside = jnp.where(
            ghost_row == 0,
            pltpu.roll(tile, 7, 0) - 8.0 * tile,
            jnp.where(ghost_row == 1, pltpu.roll(tile, 1, 0), 0.0),
        )
        rate[f, x, pl.ds(0, 8), :] = rate[f, x, pl.ds(0, 8), :] + ghost_scale * inside

    def raw_flux(ref, x, rows):
        values = [ref[f, x, rows, :] for f in range(fields)]
        inverse = 1.0 / values[0]
        return fluxes(values, 1, inverse, pressure_of(values, inverse))

    for (begin, size), pair in zip(pieces, crossings):
        for copy in pair:
            copy.wait_recv()
        if begin == 0:
            high, low = split(
                jnp.concatenate([ref[f, x] for ref in (low_left, low_right) for f, x in planes], axis=0)
            )
            for tile in range(2):
                value = change_basis(1, tile, high, low)
                for side, ref in enumerate((fx_left, fx_right)):
                    for p, (f, x) in enumerate(planes):
                        row = (side * len(planes) + p) * TILE
                        ref[f, x, pl.ds(tile * TILE, TILE), :] = value[row : row + TILE]
        for first in range(begin, begin + size, 8):
            rows = pl.ds(first, 8)
            if begin in (0, inner):
                own, left, right = [
                    [raw_flux(ref, x, rows) for x in range(axial)] for ref in (state, fx_left, fx_right)
                ]
            else:
                own, left, right = [
                    [[ref[f, x, rows, :] for f in range(fields)] for x in range(axial)]
                    for ref in (fx_own, fx_left, fx_right)
                ]
            for f in range(fields):
                terms = (
                    8.0 * (own[1][f] - left[1][f]) - (right[0][f] - left[0][f]),
                    8.0 * (right[0][f] - own[0][f]) - (right[1][f] - left[1][f]),
                )
                for x, term in enumerate(terms):
                    out[f, x, rows, :] = rate[f, x, rows, :] - (STEP_DT / 12.0) * term

    for pair in crossings:
        for copy in pair:
            copy.wait_send()
    for group in moments:
        for copy in group:
            copy.wait_send()
    for copy in edges:
        copy.wait_send()


def shards(state, start, modes):
    fields, axial, cells, cycles = state.shape
    inner = modes.shape[0]
    cfg = dict(plan(cells, lax.axis_size("azim")), cells=cells)
    width, depth = cfg["width"], cfg["depth"]
    turned = state.transpose(0, 1, 3, 2)
    if width != cells:
        turned = jnp.concatenate([turned] * (width // cells), axis=3)
    full = (fields, axial, cycles, width)
    columns = 2 * fields * axial * inner // CHUNKS
    hbm = pl.BlockSpec(memory_space=pltpu.HBM)
    vmem = pl.BlockSpec(memory_space=pltpu.VMEM)
    peers, pieces = len(cfg["ranks"]), len(pieces_of(inner, cycles))
    tables = [jnp.asarray(cfg[name]) for name in ("table", "bases")]
    operands = (turned, modes.reshape(1, inner), *tables)
    step = pl.pallas_call(
        functools.partial(kernel, cfg),
        out_shape=jax.ShapeDtypeStruct(full, F32),
        in_specs=[hbm] * 4,
        out_specs=vmem,
        scratch_shapes=[
            pltpu.VMEM(full, F32),
            pltpu.VMEM((1, inner), jnp.int32),
            *[pltpu.VMEM(table.shape, BF16) for table in tables],
            pltpu.VMEM((inner, width), F32),
            pltpu.VMEM((inner, width), F32),
            pltpu.VMEM((CHUNKS, columns, width), BF16),
            pltpu.VMEM((CHUNKS, columns, width), BF16),
            pltpu.VMEM((CHUNKS, columns, width), F32),
            pltpu.VMEM((CHUNKS, depth, columns), F32),
            pltpu.VMEM((CHUNKS, depth, columns), F32),
        ]
        + [pltpu.VMEM(full, F32)] * 6
        + [pltpu.VMEM((fields, axial, TILE, width), F32)] * 3
        + [pltpu.VMEM((cycles, LANES), F32)] * 4
        + [
            pltpu.VMEM((fields, axial, 8, width), F32),
            pltpu.SemaphoreType.DMA((5,)),
            pltpu.SemaphoreType.DMA((CHUNKS, peers)),
            pltpu.SemaphoreType.DMA((CHUNKS, peers)),
            pltpu.SemaphoreType.DMA((2, pieces)),
            pltpu.SemaphoreType.DMA((2, pieces)),
            pltpu.SemaphoreType.DMA((3,)),
            pltpu.SemaphoreType.DMA((3,)),
        ],
        compiler_params=pltpu.CompilerParams(
            collective_id=0, has_side_effects=True, vmem_limit_bytes=48 * 1024 * 1024
        ),
        name="jet_section",
    )(*[pltpu.with_memory_space_constraint(operand, pltpu.HBM) for operand in operands])
    if width != cells:
        step = step[..., :cells]
    return start + step.transpose(0, 1, 3, 2)


def solution(mesh):
    in_specs = (P(None, "axial", "azim", None), P(None, "axial", "azim", None), P())
    out_specs = P(None, "axial", "azim", None)
    return jax.shard_map(shards, mesh=mesh, in_specs=in_specs, out_specs=out_specs, check_vma=False)
```

```python
import functools
import math

import jax
import jax.numpy as jnp
import numpy as np
from jax import lax
from jax.experimental import pallas as pl
from jax.experimental.pallas import tpu as pltpu
from jax.sharding import PartitionSpec as P

STEP_DT = 0.05
LANES = 128
CHUNKS = 2
BLOCK = 16
MSTEP = 8
TILE = 8
FLOOR = 1e-9
F32 = jnp.float32
BF16 = jnp.bfloat16
MESH = pl.DeviceIdType.MESH


def split_np(values):
    high = values.astype(np.float32).astype(jnp.bfloat16)
    low = (values - high.astype(np.float64)).astype(np.float32).astype(jnp.bfloat16)
    return high, low


def round_up(value, multiple):
    return -(-value // multiple) * multiple


@functools.lru_cache(None)
def plan(cells, count):
    total = cells * count
    width = round_up(cells, LANES)
    where = np.arange(cells)

    def coupling(offset):
        distance = offset * cells + where[:, None] - where[None, :]
        sine = np.sin(np.pi * distance / total)
        return np.where(distance == 0, 0.0, 1.0 / (total * np.where(distance == 0, 1.0, sine)))

    def wide(rows):
        return np.concatenate([rows] * (width // cells), axis=1)

    def padded(rows):
        return np.pad(rows, ((0, 0), (0, width - cells)))

    local = np.zeros((width, width))
    local[:cells] = wide(coupling(0).T)
    starts, ranks, outgoing, incoming = [], [], [], []
    for offset in range(1, count):
        left, values, right = np.linalg.svd(coupling(offset))
        rank = round_up(max(int(np.sum(values > FLOOR)), 1), 8)
        starts.append(sum(ranks))
        ranks.append(rank)
        outgoing.append(padded(right[:rank]))
        incoming.append(wide((left[:, :rank] * values[:rank]).T))
    depth = sum(ranks)
    out_high, out_low = split_np(np.concatenate(outgoing))
    in_high, in_low = split_np(np.concatenate(incoming))
    stacked = round_up(3 * depth, LANES)
    blank = np.zeros((stacked - 3 * depth, width), jnp.bfloat16)
    table = np.concatenate([*split_np(local), out_high, out_low, in_high, in_high, in_low, blank])

    def band(tile):
        bound = min(2 * MSTEP * TILE * (tile + 1), total // 2)
        waves = np.arange(1, bound)
        phase = 2 * np.pi * ((where[:, None] * waves) % total) / total
        scale = np.sqrt(2.0 / total)
        columns = [np.full((cells, 1), 1.0 / np.sqrt(total)), scale * np.cos(phase), scale * np.sin(phase)]
        left, values, _ = np.linalg.svd(np.concatenate(columns, axis=1))
        return left, int(np.sum(values > FLOOR))

    (first, low), (second, high) = band(0), band(1)
    assert low + high <= width
    low = min(cells, low + (width - low - high) // 2)
    high = min(cells, width - low)
    pack, unpack = [], []
    for base, lanes in ((first[:, :low], (0, low)), (second[:, :high], (low, low + high))):
        into = np.zeros((width, width))
        into[:cells, lanes[0] : lanes[1]] = base
        out_of = np.zeros((width, width))
        out_of[lanes[0] : lanes[1]] = wide(base.T)
        pack.append(split_np(into))
        unpack.append(split_np(out_of))
    bases = np.concatenate(
        [pair[part] for pairs in (pack, unpack) for part in range(2) for pair in pairs]
    )
    return dict(
        width=width, depth=depth, stacked=stacked, starts=starts, ranks=ranks, table=table, bases=bases
    )


def pieces_of(inner, cycles):
    span = inner // CHUNKS
    half = span // 2
    pieces = [(inner, cycles - inner), (2 * TILE, span - 2 * TILE), (0, 2 * TILE)]
    pieces += [(c * span, span) for c in range(1, CHUNKS - 1)]
    return pieces + [(inner - span, half), (inner - half, half // 2), (inner - half // 2, half // 2)]


def split(values):
    high = values.astype(BF16)
    return high, (values - high.astype(F32)).astype(BF16)


def mm(a, b):
    return jnp.dot(a, b, preferred_element_type=F32)


def pressure_of(values, inverse):
    kinetic = (values[1] * values[1] + values[2] * values[2] + values[3] * values[3]) * inverse
    return 0.4 * (values[4] - 0.5 * kinetic)


def fluxes(values, direction, inverse, pressure):
    velocity = values[direction] * inverse
    parts = [
        values[direction],
        values[1] * velocity,
        values[2] * velocity,
        values[3] * velocity,
        (values[4] + pressure) * velocity,
    ]
    parts[direction] = parts[direction] + pressure
    return parts


def turns(steps, total):
    quarter = total // 2
    quadrant = (steps + quarter // 2) // quarter
    angle = (steps - quadrant * quarter).astype(F32) * (math.pi / total)
    square = angle * angle
    sine = angle + angle * square * (
        -1.0 / 6 + square * (1.0 / 120 + square * (-1.0 / 5040 + square * (1.0 / 362880)))
    )
    cosine = 1.0 + square * (
        -0.5
        + square * (1.0 / 24 + square * (-1.0 / 720 + square * (1.0 / 40320 - square * (1.0 / 3628800))))
    )
    odd = (quadrant & 1) == 1
    first, second = jnp.where(odd, cosine, sine), jnp.where(odd, sine, cosine)
    return (
        jnp.where((quadrant & 2) == 2, -first, first),
        jnp.where(((quadrant + 1) & 2) == 2, -second, second),
    )


def kernel(
    cfg,
    state_hbm, modes_hbm, table_hbm, bases_hbm, out,
    state, modes, table, bases, cosines, sines,
    x_high, x_low, near, mom_own, mom_in,
    fx_own, fx_left, fx_right, g_turn, g_out, rate, low_own, low_left, low_right,
    edge_right, edge_left, edge_from_left, edge_from_right, ghost,
    load_sem, mom_send, mom_recv, fx_send, fx_recv, edge_send, edge_recv,
):
    fields, axial, cycles, width = state.shape
    cells, inner = cfg["cells"], modes.shape[1]
    depth, stacked = cfg["depth"], cfg["stacked"]
    starts, ranks = cfg["starts"], cfg["ranks"]
    count, ring = lax.axis_size("azim"), lax.axis_size("axial")
    d, a = lax.axis_index("azim"), lax.axis_index("axial")
    total = cells * count
    planes = [(f, x) for f in range(fields) for x in range(axial)]
    span = inner // CHUNKS

    def z_at(offset):
        return {"azim": lax.rem(d + offset, count)}

    x_right = {"axial": lax.rem(a + 1, ring)}
    x_left = {"axial": lax.rem(a + ring - 1, ring)}

    def remote(src, dst, send, recv, device):
        return pltpu.make_async_remote_copy(
            src_ref=src, dst_ref=dst, send_sem=send, recv_sem=recv,
            device_id=device, device_id_type=MESH,
        )

    outer_rows, inner_rows = pl.ds(inner, cycles - inner), pl.ds(0, inner)
    barrier = pltpu.get_barrier_semaphore()
    leads = d == 0

    def greet(device):
        pl.semaphore_signal(barrier, inc=1, device_id=device, device_id_type=MESH)

    for device in (x_right, x_left):
        greet(device)
    for offset in range(1, count):
        pl.when(jnp.logical_not(leads) & (z_at(offset)["azim"] != 0))(
            functools.partial(greet, z_at(offset))
        )
    loads = [
        pltpu.make_async_copy(modes_hbm, modes, load_sem.at[0]),
        pltpu.make_async_copy(
            state_hbm.at[:, :, inner_rows], state.at[:, :, inner_rows], load_sem.at[1]
        ),
        pltpu.make_async_copy(
            state_hbm.at[:, :, outer_rows], state.at[:, :, outer_rows], load_sem.at[2]
        ),
        pltpu.make_async_copy(table_hbm, table, load_sem.at[3]),
        pltpu.make_async_copy(bases_hbm, bases, load_sem.at[4]),
    ]
    for copy in loads:
        copy.start()

    moments = [
        [
            remote(
                mom_own.at[c, pl.ds(starts[k], ranks[k])], mom_in.at[c, pl.ds(starts[k], ranks[k])],
                mom_send.at[c, k], mom_recv.at[c, k], z_at(k + 1),
            )
            for k in range(len(ranks))
        ]
        for c in range(CHUNKS)
    ]
    pieces = pieces_of(inner, cycles)
    crossings = []
    for k, (first, size) in enumerate(pieces):
        rows = pl.ds(first, size)
        source = (state_hbm if first == inner else fx_own).at[:, :, rows]
        targets = fx_left.at[:, :, rows], fx_right.at[:, :, rows]
        if first == 0:
            source, targets = low_own, (low_left, low_right)
        crossings.append(
            [
                remote(source, target, fx_send.at[side, k], fx_recv.at[side, k], device)
                for side, (target, device) in enumerate(zip(targets, (x_right, x_left)))
            ]
        )
    edges = [
        remote(edge_right, edge_from_left, edge_send.at[0], edge_recv.at[0], z_at(1)),
        remote(edge_left, edge_from_right, edge_send.at[1], edge_recv.at[1], z_at(count - 1)),
        remote(
            g_out.at[:, :, pl.ds(0, 8)], ghost, edge_send.at[2], edge_recv.at[2], z_at(count // 2)
        ),
    ]

    pl.semaphore_wait(barrier, jnp.where(leads, 2, count + 1))
    for copy in crossings[0]:
        copy.start()
    for offset in range(1, count):
        pl.when(leads | (z_at(offset)["azim"] == 0))(functools.partial(greet, z_at(offset)))

    loads[0].wait()
    kept = jnp.broadcast_to(modes[...], (inner, inner)).astype(F32)
    same = lax.broadcasted_iota(jnp.int32, (inner, inner), 0) == lax.broadcasted_iota(
        jnp.int32, (inner, inner), 1
    )
    odd_count = 2.0 * jnp.sum(jnp.where(same, kept, 0.0), axis=1, keepdims=True) - 1.0
    share = odd_count * (1.0 / total)
    lane = lax.broadcasted_iota(jnp.int32, (inner, width), 1)
    place = (lax.rem(lane, cells) + d * cells).astype(F32)
    steps = (odd_count * place).astype(jnp.int32) & (2 * total - 1)
    sine, cosine = turns(steps, total)
    sines[...] = sine
    cosines[...] = cosine

    def axial_flux(values, x, rows):
        inverse = 1.0 / values[0]
        for f, part in enumerate(fluxes(values, 1, inverse, pressure_of(values, inverse))):
            fx_own[f, x, rows, :] = part

    loads[1].wait()
    loads[3].wait()
    out_table = table[pl.ds(2 * width, 2 * depth), :]
    contract_lanes = (((1,), (1,)), ((), ()))
    for c in range(CHUNKS):
        rows = pl.ds(c * span, span)
        for p, (f, x) in enumerate(planes):
            value = state[f, x, rows, :]
            for part, wave in enumerate((cosines, sines)):
                high, low = split(value * wave[rows, :])
                slot = pl.ds((2 * p + part) * span, span)
                x_high[c, slot, :] = high
                x_low[c, slot, :] = low
        sums = lax.dot_general(
            out_table, x_high[c], contract_lanes, preferred_element_type=F32
        ) + lax.dot_general(out_table, x_low[c], contract_lanes, preferred_element_type=F32)
        sums = sums[:depth] + sums[depth:]
        for k in range(len(ranks)):
            wrapped = (1 - 2 * ((d + k + 1) // count)).astype(F32)
            mom_own[c, pl.ds(starts[k], ranks[k]), :] = (
                sums[starts[k] : starts[k] + ranks[k]] * wrapped
            )
        if c == 0:

            @pl.when(leads)
            def _():
                pl.semaphore_wait(barrier, count - 1)

        for copy in moments[c]:
            copy.start()

    local_high, local_low = table[pl.ds(0, width), :], table[pl.ds(width, width), :]
    for c in range(CHUNKS):
        near[c] = mm(x_high[c], local_high) + mm(x_low[c], local_high) + mm(x_high[c], local_low)

    ends = [
        (first + size, pair) for (first, size), pair in zip(pieces, crossings) if first not in (0, inner)
    ]

    def base(which, part, tile):
        return bases[pl.ds((4 * which + 2 * part + tile) * width, width), :]

    def change_basis(which, tile, high, low):
        rows = high.shape[0]
        both = mm(jnp.concatenate([high, low], axis=0), base(which, 0, tile))
        return both[:rows] + both[rows:] + mm(high, base(which, 1, tile))

    in_table = table[pl.ds(2 * width + 2 * depth, stacked), :]
    for c in range(CHUNKS):
        for copy in moments[c]:
            copy.wait_recv()
        high = mom_in[c].astype(BF16).astype(F32)
        low = (mom_in[c] - high).astype(BF16).astype(F32)
        parts = [high, low, high]
        if stacked > 3 * depth:
            parts.append(jnp.zeros((stacked - 3 * depth, high.shape[1]), F32))
        stack = jnp.concatenate(parts, axis=0).T.astype(BF16)
        near[c] = near[c] + mm(stack, in_table)
        for first in reversed(range(0, span, BLOCK)) if c == 0 else range(0, span, BLOCK):
            rows = pl.ds(c * span + first, BLOCK)
            wave_sine, wave_cosine = sines[rows, :], cosines[rows, :]
            weight = share[c * span + first : c * span + first + BLOCK]
            for x in range(axial):
                values = []
                for f in range(fields):
                    slot = 2 * (f * axial + x) * span + first
                    kept_value = (
                        wave_sine * near[c, pl.ds(slot, BLOCK), :]
                        - wave_cosine * near[c, pl.ds(slot + span, BLOCK), :]
                        + weight * state[f, x, rows, :]
                    )
                    state[f, x, rows, :] = kept_value
                    values.append(kept_value)
                axial_flux(values, x, rows)
            for end, pair in ends:
                if 0 < end - (c * span + first) <= BLOCK:
                    for copy in pair:
                        copy.start()
        if c == 0:
            loads[4].wait()
            packed = 0.0
            for tile in range(2):
                rows = pl.ds(tile * TILE, TILE)
                value = jnp.concatenate([state[f, x, rows, :] for f, x in planes], axis=0)
                packed = packed + change_basis(0, tile, *split(value))
            for p, (f, x) in enumerate(planes):
                low_own[f, x] = packed[p * TILE : (p + 1) * TILE]
            for copy in crossings[2]:
                copy.start()

    radius_of = lambda first, size: (
        lax.broadcasted_iota(jnp.int32, (size, width), 0) + first
    ).astype(F32) + 0.5
    loads[2].wait()
    for first in range(0, cycles, BLOCK):
        rows = pl.ds(first, BLOCK)
        radius = radius_of(first, BLOCK)
        inv_radius = 1.0 / radius
        for x in range(axial):
            values = [state[f, x, rows, :] for f in range(fields)]
            inverse = 1.0 / values[0]
            pressure = pressure_of(values, inverse)
            for f, part in enumerate(fluxes(values, 3, inverse, pressure)):
                g_turn[f, x, rows, :] = part
            for f, part in enumerate(fluxes(values, 2, inverse, pressure)):
                g_out[f, x, rows, :] = part * radius
            rate[2, x, rows, :] = (values[3] * values[3] * inverse + pressure) * inv_radius
            rate[3, x, rows, :] = -(values[2] * values[3] * inverse) * inv_radius

    edge_lane = lax.broadcasted_iota(jnp.int32, (cycles, LANES), 1)
    pack_right = jnp.zeros((cycles, LANES), F32)
    pack_left = jnp.zeros((cycles, LANES), F32)
    for p, (f, x) in enumerate(planes):
        mine = (edge_lane >> 1) == p
        ends = g_turn[f, x, :, pl.ds(width - LANES, LANES)]
        pack_right = jnp.where(mine, pltpu.roll(ends, 2 * p + 2, 1), pack_right)
        heads = g_turn[f, x, :, pl.ds(0, LANES)]
        pack_left = jnp.where(mine, pltpu.roll(heads, 2 * p, 1) if p else heads, pack_left)
    edge_right[...] = pack_right
    edge_left[...] = pack_left
    for copy in edges:
        copy.start()

    inv_radius = 1.0 / radius_of(0, cycles)
    angular = inv_radius * (1.0 / (12.0 * (2.0 * math.pi / total)))
    radial = inv_radius * (1.0 / 12.0)
    tail_row = lax.broadcasted_iota(jnp.int32, (8, width), 0)
    beyond = jnp.where(
        tail_row < 2, (tail_row.astype(F32) + (cycles + 0.5)) * (1.0 / (cycles - 0.5)), 0.0
    )
    for f, x in planes:
        g = g_turn[f, x]
        turn_term = 8.0 * (pltpu.roll(g, width - 1, 1) - pltpu.roll(g, 1, 1)) - (
            pltpu.roll(g, width - 2, 1) - pltpu.roll(g, 2, 1)
        )
        g = g_out[f, x]
        tall = cycles + 8
        g = jnp.concatenate([g, beyond * g[cycles - 1 :]], axis=0)
        out_term = (
            8.0 * (pltpu.roll(g, tall - 1, 0) - pltpu.roll(g, 1, 0))
            - (pltpu.roll(g, tall - 2, 0) - pltpu.roll(g, 2, 0))
        )[:cycles]
        change = -(turn_term * angular + out_term * radial)
        if f in (2, 3):
            change = change + rate[f, x]
        rate[f, x] = STEP_DT * change

    for copy in edges:
        copy.wait_recv()
    from_left = edge_from_left[...] - edge_right[...]
    from_right = edge_from_right[...] - edge_left[...]
    even = (edge_lane & 1) == 0
    scale = -STEP_DT * angular[:, :LANES]
    from_left = scale * jnp.where(
        even, from_left - 8.0 * pltpu.roll(from_left, LANES - 1, 1), from_left
    )
    from_right = scale * jnp.where(
        even, -from_right, 8.0 * pltpu.roll(from_right, 1, 1) - from_right
    )
    head, end = pl.ds(0, LANES), pl.ds((cells - 1) // LANES * LANES, LANES)
    end_lane = (cells - 2) % LANES
    ghost_row = lax.broadcasted_iota(jnp.int32, (8, width), 0)
    ghost_scale = -STEP_DT * radial[:8]
    for p, (f, x) in enumerate(planes):
        value = pltpu.roll(from_left, (LANES - 2 * p) % LANES, 1) if p else from_left
        rate[f, x, :, head] = rate[f, x, :, head] + jnp.where(edge_lane < 2, value, 0.0)
        value = pltpu.roll(from_right, (end_lane - 2 * p) % LANES, 1)
        mine = (edge_lane >= end_lane) & (edge_lane < end_lane + 2)
        rate[f, x, :, end] = rate[f, x, :, end] + jnp.where(mine, value, 0.0)
        tile = -ghost[f, x] if f in (2, 3) else ghost[f, x]
        inside = jnp.where(
            ghost_row == 0,
            pltpu.roll(tile, 7, 0) - 8.0 * tile,
            jnp.where(ghost_row == 1, pltpu.roll(tile, 1, 0), 0.0),
        )
        rate[f, x, pl.ds(0, 8), :] = rate[f, x, pl.ds(0, 8), :] + ghost_scale * inside

    def raw_flux(ref, x, rows):
        values = [ref[f, x, rows, :] for f in range(fields)]
        inverse = 1.0 / values[0]
        return fluxes(values, 1, inverse, pressure_of(values, inverse))

    for (begin, size), pair in zip(pieces, crossings):
        for copy in pair:
            copy.wait_recv()
        if begin == 0:
            high, low = split(
                jnp.concatenate([ref[f, x] for ref in (low_left, low_right) for f, x in planes], axis=0)
            )
            for tile in range(2):
                value = change_basis(1, tile, high, low)
                for side, ref in enumerate((fx_left, fx_right)):
                    for p, (f, x) in enumerate(planes):
                        row = (side * len(planes) + p) * TILE
                        ref[f, x, pl.ds(tile * TILE, TILE), :] = value[row : row + TILE]
        for first in range(begin, begin + size, 8):
            rows = pl.ds(first, 8)
            if begin in (0, inner):
                own, left, right = [
                    [raw_flux(ref, x, rows) for x in range(axial)] for ref in (state, fx_left, fx_right)
                ]
            else:
                own, left, right = [
                    [[ref[f, x, rows, :] for f in range(fields)] for x in range(axial)]
                    for ref in (fx_own, fx_left, fx_right)
                ]
            for f in range(fields):
                terms = (
                    8.0 * (own[1][f] - left[1][f]) - (right[0][f] - left[0][f]),
                    8.0 * (right[0][f] - own[0][f]) - (right[1][f] - left[1][f]),
                )
                for x, term in enumerate(terms):
                    out[f, x, rows, :] = rate[f, x, rows, :] - (STEP_DT / 12.0) * term

    for pair in crossings:
        for copy in pair:
            copy.wait_send()
    for group in moments:
        for copy in group:
            copy.wait_send()
    for copy in edges:
        copy.wait_send()


def shards(state, start, modes):
    fields, axial, cells, cycles = state.shape
    inner = modes.shape[0]
    cfg = dict(plan(cells, lax.axis_size("azim")), cells=cells)
    width, depth = cfg["width"], cfg["depth"]
    turned = state.transpose(0, 1, 3, 2)
    if width != cells:
        turned = jnp.concatenate([turned] * (width // cells), axis=3)
    full = (fields, axial, cycles, width)
    columns = 2 * fields * axial * inner // CHUNKS
    hbm = pl.BlockSpec(memory_space=pltpu.HBM)
    vmem = pl.BlockSpec(memory_space=pltpu.VMEM)
    peers, pieces = len(cfg["ranks"]), len(pieces_of(inner, cycles))
    tables = [jnp.asarray(cfg[name]) for name in ("table", "bases")]
    operands = (turned, modes.reshape(1, inner), *tables)
    step = pl.pallas_call(
        functools.partial(kernel, cfg),
        out_shape=jax.ShapeDtypeStruct(full, F32),
        in_specs=[hbm] * 4,
        out_specs=vmem,
        scratch_shapes=[
            pltpu.VMEM(full, F32),
            pltpu.VMEM((1, inner), jnp.int32),
            *[pltpu.VMEM(table.shape, BF16) for table in tables],
            pltpu.VMEM((inner, width), F32),
            pltpu.VMEM((inner, width), F32),
            pltpu.VMEM((CHUNKS, columns, width), BF16),
            pltpu.VMEM((CHUNKS, columns, width), BF16),
            pltpu.VMEM((CHUNKS, columns, width), F32),
            pltpu.VMEM((CHUNKS, depth, columns), F32),
            pltpu.VMEM((CHUNKS, depth, columns), F32),
        ]
        + [pltpu.VMEM(full, F32)] * 6
        + [pltpu.VMEM((fields, axial, TILE, width), F32)] * 3
        + [pltpu.VMEM((cycles, LANES), F32)] * 4
        + [
            pltpu.VMEM((fields, axial, 8, width), F32),
            pltpu.SemaphoreType.DMA((5,)),
            pltpu.SemaphoreType.DMA((CHUNKS, peers)),
            pltpu.SemaphoreType.DMA((CHUNKS, peers)),
            pltpu.SemaphoreType.DMA((2, pieces)),
            pltpu.SemaphoreType.DMA((2, pieces)),
            pltpu.SemaphoreType.DMA((3,)),
            pltpu.SemaphoreType.DMA((3,)),
        ],
        compiler_params=pltpu.CompilerParams(
            collective_id=0, has_side_effects=True, vmem_limit_bytes=48 * 1024 * 1024
        ),
        name="jet_section",
    )(*[pltpu.with_memory_space_constraint(operand, pltpu.HBM) for operand in operands])
    if width != cells:
        step = step[..., :cells]
    return start + step.transpose(0, 1, 3, 2)


def solution(mesh):
    in_specs = (P(None, "axial", "azim", None), P(None, "axial", "azim", None), P())
    out_specs = P(None, "axial", "azim", None)
    return jax.shard_map(shards, mesh=mesh, in_specs=in_specs, out_specs=out_specs, check_vma=False)
```

```python
import functools
import math

import jax
import jax.numpy as jnp
import numpy as np
from jax import lax
from jax.experimental import pallas as pl
from jax.experimental.pallas import tpu as pltpu
from jax.sharding import PartitionSpec as P

STEP_DT = 0.05
LANES = 128
CHUNKS = 2
BLOCK = 16
MSTEP = 8
TILE = 8
GROUP = 4
PACKED = 6
CUT = 1e-6
FLOOR = 1e-9
F32 = jnp.float32
BF16 = jnp.bfloat16
MESH = pl.DeviceIdType.MESH


def split_np(values):
    high = values.astype(np.float32).astype(jnp.bfloat16)
    low = (values - high.astype(np.float64)).astype(np.float32).astype(jnp.bfloat16)
    return high, low


def round_up(value, multiple):
    return -(-value // multiple) * multiple


@functools.lru_cache(None)
def plan(cells, count):
    total = cells * count
    width = round_up(cells, LANES)
    where = np.arange(cells)

    def coupling(offset):
        distance = offset * cells + where[:, None] - where[None, :]
        sine = np.sin(np.pi * distance / total)
        return np.where(distance == 0, 0.0, 1.0 / (total * np.where(distance == 0, 1.0, sine)))

    def wide(rows):
        return np.concatenate([rows] * (width // cells), axis=1)

    def padded(rows):
        return np.pad(rows, ((0, 0), (0, width - cells)))

    local = np.zeros((width, width))
    local[:cells] = wide(coupling(0).T)
    starts, ranks, outgoing, incoming = [], [], [], []
    for offset in range(1, count):
        left, values, right = np.linalg.svd(coupling(offset))
        rank = round_up(max(int(np.sum(values > FLOOR)), 1), 8)
        starts.append(sum(ranks))
        ranks.append(rank)
        outgoing.append(padded(right[:rank]))
        incoming.append(wide((left[:, :rank] * values[:rank]).T))
    depth = sum(ranks)
    out_high, out_low = split_np(np.concatenate(outgoing))
    in_high, in_low = split_np(np.concatenate(incoming))
    stacked = round_up(3 * depth, LANES)
    blank = np.zeros((stacked - 3 * depth, width), jnp.bfloat16)
    table = np.concatenate([*split_np(local), out_high, out_low, in_high, in_high, in_low, blank])

    def band(group):
        bound = min(2 * MSTEP * GROUP * (group + 1), total // 2)
        waves = np.arange(1, bound)
        phase = 2 * np.pi * ((where[:, None] * waves) % total) / total
        scale = np.sqrt(2.0 / total)
        columns = [np.full((cells, 1), 1.0 / np.sqrt(total)), scale * np.cos(phase), scale * np.sin(phase)]
        left, values, _ = np.linalg.svd(np.concatenate(columns, axis=1))
        return left, np.append(values, np.zeros(cells + 1 - len(values)))

    blocks = [None] * PACKED
    for low in range(PACKED // 2):
        high = PACKED - 1 - low
        (first, first_values), (second, second_values) = band(low), band(high)
        sizes = range(max(width - cells, 0), min(cells, width) + 1)
        size = min(sizes, key=lambda n: max(first_values[n], second_values[width - n]))
        assert max(first_values[size], second_values[width - size]) < CUT
        blocks[low] = np.zeros((width, width))
        blocks[low][:cells, :size] = first[:, :size]
        blocks[high] = np.zeros((width, width))
        blocks[high][:cells, size:] = second[:, : width - size]
    halves = [split_np(block) for block in blocks]
    bases = np.concatenate([pair[part] for part in range(2) for pair in halves])
    return dict(
        width=width, depth=depth, stacked=stacked, starts=starts, ranks=ranks, table=table, bases=bases
    )


def pieces_of(inner, cycles):
    span = inner // CHUNKS
    half = span // 2
    packed = PACKED * GROUP
    pieces = [(inner, cycles - inner), (packed, span - packed), (0, packed)]
    pieces += [(c * span, span) for c in range(1, CHUNKS - 1)]
    return pieces + [(inner - span, half), (inner - half, half // 2), (inner - half // 2, half // 2)]


def split(values):
    high = values.astype(BF16)
    return high, (values - high.astype(F32)).astype(BF16)


def mm(a, b):
    return jnp.dot(a, b, preferred_element_type=F32)


def mm_lanes(a, b):
    return lax.dot_general(a, b, (((1,), (1,)), ((), ())), preferred_element_type=F32)


def pressure_of(values, inverse):
    kinetic = (values[1] * values[1] + values[2] * values[2] + values[3] * values[3]) * inverse
    return 0.4 * (values[4] - 0.5 * kinetic)


def fluxes(values, direction, inverse, pressure):
    velocity = values[direction] * inverse
    parts = [
        values[direction],
        values[1] * velocity,
        values[2] * velocity,
        values[3] * velocity,
        (values[4] + pressure) * velocity,
    ]
    parts[direction] = parts[direction] + pressure
    return parts


def turns(steps, total):
    quarter = total // 2
    quadrant = (steps + quarter // 2) // quarter
    angle = (steps - quadrant * quarter).astype(F32) * (math.pi / total)
    square = angle * angle
    sine = angle + angle * square * (
        -1.0 / 6 + square * (1.0 / 120 + square * (-1.0 / 5040 + square * (1.0 / 362880)))
    )
    cosine = 1.0 + square * (
        -0.5
        + square * (1.0 / 24 + square * (-1.0 / 720 + square * (1.0 / 40320 - square * (1.0 / 3628800))))
    )
    odd = (quadrant & 1) == 1
    first, second = jnp.where(odd, cosine, sine), jnp.where(odd, sine, cosine)
    return (
        jnp.where((quadrant & 2) == 2, -first, first),
        jnp.where(((quadrant + 1) & 2) == 2, -second, second),
    )


def kernel(
    cfg,
    state_hbm, modes_hbm, table_hbm, bases_hbm, out,
    state, modes, table, bases, cosines, sines,
    x_high, x_low, near, mom_own, mom_in,
    fx_own, fx_left, fx_right, g_turn, g_out, rate, low_own, low_left, low_right,
    edge_right, edge_left, edge_from_left, edge_from_right, ghost,
    load_sem, mom_send, mom_recv, fx_send, fx_recv, edge_send, edge_recv,
):
    fields, axial, cycles, width = state.shape
    cells, inner = cfg["cells"], modes.shape[1]
    depth, stacked = cfg["depth"], cfg["stacked"]
    starts, ranks = cfg["starts"], cfg["ranks"]
    count, ring = lax.axis_size("azim"), lax.axis_size("axial")
    d, a = lax.axis_index("azim"), lax.axis_index("axial")
    total = cells * count
    planes = [(f, x) for f in range(fields) for x in range(axial)]
    span = inner // CHUNKS

    def z_at(offset):
        return {"azim": lax.rem(d + offset, count)}

    x_right = {"axial": lax.rem(a + 1, ring)}
    x_left = {"axial": lax.rem(a + ring - 1, ring)}

    def remote(src, dst, send, recv, device):
        return pltpu.make_async_remote_copy(
            src_ref=src, dst_ref=dst, send_sem=send, recv_sem=recv,
            device_id=device, device_id_type=MESH,
        )

    outer_rows, inner_rows = pl.ds(inner, cycles - inner), pl.ds(0, inner)
    barrier = pltpu.get_barrier_semaphore()
    leads = d == 0

    def greet(device):
        pl.semaphore_signal(barrier, inc=1, device_id=device, device_id_type=MESH)

    for device in (x_right, x_left):
        greet(device)
    for offset in range(1, count):
        pl.when(jnp.logical_not(leads) & (z_at(offset)["azim"] != 0))(
            functools.partial(greet, z_at(offset))
        )
    loads = [
        pltpu.make_async_copy(modes_hbm, modes, load_sem.at[0]),
        pltpu.make_async_copy(
            state_hbm.at[:, :, inner_rows], state.at[:, :, inner_rows], load_sem.at[1]
        ),
        pltpu.make_async_copy(
            state_hbm.at[:, :, outer_rows], state.at[:, :, outer_rows], load_sem.at[2]
        ),
        pltpu.make_async_copy(table_hbm, table, load_sem.at[3]),
        pltpu.make_async_copy(bases_hbm, bases, load_sem.at[4]),
    ]
    for copy in loads:
        copy.start()

    moments = [
        [
            remote(
                mom_own.at[c, pl.ds(starts[k], ranks[k])], mom_in.at[c, pl.ds(starts[k], ranks[k])],
                mom_send.at[c, k], mom_recv.at[c, k], z_at(k + 1),
            )
            for k in range(len(ranks))
        ]
        for c in range(CHUNKS)
    ]
    pieces = pieces_of(inner, cycles)
    crossings = []
    for k, (first, size) in enumerate(pieces):
        rows = pl.ds(first, size)
        source = (state_hbm if first == inner else fx_own).at[:, :, rows]
        targets = fx_left.at[:, :, rows], fx_right.at[:, :, rows]
        if first == 0:
            source, targets = low_own, (low_left, low_right)
        crossings.append(
            [
                remote(source, target, fx_send.at[side, k], fx_recv.at[side, k], device)
                for side, (target, device) in enumerate(zip(targets, (x_right, x_left)))
            ]
        )
    edges = [
        remote(edge_right, edge_from_left, edge_send.at[0], edge_recv.at[0], z_at(1)),
        remote(edge_left, edge_from_right, edge_send.at[1], edge_recv.at[1], z_at(count - 1)),
        remote(
            g_out.at[:, :, pl.ds(0, 8)], ghost, edge_send.at[2], edge_recv.at[2], z_at(count // 2)
        ),
    ]

    pl.semaphore_wait(barrier, jnp.where(leads, 2, count + 1))
    for copy in crossings[0]:
        copy.start()
    for offset in range(1, count):
        pl.when(leads | (z_at(offset)["azim"] == 0))(functools.partial(greet, z_at(offset)))

    loads[0].wait()
    kept = jnp.broadcast_to(modes[...], (inner, inner)).astype(F32)
    same = lax.broadcasted_iota(jnp.int32, (inner, inner), 0) == lax.broadcasted_iota(
        jnp.int32, (inner, inner), 1
    )
    odd_count = 2.0 * jnp.sum(jnp.where(same, kept, 0.0), axis=1, keepdims=True) - 1.0
    share = odd_count * (1.0 / total)
    lane = lax.broadcasted_iota(jnp.int32, (inner, width), 1)
    place = (lax.rem(lane, cells) + d * cells).astype(F32)
    steps = (odd_count * place).astype(jnp.int32) & (2 * total - 1)
    sine, cosine = turns(steps, total)
    sines[...] = sine
    cosines[...] = cosine

    def axial_flux(values, x, rows):
        inverse = 1.0 / values[0]
        for f, part in enumerate(fluxes(values, 1, inverse, pressure_of(values, inverse))):
            fx_own[f, x, rows, :] = part

    loads[1].wait()
    loads[3].wait()
    out_table = table[pl.ds(2 * width, 2 * depth), :]
    for c in range(CHUNKS):
        rows = pl.ds(c * span, span)
        for p, (f, x) in enumerate(planes):
            value = state[f, x, rows, :]
            for part, wave in enumerate((cosines, sines)):
                high, low = split(value * wave[rows, :])
                slot = pl.ds((2 * p + part) * span, span)
                x_high[c, slot, :] = high
                x_low[c, slot, :] = low
        sums = mm_lanes(out_table, x_high[c]) + mm_lanes(out_table, x_low[c])
        sums = sums[:depth] + sums[depth:]
        for k in range(len(ranks)):
            wrapped = (1 - 2 * ((d + k + 1) // count)).astype(F32)
            mom_own[c, pl.ds(starts[k], ranks[k]), :] = (
                sums[starts[k] : starts[k] + ranks[k]] * wrapped
            )
        if c == 0:

            @pl.when(leads)
            def _():
                pl.semaphore_wait(barrier, count - 1)

        for copy in moments[c]:
            copy.start()

    local_high, local_low = table[pl.ds(0, width), :], table[pl.ds(width, width), :]
    for c in range(CHUNKS):
        near[c] = mm(x_high[c], local_high) + mm(x_low[c], local_high) + mm(x_high[c], local_low)

    ends = [
        (first + size, pair) for (first, size), pair in zip(pieces, crossings) if first not in (0, inner)
    ]

    def into_basis(group, high, low):
        rows, at = high.shape[0], lambda part: pl.ds((PACKED * part + group) * width, width)
        both = mm(jnp.concatenate([high, low], axis=0), bases[at(0), :])
        return both[:rows] + both[rows:] + mm(high, bases[at(1), :])

    def from_basis(group, high, low):
        rows, at = high.shape[0], lambda part: pl.ds((PACKED * part + group) * width, width)
        both = mm_lanes(jnp.concatenate([high, low], axis=0), bases[at(0), :])
        return both[:rows] + both[rows:] + mm_lanes(high, bases[at(1), :])

    def upper(rows):
        return (lax.broadcasted_iota(jnp.int32, (rows, width), 0) & GROUP) == 0

    def swapped(tile):
        return pltpu.roll(tile, GROUP, 0)

    in_table = table[pl.ds(2 * width + 2 * depth, stacked), :]
    for c in range(CHUNKS):
        for copy in moments[c]:
            copy.wait_recv()
        high = mom_in[c].astype(BF16).astype(F32)
        low = (mom_in[c] - high).astype(BF16).astype(F32)
        parts = [high, low, high]
        if stacked > 3 * depth:
            parts.append(jnp.zeros((stacked - 3 * depth, high.shape[1]), F32))
        stack = jnp.concatenate(parts, axis=0).T.astype(BF16)
        near[c] = near[c] + mm(stack, in_table)
        for first in reversed(range(0, span, BLOCK)) if c == 0 else range(0, span, BLOCK):
            rows = pl.ds(c * span + first, BLOCK)
            wave_sine, wave_cosine = sines[rows, :], cosines[rows, :]
            weight = share[c * span + first : c * span + first + BLOCK]
            for x in range(axial):
                values = []
                for f in range(fields):
                    slot = 2 * (f * axial + x) * span + first
                    kept_value = (
                        wave_sine * near[c, pl.ds(slot, BLOCK), :]
                        - wave_cosine * near[c, pl.ds(slot + span, BLOCK), :]
                        + weight * state[f, x, rows, :]
                    )
                    state[f, x, rows, :] = kept_value
                    values.append(kept_value)
                axial_flux(values, x, rows)
            for end, pair in ends:
                if 0 < end - (c * span + first) <= BLOCK:
                    for copy in pair:
                        copy.start()
        if c == 0:
            loads[4].wait()
            tiles = [
                [state[f, x, pl.ds(TILE * t, TILE), :] for f, x in planes] for t in range(PACKED * GROUP // TILE)
            ]
            first, middle, last = [split(jnp.concatenate(tile, axis=0)) for tile in tiles]
            middle_swapped, last_swapped = [
                split(jnp.concatenate([swapped(part) for part in tile], axis=0)) for tile in tiles[1:]
            ]
            outside = jnp.where(
                upper(len(planes) * TILE),
                into_basis(0, *first) + into_basis(5, *last_swapped),
                into_basis(1, *first) + into_basis(4, *last_swapped),
            )
            inside = into_basis(2, *middle) + into_basis(3, *middle_swapped)
            for p, (f, x) in enumerate(planes):
                low_own[f, x] = outside[p * TILE : (p + 1) * TILE]
            for f in range(fields):
                even, odd = [inside[p * TILE : (p + 1) * TILE] for p in (2 * f, 2 * f + 1)]
                low_own[f, axial] = jnp.where(upper(TILE), even, swapped(odd))
            for copy in crossings[2]:
                copy.start()

    radius_of = lambda first, size: (
        lax.broadcasted_iota(jnp.int32, (size, width), 0) + first
    ).astype(F32) + 0.5
    loads[2].wait()
    for first in range(0, cycles, BLOCK):
        rows = pl.ds(first, BLOCK)
        radius = radius_of(first, BLOCK)
        inv_radius = 1.0 / radius
        for x in range(axial):
            values = [state[f, x, rows, :] for f in range(fields)]
            inverse = 1.0 / values[0]
            pressure = pressure_of(values, inverse)
            for f, part in enumerate(fluxes(values, 3, inverse, pressure)):
                g_turn[f, x, rows, :] = part
            for f, part in enumerate(fluxes(values, 2, inverse, pressure)):
                g_out[f, x, rows, :] = part * radius
            rate[2, x, rows, :] = (values[3] * values[3] * inverse + pressure) * inv_radius
            rate[3, x, rows, :] = -(values[2] * values[3] * inverse) * inv_radius

    edge_lane = lax.broadcasted_iota(jnp.int32, (cycles, LANES), 1)
    pack_right = jnp.zeros((cycles, LANES), F32)
    pack_left = jnp.zeros((cycles, LANES), F32)
    for p, (f, x) in enumerate(planes):
        mine = (edge_lane >> 1) == p
        ends = g_turn[f, x, :, pl.ds(width - LANES, LANES)]
        pack_right = jnp.where(mine, pltpu.roll(ends, 2 * p + 2, 1), pack_right)
        heads = g_turn[f, x, :, pl.ds(0, LANES)]
        pack_left = jnp.where(mine, pltpu.roll(heads, 2 * p, 1) if p else heads, pack_left)
    edge_right[...] = pack_right
    edge_left[...] = pack_left
    for copy in edges:
        copy.start()

    inv_radius = 1.0 / radius_of(0, cycles)
    angular = inv_radius * (1.0 / (12.0 * (2.0 * math.pi / total)))
    radial = inv_radius * (1.0 / 12.0)
    tail_row = lax.broadcasted_iota(jnp.int32, (8, width), 0)
    beyond = jnp.where(
        tail_row < 2, (tail_row.astype(F32) + (cycles + 0.5)) * (1.0 / (cycles - 0.5)), 0.0
    )
    for f, x in planes:
        g = g_turn[f, x]
        turn_term = 8.0 * (pltpu.roll(g, width - 1, 1) - pltpu.roll(g, 1, 1)) - (
            pltpu.roll(g, width - 2, 1) - pltpu.roll(g, 2, 1)
        )
        g = g_out[f, x]
        tall = cycles + 8
        g = jnp.concatenate([g, beyond * g[cycles - 1 :]], axis=0)
        out_term = (
            8.0 * (pltpu.roll(g, tall - 1, 0) - pltpu.roll(g, 1, 0))
            - (pltpu.roll(g, tall - 2, 0) - pltpu.roll(g, 2, 0))
        )[:cycles]
        change = -(turn_term * angular + out_term * radial)
        if f in (2, 3):
            change = change + rate[f, x]
        rate[f, x] = STEP_DT * change

    for copy in edges:
        copy.wait_recv()
    from_left = edge_from_left[...] - edge_right[...]
    from_right = edge_from_right[...] - edge_left[...]
    even = (edge_lane & 1) == 0
    scale = -STEP_DT * angular[:, :LANES]
    from_left = scale * jnp.where(
        even, from_left - 8.0 * pltpu.roll(from_left, LANES - 1, 1), from_left
    )
    from_right = scale * jnp.where(
        even, -from_right, 8.0 * pltpu.roll(from_right, 1, 1) - from_right
    )
    head, end = pl.ds(0, LANES), pl.ds((cells - 1) // LANES * LANES, LANES)
    end_lane = (cells - 2) % LANES
    ghost_row = lax.broadcasted_iota(jnp.int32, (8, width), 0)
    ghost_scale = -STEP_DT * radial[:8]
    for p, (f, x) in enumerate(planes):
        value = pltpu.roll(from_left, (LANES - 2 * p) % LANES, 1) if p else from_left
        rate[f, x, :, head] = rate[f, x, :, head] + jnp.where(edge_lane < 2, value, 0.0)
        value = pltpu.roll(from_right, (end_lane - 2 * p) % LANES, 1)
        mine = (edge_lane >= end_lane) & (edge_lane < end_lane + 2)
        rate[f, x, :, end] = rate[f, x, :, end] + jnp.where(mine, value, 0.0)
        tile = -ghost[f, x] if f in (2, 3) else ghost[f, x]
        inside = jnp.where(
            ghost_row == 0,
            pltpu.roll(tile, 7, 0) - 8.0 * tile,
            jnp.where(ghost_row == 1, pltpu.roll(tile, 1, 0), 0.0),
        )
        rate[f, x, pl.ds(0, 8), :] = rate[f, x, pl.ds(0, 8), :] + ghost_scale * inside

    def raw_flux(ref, x, rows):
        values = [ref[f, x, rows, :] for f in range(fields)]
        inverse = 1.0 / values[0]
        return fluxes(values, 1, inverse, pressure_of(values, inverse))

    for (begin, size), pair in zip(pieces, crossings):
        for copy in pair:
            copy.wait_recv()
        if begin == 0:
            sides = (low_left, low_right)
            outside = split(jnp.concatenate([ref[f, x] for ref in sides for f, x in planes], axis=0))
            inside = split(jnp.concatenate([ref[f, axial] for ref in sides for f in range(fields)], axis=0))
            half = upper(2 * len(planes) * TILE)
            head = jnp.where(half, from_basis(0, *outside), from_basis(1, *outside))
            last = jnp.where(half, from_basis(5, *outside), from_basis(4, *outside))
            second, third = from_basis(2, *inside), from_basis(3, *inside)
            for side, ref in enumerate((fx_left, fx_right)):
                for p, (f, x) in enumerate(planes):
                    row = (side * len(planes) + p) * TILE
                    ref[f, x, pl.ds(0, TILE), :] = head[row : row + TILE]
                    ref[f, x, pl.ds(2 * TILE, TILE), :] = swapped(last[row : row + TILE])
                    row = (side * fields + f) * TILE
                    early, late = second[row : row + TILE], third[row : row + TILE]
                    early, late = (early, swapped(late)) if x == 0 else (swapped(early), late)
                    ref[f, x, pl.ds(TILE, TILE), :] = jnp.where(upper(TILE), early, late)
        for first in range(begin, begin + size, 8):
            rows = pl.ds(first, 8)
            if begin in (0, inner):
                own, left, right = [
                    [raw_flux(ref, x, rows) for x in range(axial)] for ref in (state, fx_left, fx_right)
                ]
            else:
                own, left, right = [
                    [[ref[f, x, rows, :] for f in range(fields)] for x in range(axial)]
                    for ref in (fx_own, fx_left, fx_right)
                ]
            for f in range(fields):
                terms = (
                    8.0 * (own[1][f] - left[1][f]) - (right[0][f] - left[0][f]),
                    8.0 * (right[0][f] - own[0][f]) - (right[1][f] - left[1][f]),
                )
                for x, term in enumerate(terms):
                    out[f, x, rows, :] = rate[f, x, rows, :] - (STEP_DT / 12.0) * term

    for pair in crossings:
        for copy in pair:
            copy.wait_send()
    for group in moments:
        for copy in group:
            copy.wait_send()
    for copy in edges:
        copy.wait_send()


def shards(state, start, modes):
    fields, axial, cells, cycles = state.shape
    inner = modes.shape[0]
    cfg = dict(plan(cells, lax.axis_size("azim")), cells=cells)
    width, depth = cfg["width"], cfg["depth"]
    turned = state.transpose(0, 1, 3, 2)
    if width != cells:
        turned = jnp.concatenate([turned] * (width // cells), axis=3)
    full = (fields, axial, cycles, width)
    columns = 2 * fields * axial * inner // CHUNKS
    hbm = pl.BlockSpec(memory_space=pltpu.HBM)
    vmem = pl.BlockSpec(memory_space=pltpu.VMEM)
    peers, pieces = len(cfg["ranks"]), len(pieces_of(inner, cycles))
    tables = [jnp.asarray(cfg[name]) for name in ("table", "bases")]
    operands = (turned, modes.reshape(1, inner), *tables)
    step = pl.pallas_call(
        functools.partial(kernel, cfg),
        out_shape=jax.ShapeDtypeStruct(full, F32),
        in_specs=[hbm] * 4,
        out_specs=vmem,
        scratch_shapes=[
            pltpu.VMEM(full, F32),
            pltpu.VMEM((1, inner), jnp.int32),
            *[pltpu.VMEM(table.shape, BF16) for table in tables],
            pltpu.VMEM((inner, width), F32),
            pltpu.VMEM((inner, width), F32),
            pltpu.VMEM((CHUNKS, columns, width), BF16),
            pltpu.VMEM((CHUNKS, columns, width), BF16),
            pltpu.VMEM((CHUNKS, columns, width), F32),
            pltpu.VMEM((CHUNKS, depth, columns), F32),
            pltpu.VMEM((CHUNKS, depth, columns), F32),
        ]
        + [pltpu.VMEM(full, F32)] * 6
        + [pltpu.VMEM((fields, axial + 1, TILE, width), F32)] * 3
        + [pltpu.VMEM((cycles, LANES), F32)] * 4
        + [
            pltpu.VMEM((fields, axial, 8, width), F32),
            pltpu.SemaphoreType.DMA((5,)),
            pltpu.SemaphoreType.DMA((CHUNKS, peers)),
            pltpu.SemaphoreType.DMA((CHUNKS, peers)),
            pltpu.SemaphoreType.DMA((2, pieces)),
            pltpu.SemaphoreType.DMA((2, pieces)),
            pltpu.SemaphoreType.DMA((3,)),
            pltpu.SemaphoreType.DMA((3,)),
        ],
        compiler_params=pltpu.CompilerParams(
            collective_id=0, has_side_effects=True, vmem_limit_bytes=48 * 1024 * 1024
        ),
        name="jet_section",
    )(*[pltpu.with_memory_space_constraint(operand, pltpu.HBM) for operand in operands])
    if width != cells:
        step = step[..., :cells]
    return start + step.transpose(0, 1, 3, 2)


def solution(mesh):
    in_specs = (P(None, "axial", "azim", None), P(None, "axial", "azim", None), P())
    out_specs = P(None, "axial", "azim", None)
    return jax.shard_map(shards, mesh=mesh, in_specs=in_specs, out_specs=out_specs, check_vma=False)
```

```python
import functools
import math

import jax
import jax.numpy as jnp
import numpy as np
from jax import lax
from jax.experimental import pallas as pl
from jax.experimental.pallas import tpu as pltpu
from jax.sharding import PartitionSpec as P

STEP_DT = 0.05
LANES = 128
CHUNKS = 2
BLOCK = 16
MSTEP = 8
TILE = 8
GROUP = 4
PACKED = 6
CUT = 1e-6
FLOOR = 1e-9
F32 = jnp.float32
BF16 = jnp.bfloat16
MESH = pl.DeviceIdType.MESH


def split_np(values):
    high = values.astype(np.float32).astype(jnp.bfloat16)
    low = (values - high.astype(np.float64)).astype(np.float32).astype(jnp.bfloat16)
    return high, low


def round_up(value, multiple):
    return -(-value // multiple) * multiple


@functools.lru_cache(None)
def plan(cells, count):
    total = cells * count
    width = round_up(cells, LANES)
    where = np.arange(cells)

    def coupling(offset):
        distance = offset * cells + where[:, None] - where[None, :]
        sine = np.sin(np.pi * distance / total)
        return np.where(distance == 0, 0.0, 1.0 / (total * np.where(distance == 0, 1.0, sine)))

    def wide(rows):
        return np.concatenate([rows] * (width // cells), axis=1)

    def padded(rows):
        return np.pad(rows, ((0, 0), (0, width - cells)))

    local = np.zeros((width, width))
    local[:cells] = wide(coupling(0).T)
    starts, ranks, outgoing, incoming = [], [], [], []
    for offset in range(1, count):
        left, values, right = np.linalg.svd(coupling(offset))
        rank = round_up(max(int(np.sum(values > FLOOR)), 1), 8)
        starts.append(sum(ranks))
        ranks.append(rank)
        outgoing.append(padded(right[:rank]))
        incoming.append(wide((left[:, :rank] * values[:rank]).T))
    depth = sum(ranks)
    out_high, out_low = split_np(np.concatenate(outgoing))
    in_high, in_low = split_np(np.concatenate(incoming))
    stacked = round_up(3 * depth, LANES)
    blank = np.zeros((stacked - 3 * depth, width), jnp.bfloat16)
    table = np.concatenate([*split_np(local), out_high, out_low, in_high, in_high, in_low, blank])

    def band(group):
        bound = min(2 * MSTEP * GROUP * (group + 1), total // 2)
        waves = np.arange(1, bound)
        phase = 2 * np.pi * ((where[:, None] * waves) % total) / total
        scale = np.sqrt(2.0 / total)
        columns = [np.full((cells, 1), 1.0 / np.sqrt(total)), scale * np.cos(phase), scale * np.sin(phase)]
        left, values, _ = np.linalg.svd(np.concatenate(columns, axis=1))
        return left, np.append(values, np.zeros(cells + 1 - len(values)))

    blocks = [None] * PACKED
    for low in range(PACKED // 2):
        high = PACKED - 1 - low
        (first, first_values), (second, second_values) = band(low), band(high)
        sizes = range(max(width - cells, 0), min(cells, width) + 1)
        size = min(sizes, key=lambda n: max(first_values[n], second_values[width - n]))
        assert max(first_values[size], second_values[width - size]) < CUT
        blocks[low] = np.zeros((width, width))
        blocks[low][:cells, :size] = first[:, :size]
        blocks[high] = np.zeros((width, width))
        blocks[high][:cells, size:] = second[:, : width - size]
    halves = [split_np(block) for block in blocks]
    bases = np.concatenate([pair[part] for part in range(2) for pair in halves])
    return dict(
        width=width, depth=depth, stacked=stacked, starts=starts, ranks=ranks, table=table, bases=bases
    )


def pieces_of(inner, cycles):
    span = inner // CHUNKS
    half = span // 2
    packed = PACKED * GROUP
    pieces = [(inner, cycles - inner), (packed, span - packed), (0, packed)]
    pieces += [(c * span, span) for c in range(1, CHUNKS - 1)]
    return pieces + [(inner - span, half), (inner - half, half // 2), (inner - half // 2, half // 2)]


def split(values):
    high = values.astype(BF16)
    return high, (values - high.astype(F32)).astype(BF16)


def mm(a, b):
    return jnp.dot(a, b, preferred_element_type=F32)


def mm_lanes(a, b):
    return lax.dot_general(a, b, (((1,), (1,)), ((), ())), preferred_element_type=F32)


def pressure_of(values, inverse):
    kinetic = (values[1] * values[1] + values[2] * values[2] + values[3] * values[3]) * inverse
    return 0.4 * (values[4] - 0.5 * kinetic)


def fluxes(values, direction, inverse, pressure):
    velocity = values[direction] * inverse
    parts = [
        values[direction],
        values[1] * velocity,
        values[2] * velocity,
        values[3] * velocity,
        (values[4] + pressure) * velocity,
    ]
    parts[direction] = parts[direction] + pressure
    return parts


def turns(steps, total):
    quarter = total // 2
    quadrant = (steps + quarter // 2) // quarter
    angle = (steps - quadrant * quarter).astype(F32) * (math.pi / total)
    square = angle * angle
    sine = angle + angle * square * (
        -1.0 / 6 + square * (1.0 / 120 + square * (-1.0 / 5040 + square * (1.0 / 362880)))
    )
    cosine = 1.0 + square * (
        -0.5
        + square * (1.0 / 24 + square * (-1.0 / 720 + square * (1.0 / 40320 - square * (1.0 / 3628800))))
    )
    odd = (quadrant & 1) == 1
    first, second = jnp.where(odd, cosine, sine), jnp.where(odd, sine, cosine)
    return (
        jnp.where((quadrant & 2) == 2, -first, first),
        jnp.where(((quadrant + 1) & 2) == 2, -second, second),
    )


def kernel(
    cfg,
    state_hbm, start_hbm, modes_hbm, table_hbm, bases_hbm, out,
    state, begun, modes, table, bases, cosines, sines,
    x_high, x_low, near, mom_own, mom_in,
    fx_own, fx_left, fx_right, g_turn, g_out, rate, low_own, low_left, low_right,
    edge_right, edge_left, edge_from_left, edge_from_right, ghost,
    load_sem, mom_send, mom_recv, fx_send, fx_recv, edge_send, edge_recv,
):
    fields, axial, cycles, width = state.shape
    cells, inner = cfg["cells"], modes.shape[1]
    depth, stacked = cfg["depth"], cfg["stacked"]
    starts, ranks = cfg["starts"], cfg["ranks"]
    count, ring = lax.axis_size("azim"), lax.axis_size("axial")
    d, a = lax.axis_index("azim"), lax.axis_index("axial")
    total = cells * count
    planes = [(f, x) for f in range(fields) for x in range(axial)]
    span = inner // CHUNKS

    def z_at(offset):
        return {"azim": lax.rem(d + offset, count)}

    x_right = {"axial": lax.rem(a + 1, ring)}
    x_left = {"axial": lax.rem(a + ring - 1, ring)}

    def remote(src, dst, send, recv, device):
        return pltpu.make_async_remote_copy(
            src_ref=src, dst_ref=dst, send_sem=send, recv_sem=recv,
            device_id=device, device_id_type=MESH,
        )

    outer_rows, inner_rows = pl.ds(inner, cycles - inner), pl.ds(0, inner)
    barrier = pltpu.get_barrier_semaphore()
    leads = d == 0

    def greet(device):
        pl.semaphore_signal(barrier, inc=1, device_id=device, device_id_type=MESH)

    for device in (x_right, x_left):
        greet(device)
    for offset in range(1, count):
        pl.when(jnp.logical_not(leads) & (z_at(offset)["azim"] != 0))(
            functools.partial(greet, z_at(offset))
        )
    loads = [
        pltpu.make_async_copy(modes_hbm, modes, load_sem.at[0]),
        pltpu.make_async_copy(
            state_hbm.at[:, :, inner_rows], state.at[:, :, inner_rows], load_sem.at[1]
        ),
        pltpu.make_async_copy(
            state_hbm.at[:, :, outer_rows], state.at[:, :, outer_rows], load_sem.at[2]
        ),
        pltpu.make_async_copy(table_hbm, table, load_sem.at[3]),
        pltpu.make_async_copy(bases_hbm, bases, load_sem.at[4]),
        pltpu.make_async_copy(start_hbm, begun, load_sem.at[5]),
    ]
    for copy in loads:
        copy.start()

    moments = [
        [
            remote(
                mom_own.at[c, pl.ds(starts[k], ranks[k])], mom_in.at[c, pl.ds(starts[k], ranks[k])],
                mom_send.at[c, k], mom_recv.at[c, k], z_at(k + 1),
            )
            for k in range(len(ranks))
        ]
        for c in range(CHUNKS)
    ]
    pieces = pieces_of(inner, cycles)
    crossings = []
    for k, (first, size) in enumerate(pieces):
        rows = pl.ds(first, size)
        source = (state_hbm if first == inner else fx_own).at[:, :, rows]
        targets = fx_left.at[:, :, rows], fx_right.at[:, :, rows]
        if first == 0:
            source, targets = low_own, (low_left, low_right)
        crossings.append(
            [
                remote(source, target, fx_send.at[side, k], fx_recv.at[side, k], device)
                for side, (target, device) in enumerate(zip(targets, (x_right, x_left)))
            ]
        )
    edges = [
        remote(edge_right, edge_from_left, edge_send.at[0], edge_recv.at[0], z_at(1)),
        remote(edge_left, edge_from_right, edge_send.at[1], edge_recv.at[1], z_at(count - 1)),
        remote(
            g_out.at[:, :, pl.ds(0, 8)], ghost, edge_send.at[2], edge_recv.at[2], z_at(count // 2)
        ),
    ]

    pl.semaphore_wait(barrier, jnp.where(leads, 2, count + 1))
    for copy in crossings[0]:
        copy.start()
    for offset in range(1, count):
        pl.when(leads | (z_at(offset)["azim"] == 0))(functools.partial(greet, z_at(offset)))

    loads[0].wait()
    kept = jnp.broadcast_to(modes[...], (inner, inner)).astype(F32)
    same = lax.broadcasted_iota(jnp.int32, (inner, inner), 0) == lax.broadcasted_iota(
        jnp.int32, (inner, inner), 1
    )
    odd_count = 2.0 * jnp.sum(jnp.where(same, kept, 0.0), axis=1, keepdims=True) - 1.0
    share = odd_count * (1.0 / total)
    lane = lax.broadcasted_iota(jnp.int32, (inner, width), 1)
    place = (lax.rem(lane, cells) + d * cells).astype(F32)
    steps = (odd_count * place).astype(jnp.int32) & (2 * total - 1)
    sine, cosine = turns(steps, total)
    sines[...] = sine
    cosines[...] = cosine

    def axial_flux(values, x, rows):
        inverse = 1.0 / values[0]
        for f, part in enumerate(fluxes(values, 1, inverse, pressure_of(values, inverse))):
            fx_own[f, x, rows, :] = part

    loads[1].wait()
    loads[3].wait()
    out_table = table[pl.ds(2 * width, 2 * depth), :]
    for c in range(CHUNKS):
        rows = pl.ds(c * span, span)
        for p, (f, x) in enumerate(planes):
            value = state[f, x, rows, :]
            for part, wave in enumerate((cosines, sines)):
                high, low = split(value * wave[rows, :])
                slot = pl.ds((2 * p + part) * span, span)
                x_high[c, slot, :] = high
                x_low[c, slot, :] = low
        sums = mm_lanes(out_table, x_high[c]) + mm_lanes(out_table, x_low[c])
        sums = sums[:depth] + sums[depth:]
        for k in range(len(ranks)):
            wrapped = (1 - 2 * ((d + k + 1) // count)).astype(F32)
            mom_own[c, pl.ds(starts[k], ranks[k]), :] = (
                sums[starts[k] : starts[k] + ranks[k]] * wrapped
            )
        if c == 0:

            @pl.when(leads)
            def _():
                pl.semaphore_wait(barrier, count - 1)

        for copy in moments[c]:
            copy.start()

    local_high, local_low = table[pl.ds(0, width), :], table[pl.ds(width, width), :]
    for c in range(CHUNKS):
        near[c] = mm(x_high[c], local_high) + mm(x_low[c], local_high) + mm(x_high[c], local_low)

    ends = [
        (first + size, pair) for (first, size), pair in zip(pieces, crossings) if first not in (0, inner)
    ]

    def into_basis(group, high, low):
        rows, at = high.shape[0], lambda part: pl.ds((PACKED * part + group) * width, width)
        both = mm(jnp.concatenate([high, low], axis=0), bases[at(0), :])
        return both[:rows] + both[rows:] + mm(high, bases[at(1), :])

    def from_basis(group, high, low):
        rows, at = high.shape[0], lambda part: pl.ds((PACKED * part + group) * width, width)
        both = mm_lanes(jnp.concatenate([high, low], axis=0), bases[at(0), :])
        return both[:rows] + both[rows:] + mm_lanes(high, bases[at(1), :])

    def upper(rows):
        return (lax.broadcasted_iota(jnp.int32, (rows, width), 0) & GROUP) == 0

    def swapped(tile):
        return pltpu.roll(tile, GROUP, 0)

    in_table = table[pl.ds(2 * width + 2 * depth, stacked), :]
    for c in range(CHUNKS):
        for copy in moments[c]:
            copy.wait_recv()
        high = mom_in[c].astype(BF16).astype(F32)
        low = (mom_in[c] - high).astype(BF16).astype(F32)
        parts = [high, low, high]
        if stacked > 3 * depth:
            parts.append(jnp.zeros((stacked - 3 * depth, high.shape[1]), F32))
        stack = jnp.concatenate(parts, axis=0).T.astype(BF16)
        near[c] = near[c] + mm(stack, in_table)
        for first in reversed(range(0, span, BLOCK)) if c == 0 else range(0, span, BLOCK):
            rows = pl.ds(c * span + first, BLOCK)
            wave_sine, wave_cosine = sines[rows, :], cosines[rows, :]
            weight = share[c * span + first : c * span + first + BLOCK]
            for x in range(axial):
                values = []
                for f in range(fields):
                    slot = 2 * (f * axial + x) * span + first
                    kept_value = (
                        wave_sine * near[c, pl.ds(slot, BLOCK), :]
                        - wave_cosine * near[c, pl.ds(slot + span, BLOCK), :]
                        + weight * state[f, x, rows, :]
                    )
                    state[f, x, rows, :] = kept_value
                    values.append(kept_value)
                axial_flux(values, x, rows)
            for end, pair in ends:
                if 0 < end - (c * span + first) <= BLOCK:
                    for copy in pair:
                        copy.start()
        if c == 0:
            loads[4].wait()
            tiles = [
                [state[f, x, pl.ds(TILE * t, TILE), :] for f, x in planes] for t in range(PACKED * GROUP // TILE)
            ]
            first, middle, last = [split(jnp.concatenate(tile, axis=0)) for tile in tiles]
            middle_swapped, last_swapped = [
                split(jnp.concatenate([swapped(part) for part in tile], axis=0)) for tile in tiles[1:]
            ]
            outside = jnp.where(
                upper(len(planes) * TILE),
                into_basis(0, *first) + into_basis(5, *last_swapped),
                into_basis(1, *first) + into_basis(4, *last_swapped),
            )
            inside = into_basis(2, *middle) + into_basis(3, *middle_swapped)
            for p, (f, x) in enumerate(planes):
                low_own[f, x] = outside[p * TILE : (p + 1) * TILE]
            for f in range(fields):
                even, odd = [inside[p * TILE : (p + 1) * TILE] for p in (2 * f, 2 * f + 1)]
                low_own[f, axial] = jnp.where(upper(TILE), even, swapped(odd))
            for copy in crossings[2]:
                copy.start()

    radius_of = lambda first, size: (
        lax.broadcasted_iota(jnp.int32, (size, width), 0) + first
    ).astype(F32) + 0.5
    loads[2].wait()
    for first in range(0, cycles, BLOCK):
        rows = pl.ds(first, BLOCK)
        radius = radius_of(first, BLOCK)
        inv_radius = 1.0 / radius
        for x in range(axial):
            values = [state[f, x, rows, :] for f in range(fields)]
            inverse = 1.0 / values[0]
            pressure = pressure_of(values, inverse)
            for f, part in enumerate(fluxes(values, 3, inverse, pressure)):
                g_turn[f, x, rows, :] = part
            for f, part in enumerate(fluxes(values, 2, inverse, pressure)):
                g_out[f, x, rows, :] = part * radius
            rate[2, x, rows, :] = (values[3] * values[3] * inverse + pressure) * inv_radius
            rate[3, x, rows, :] = -(values[2] * values[3] * inverse) * inv_radius

    edge_lane = lax.broadcasted_iota(jnp.int32, (cycles, LANES), 1)
    pack_right = jnp.zeros((cycles, LANES), F32)
    pack_left = jnp.zeros((cycles, LANES), F32)
    for p, (f, x) in enumerate(planes):
        mine = (edge_lane >> 1) == p
        ends = g_turn[f, x, :, pl.ds(width - LANES, LANES)]
        pack_right = jnp.where(mine, pltpu.roll(ends, 2 * p + 2, 1), pack_right)
        heads = g_turn[f, x, :, pl.ds(0, LANES)]
        pack_left = jnp.where(mine, pltpu.roll(heads, 2 * p, 1) if p else heads, pack_left)
    edge_right[...] = pack_right
    edge_left[...] = pack_left
    for copy in edges:
        copy.start()

    loads[5].wait()
    inv_radius = 1.0 / radius_of(0, cycles)
    angular = inv_radius * (1.0 / (12.0 * (2.0 * math.pi / total)))
    radial = inv_radius * (1.0 / 12.0)
    tail_row = lax.broadcasted_iota(jnp.int32, (8, width), 0)
    beyond = jnp.where(
        tail_row < 2, (tail_row.astype(F32) + (cycles + 0.5)) * (1.0 / (cycles - 0.5)), 0.0
    )
    for f, x in planes:
        g = g_turn[f, x]
        turn_term = 8.0 * (pltpu.roll(g, width - 1, 1) - pltpu.roll(g, 1, 1)) - (
            pltpu.roll(g, width - 2, 1) - pltpu.roll(g, 2, 1)
        )
        g = g_out[f, x]
        tall = cycles + 8
        g = jnp.concatenate([g, beyond * g[cycles - 1 :]], axis=0)
        out_term = (
            8.0 * (pltpu.roll(g, tall - 1, 0) - pltpu.roll(g, 1, 0))
            - (pltpu.roll(g, tall - 2, 0) - pltpu.roll(g, 2, 0))
        )[:cycles]
        change = -(turn_term * angular + out_term * radial)
        if f in (2, 3):
            change = change + rate[f, x]
        rate[f, x] = begun[f, x] + STEP_DT * change

    for copy in edges:
        copy.wait_recv()
    from_left = edge_from_left[...] - edge_right[...]
    from_right = edge_from_right[...] - edge_left[...]
    even = (edge_lane & 1) == 0
    scale = -STEP_DT * angular[:, :LANES]
    from_left = scale * jnp.where(
        even, from_left - 8.0 * pltpu.roll(from_left, LANES - 1, 1), from_left
    )
    from_right = scale * jnp.where(
        even, -from_right, 8.0 * pltpu.roll(from_right, 1, 1) - from_right
    )
    head, end = pl.ds(0, LANES), pl.ds((cells - 1) // LANES * LANES, LANES)
    end_lane = (cells - 2) % LANES
    ghost_row = lax.broadcasted_iota(jnp.int32, (8, width), 0)
    ghost_scale = -STEP_DT * radial[:8]
    for p, (f, x) in enumerate(planes):
        value = pltpu.roll(from_left, (LANES - 2 * p) % LANES, 1) if p else from_left
        rate[f, x, :, head] = rate[f, x, :, head] + jnp.where(edge_lane < 2, value, 0.0)
        value = pltpu.roll(from_right, (end_lane - 2 * p) % LANES, 1)
        mine = (edge_lane >= end_lane) & (edge_lane < end_lane + 2)
        rate[f, x, :, end] = rate[f, x, :, end] + jnp.where(mine, value, 0.0)
        tile = -ghost[f, x] if f in (2, 3) else ghost[f, x]
        inside = jnp.where(
            ghost_row == 0,
            pltpu.roll(tile, 7, 0) - 8.0 * tile,
            jnp.where(ghost_row == 1, pltpu.roll(tile, 1, 0), 0.0),
        )
        rate[f, x, pl.ds(0, 8), :] = rate[f, x, pl.ds(0, 8), :] + ghost_scale * inside

    def raw_flux(ref, x, rows):
        values = [ref[f, x, rows, :] for f in range(fields)]
        inverse = 1.0 / values[0]
        return fluxes(values, 1, inverse, pressure_of(values, inverse))

    for (begin, size), pair in zip(pieces, crossings):
        for copy in pair:
            copy.wait_recv()
        if begin == 0:
            sides = (low_left, low_right)
            outside = split(jnp.concatenate([ref[f, x] for ref in sides for f, x in planes], axis=0))
            inside = split(jnp.concatenate([ref[f, axial] for ref in sides for f in range(fields)], axis=0))
            half = upper(2 * len(planes) * TILE)
            head = jnp.where(half, from_basis(0, *outside), from_basis(1, *outside))
            last = jnp.where(half, from_basis(5, *outside), from_basis(4, *outside))
            second, third = from_basis(2, *inside), from_basis(3, *inside)
            for side, ref in enumerate((fx_left, fx_right)):
                for p, (f, x) in enumerate(planes):
                    row = (side * len(planes) + p) * TILE
                    ref[f, x, pl.ds(0, TILE), :] = head[row : row + TILE]
                    ref[f, x, pl.ds(2 * TILE, TILE), :] = swapped(last[row : row + TILE])
                    row = (side * fields + f) * TILE
                    early, late = second[row : row + TILE], third[row : row + TILE]
                    early, late = (early, swapped(late)) if x == 0 else (swapped(early), late)
                    ref[f, x, pl.ds(TILE, TILE), :] = jnp.where(upper(TILE), early, late)
        for first in range(begin, begin + size, 8):
            rows = pl.ds(first, 8)
            if begin in (0, inner):
                own, left, right = [
                    [raw_flux(ref, x, rows) for x in range(axial)] for ref in (state, fx_left, fx_right)
                ]
            else:
                own, left, right = [
                    [[ref[f, x, rows, :] for f in range(fields)] for x in range(axial)]
                    for ref in (fx_own, fx_left, fx_right)
                ]
            for f in range(fields):
                terms = (
                    8.0 * (own[1][f] - left[1][f]) - (right[0][f] - left[0][f]),
                    8.0 * (right[0][f] - own[0][f]) - (right[1][f] - left[1][f]),
                )
                for x, term in enumerate(terms):
                    out[f, x, rows, :] = rate[f, x, rows, :] - (STEP_DT / 12.0) * term

    for pair in crossings:
        for copy in pair:
            copy.wait_send()
    for group in moments:
        for copy in group:
            copy.wait_send()
    for copy in edges:
        copy.wait_send()


def shards(state, start, modes):
    fields, axial, cells, cycles = state.shape
    inner = modes.shape[0]
    cfg = dict(plan(cells, lax.axis_size("azim")), cells=cells)
    width, depth = cfg["width"], cfg["depth"]
    turned, begun = [
        jnp.concatenate([values.transpose(0, 1, 3, 2)] * (width // cells), axis=3)
        for values in (state, start)
    ]
    full = (fields, axial, cycles, width)
    columns = 2 * fields * axial * inner // CHUNKS
    hbm = pl.BlockSpec(memory_space=pltpu.HBM)
    vmem = pl.BlockSpec(memory_space=pltpu.VMEM)
    peers, pieces = len(cfg["ranks"]), len(pieces_of(inner, cycles))
    tables = [jnp.asarray(cfg[name]) for name in ("table", "bases")]
    operands = (turned, begun, modes.reshape(1, inner), *tables)
    step = pl.pallas_call(
        functools.partial(kernel, cfg),
        out_shape=jax.ShapeDtypeStruct(full, F32),
        in_specs=[hbm] * 5,
        out_specs=vmem,
        scratch_shapes=[
            pltpu.VMEM(full, F32),
            pltpu.VMEM(full, F32),
            pltpu.VMEM((1, inner), jnp.int32),
            *[pltpu.VMEM(table.shape, BF16) for table in tables],
            pltpu.VMEM((inner, width), F32),
            pltpu.VMEM((inner, width), F32),
            pltpu.VMEM((CHUNKS, columns, width), BF16),
            pltpu.VMEM((CHUNKS, columns, width), BF16),
            pltpu.VMEM((CHUNKS, columns, width), F32),
            pltpu.VMEM((CHUNKS, depth, columns), F32),
            pltpu.VMEM((CHUNKS, depth, columns), F32),
        ]
        + [pltpu.VMEM(full, F32)] * 6
        + [pltpu.VMEM((fields, axial + 1, TILE, width), F32)] * 3
        + [pltpu.VMEM((cycles, LANES), F32)] * 4
        + [
            pltpu.VMEM((fields, axial, 8, width), F32),
            pltpu.SemaphoreType.DMA((6,)),
            pltpu.SemaphoreType.DMA((CHUNKS, peers)),
            pltpu.SemaphoreType.DMA((CHUNKS, peers)),
            pltpu.SemaphoreType.DMA((2, pieces)),
            pltpu.SemaphoreType.DMA((2, pieces)),
            pltpu.SemaphoreType.DMA((3,)),
            pltpu.SemaphoreType.DMA((3,)),
        ],
        compiler_params=pltpu.CompilerParams(
            collective_id=0, has_side_effects=True, vmem_limit_bytes=48 * 1024 * 1024
        ),
        name="jet_section",
    )(*[pltpu.with_memory_space_constraint(operand, pltpu.HBM) for operand in operands])
    return step[..., :cells].transpose(0, 1, 3, 2)


def solution(mesh):
    in_specs = (P(None, "axial", "azim", None), P(None, "axial", "azim", None), P())
    out_specs = P(None, "axial", "azim", None)
    return jax.shard_map(shards, mesh=mesh, in_specs=in_specs, out_specs=out_specs, check_vma=False)
```

```python
import functools
import math

import jax
import jax.numpy as jnp
import numpy as np
from jax import lax
from jax.experimental import pallas as pl
from jax.experimental.pallas import tpu as pltpu
from jax.sharding import PartitionSpec as P

STEP_DT = 0.05
LANES = 128
CHUNKS = 2
BLOCK = 16
MSTEP = 8
TILE = 8
GROUP = 4
PACKED = 6
CUT = 1e-6
LEVELS = 3
FLOOR = 1e-9
F32 = jnp.float32
BF16 = jnp.bfloat16
MESH = pl.DeviceIdType.MESH


def split_np(values):
    high = values.astype(np.float32).astype(jnp.bfloat16)
    low = (values - high.astype(np.float64)).astype(np.float32).astype(jnp.bfloat16)
    return high, low


def round_up(value, multiple):
    return -(-value // multiple) * multiple


@functools.lru_cache(None)
def plan(cells, count):
    total = cells * count
    width = round_up(cells, LANES)
    where = np.arange(cells)

    def coupling(offset):
        distance = offset * cells + where[:, None] - where[None, :]
        sine = np.sin(np.pi * distance / total)
        return np.where(distance == 0, 0.0, 1.0 / (total * np.where(distance == 0, 1.0, sine)))

    def wide(rows):
        return np.concatenate([rows] * (width // cells), axis=1)

    def padded(rows):
        return np.pad(rows, ((0, 0), (0, width - cells)))

    local = np.zeros((width, width))
    local[:cells] = wide(coupling(0).T)
    starts, ranks, outgoing, incoming = [], [], [], []
    for offset in range(1, count):
        left, values, right = np.linalg.svd(coupling(offset))
        rank = round_up(max(int(np.sum(values > FLOOR)), 1), 8)
        starts.append(sum(ranks))
        ranks.append(rank)
        outgoing.append(padded(right[:rank]))
        incoming.append(wide((left[:, :rank] * values[:rank]).T))
    depth = sum(ranks)
    out_high, out_low = split_np(np.concatenate(outgoing))
    in_high, in_low = split_np(np.concatenate(incoming))
    stacked = round_up(3 * depth, LANES)
    blank = np.zeros((stacked - 3 * depth, width), jnp.bfloat16)
    table = np.concatenate([*split_np(local), out_high, out_low, in_high, in_high, in_low, blank])

    def band(group):
        bound = min(2 * MSTEP * GROUP * (group + 1), total // 2)
        waves = np.arange(1, bound)
        phase = 2 * np.pi * ((where[:, None] * waves) % total) / total
        scale = np.sqrt(2.0 / total)
        columns = [np.full((cells, 1), 1.0 / np.sqrt(total)), scale * np.cos(phase), scale * np.sin(phase)]
        left, values, _ = np.linalg.svd(np.concatenate(columns, axis=1))
        return left, np.append(values, np.zeros(cells + 1 - len(values)))

    blocks = [None] * PACKED
    for low in range(PACKED // 2):
        high = PACKED - 1 - low
        (first, first_values), (second, second_values) = band(low), band(high)
        sizes = range(max(width - cells, 0), min(cells, width) + 1)
        size = min(sizes, key=lambda n: max(first_values[n], second_values[width - n]))
        assert max(first_values[size], second_values[width - size]) < CUT
        blocks[low] = np.zeros((width, width))
        blocks[low][:cells, :size] = first[:, :size]
        blocks[high] = np.zeros((width, width))
        blocks[high][:cells, size:] = second[:, : width - size]
    halves = [split_np(block) for block in blocks]
    bases = np.concatenate([pair[part] for part in range(2) for pair in halves])
    return dict(
        width=width, depth=depth, stacked=stacked, starts=starts, ranks=ranks, table=table, bases=bases
    )


def pieces_of(inner, cycles):
    span = inner // CHUNKS
    half = span // 2
    packed = PACKED * GROUP
    pieces = [(inner, cycles - inner), (packed, span - packed), (0, packed)]
    pieces += [(c * span, span) for c in range(1, CHUNKS - 1)]
    return pieces + [(inner - span, half), (inner - half, half // 2), (inner - half // 2, half // 2)]


def split(values):
    high = values.astype(BF16)
    return high, (values - high.astype(F32)).astype(BF16)


def mm(a, b):
    return jnp.dot(a, b, preferred_element_type=F32)


def mm_lanes(a, b):
    return lax.dot_general(a, b, (((1,), (1,)), ((), ())), preferred_element_type=F32)


def pressure_of(values, inverse):
    kinetic = (values[1] * values[1] + values[2] * values[2] + values[3] * values[3]) * inverse
    return 0.4 * (values[4] - 0.5 * kinetic)


def fluxes(values, direction, inverse, pressure):
    velocity = values[direction] * inverse
    parts = [
        values[direction],
        values[1] * velocity,
        values[2] * velocity,
        values[3] * velocity,
        (values[4] + pressure) * velocity,
    ]
    parts[direction] = parts[direction] + pressure
    return parts


def turns(steps, total):
    quarter = total // 2
    quadrant = (steps + quarter // 2) // quarter
    angle = (steps - quadrant * quarter).astype(F32) * (math.pi / total)
    square = angle * angle
    sine = angle + angle * square * (
        -1.0 / 6 + square * (1.0 / 120 + square * (-1.0 / 5040 + square * (1.0 / 362880)))
    )
    cosine = 1.0 + square * (
        -0.5
        + square * (1.0 / 24 + square * (-1.0 / 720 + square * (1.0 / 40320 - square * (1.0 / 3628800))))
    )
    odd = (quadrant & 1) == 1
    first, second = jnp.where(odd, cosine, sine), jnp.where(odd, sine, cosine)
    return (
        jnp.where((quadrant & 2) == 2, -first, first),
        jnp.where(((quadrant + 1) & 2) == 2, -second, second),
    )


def kernel(
    cfg,
    state_hbm, start_hbm, modes_hbm, table_hbm, bases_hbm, out,
    state, begun, modes, table, bases, cosines, sines,
    x_high, x_low, near, mom_own, mom_in,
    fx_own, fx_left, fx_right, g_turn, g_out, rate, low_own, low_left, low_right,
    edge_right, edge_left, edge_from_left, edge_from_right, ghost,
    load_sem, mom_send, mom_recv, fx_send, fx_recv, edge_send, edge_recv,
):
    fields, axial, cycles, width = state.shape
    cells, inner = cfg["cells"], modes.shape[1]
    depth, stacked = cfg["depth"], cfg["stacked"]
    starts, ranks = cfg["starts"], cfg["ranks"]
    count, ring = lax.axis_size("azim"), lax.axis_size("axial")
    d, a = lax.axis_index("azim"), lax.axis_index("axial")
    total = cells * count
    planes = [(f, x) for f in range(fields) for x in range(axial)]
    span = inner // CHUNKS

    def z_at(offset):
        return {"azim": lax.rem(d + offset, count)}

    x_right = {"axial": lax.rem(a + 1, ring)}
    x_left = {"axial": lax.rem(a + ring - 1, ring)}

    def remote(src, dst, send, recv, device):
        return pltpu.make_async_remote_copy(
            src_ref=src, dst_ref=dst, send_sem=send, recv_sem=recv,
            device_id=device, device_id_type=MESH,
        )

    outer_rows, inner_rows = pl.ds(inner, cycles - inner), pl.ds(0, inner)
    barrier = pltpu.get_barrier_semaphore()
    level = jnp.minimum(d, LEVELS - 1)
    level_mates = jnp.where(level == LEVELS - 1, count - LEVELS, 0)
    azim_peers = [z_at(offset) for offset in range(1, count)]
    peer_levels = [jnp.minimum(device["azim"], LEVELS - 1) for device in azim_peers]
    is_mate = [peer_level == level for peer_level in peer_levels]
    is_later = [peer_level > level for peer_level in peer_levels]

    def greet(device):
        pl.semaphore_signal(barrier, inc=1, device_id=device, device_id_type=MESH)

    for device in (x_right, x_left):
        greet(device)
    for device, mate in zip(azim_peers, is_mate):
        pl.when(mate)(functools.partial(greet, device))
    loads = [
        pltpu.make_async_copy(modes_hbm, modes, load_sem.at[0]),
        pltpu.make_async_copy(
            state_hbm.at[:, :, inner_rows], state.at[:, :, inner_rows], load_sem.at[1]
        ),
        pltpu.make_async_copy(
            state_hbm.at[:, :, outer_rows], state.at[:, :, outer_rows], load_sem.at[2]
        ),
        pltpu.make_async_copy(table_hbm, table, load_sem.at[3]),
        pltpu.make_async_copy(bases_hbm, bases, load_sem.at[4]),
        pltpu.make_async_copy(start_hbm, begun, load_sem.at[5]),
    ]
    for copy in loads:
        copy.start()

    moments = [
        [
            remote(
                mom_own.at[c, pl.ds(starts[k], ranks[k])], mom_in.at[c, pl.ds(starts[k], ranks[k])],
                mom_send.at[c, k], mom_recv.at[c, k], z_at(k + 1),
            )
            for k in range(len(ranks))
        ]
        for c in range(CHUNKS)
    ]
    pieces = pieces_of(inner, cycles)
    crossings = []
    for k, (first, size) in enumerate(pieces):
        rows = pl.ds(first, size)
        source = (state_hbm if first == inner else fx_own).at[:, :, rows]
        targets = fx_left.at[:, :, rows], fx_right.at[:, :, rows]
        if first == 0:
            source, targets = low_own, (low_left, low_right)
        crossings.append(
            [
                remote(source, target, fx_send.at[side, k], fx_recv.at[side, k], device)
                for side, (target, device) in enumerate(zip(targets, (x_right, x_left)))
            ]
        )
    edges = [
        remote(edge_right, edge_from_left, edge_send.at[0], edge_recv.at[0], z_at(1)),
        remote(edge_left, edge_from_right, edge_send.at[1], edge_recv.at[1], z_at(count - 1)),
        remote(
            g_out.at[:, :, pl.ds(0, 8)], ghost, edge_send.at[2], edge_recv.at[2], z_at(count // 2)
        ),
    ]

    pl.semaphore_wait(barrier, 2 + level + level_mates)
    for copy in crossings[0]:
        copy.start()
    for device, mate in zip(azim_peers, is_mate):
        pl.when(jnp.logical_not(mate))(functools.partial(greet, device))

    loads[0].wait()
    kept = jnp.broadcast_to(modes[...], (inner, inner)).astype(F32)
    same = lax.broadcasted_iota(jnp.int32, (inner, inner), 0) == lax.broadcasted_iota(
        jnp.int32, (inner, inner), 1
    )
    odd_count = 2.0 * jnp.sum(jnp.where(same, kept, 0.0), axis=1, keepdims=True) - 1.0
    share = odd_count * (1.0 / total)
    lane = lax.broadcasted_iota(jnp.int32, (inner, width), 1)
    place = (lax.rem(lane, cells) + d * cells).astype(F32)
    steps = (odd_count * place).astype(jnp.int32) & (2 * total - 1)
    sine, cosine = turns(steps, total)
    sines[...] = sine
    cosines[...] = cosine

    def axial_flux(values, x, rows):
        inverse = 1.0 / values[0]
        for f, part in enumerate(fluxes(values, 1, inverse, pressure_of(values, inverse))):
            fx_own[f, x, rows, :] = part

    loads[1].wait()
    loads[3].wait()
    out_table = table[pl.ds(2 * width, 2 * depth), :]
    for c in range(CHUNKS):
        rows = pl.ds(c * span, span)
        for p, (f, x) in enumerate(planes):
            value = state[f, x, rows, :]
            for part, wave in enumerate((cosines, sines)):
                high, low = split(value * wave[rows, :])
                slot = pl.ds((2 * p + part) * span, span)
                x_high[c, slot, :] = high
                x_low[c, slot, :] = low
        sums = mm_lanes(out_table, x_high[c]) + mm_lanes(out_table, x_low[c])
        sums = sums[:depth] + sums[depth:]
        for k in range(len(ranks)):
            wrapped = (1 - 2 * ((d + k + 1) // count)).astype(F32)
            mom_own[c, pl.ds(starts[k], ranks[k]), :] = (
                sums[starts[k] : starts[k] + ranks[k]] * wrapped
            )
        if c == 0:
            for copy, later in zip(moments[c], is_later):
                pl.when(jnp.logical_not(later))(copy.start)

            @pl.when(level < LEVELS - 1)
            def _():
                pl.semaphore_wait(barrier, count - 1 - level)

            for copy, later in zip(moments[c], is_later):
                pl.when(later)(copy.start)
        else:
            for copy in moments[c]:
                copy.start()

    local_high, local_low = table[pl.ds(0, width), :], table[pl.ds(width, width), :]
    for c in range(CHUNKS):
        near[c] = mm(x_high[c], local_high) + mm(x_low[c], local_high) + mm(x_high[c], local_low)

    ends = [
        (first + size, pair) for (first, size), pair in zip(pieces, crossings) if first not in (0, inner)
    ]

    def into_basis(group, high, low):
        rows, at = high.shape[0], lambda part: pl.ds((PACKED * part + group) * width, width)
        both = mm(jnp.concatenate([high, low], axis=0), bases[at(0), :])
        return both[:rows] + both[rows:] + mm(high, bases[at(1), :])

    def from_basis(group, high, low):
        rows, at = high.shape[0], lambda part: pl.ds((PACKED * part + group) * width, width)
        both = mm_lanes(jnp.concatenate([high, low], axis=0), bases[at(0), :])
        return both[:rows] + both[rows:] + mm_lanes(high, bases[at(1), :])

    def upper(rows):
        return (lax.broadcasted_iota(jnp.int32, (rows, width), 0) & GROUP) == 0

    def swapped(tile):
        return pltpu.roll(tile, GROUP, 0)

    in_table = table[pl.ds(2 * width + 2 * depth, stacked), :]
    for c in range(CHUNKS):
        for copy in moments[c]:
            copy.wait_recv()
        high = mom_in[c].astype(BF16).astype(F32)
        low = (mom_in[c] - high).astype(BF16).astype(F32)
        parts = [high, low, high]
        if stacked > 3 * depth:
            parts.append(jnp.zeros((stacked - 3 * depth, high.shape[1]), F32))
        stack = jnp.concatenate(parts, axis=0).T.astype(BF16)
        near[c] = near[c] + mm(stack, in_table)
        for first in reversed(range(0, span, BLOCK)) if c == 0 else range(0, span, BLOCK):
            rows = pl.ds(c * span + first, BLOCK)
            wave_sine, wave_cosine = sines[rows, :], cosines[rows, :]
            weight = share[c * span + first : c * span + first + BLOCK]
            for x in range(axial):
                values = []
                for f in range(fields):
                    slot = 2 * (f * axial + x) * span + first
                    kept_value = (
                        wave_sine * near[c, pl.ds(slot, BLOCK), :]
                        - wave_cosine * near[c, pl.ds(slot + span, BLOCK), :]
                        + weight * state[f, x, rows, :]
                    )
                    state[f, x, rows, :] = kept_value
                    values.append(kept_value)
                axial_flux(values, x, rows)
            for end, pair in ends:
                if 0 < end - (c * span + first) <= BLOCK:
                    for copy in pair:
                        copy.start()
        if c == 0:
            loads[4].wait()
            tiles = [
                [state[f, x, pl.ds(TILE * t, TILE), :] for f, x in planes] for t in range(PACKED * GROUP // TILE)
            ]
            first, middle, last = [split(jnp.concatenate(tile, axis=0)) for tile in tiles]
            middle_swapped, last_swapped = [
                split(jnp.concatenate([swapped(part) for part in tile], axis=0)) for tile in tiles[1:]
            ]
            outside = jnp.where(
                upper(len(planes) * TILE),
                into_basis(0, *first) + into_basis(5, *last_swapped),
                into_basis(1, *first) + into_basis(4, *last_swapped),
            )
            inside = into_basis(2, *middle) + into_basis(3, *middle_swapped)
            for p, (f, x) in enumerate(planes):
                low_own[f, x] = outside[p * TILE : (p + 1) * TILE]
            for f in range(fields):
                even, odd = [inside[p * TILE : (p + 1) * TILE] for p in (2 * f, 2 * f + 1)]
                low_own[f, axial] = jnp.where(upper(TILE), even, swapped(odd))
            for copy in crossings[2]:
                copy.start()

    radius_of = lambda first, size: (
        lax.broadcasted_iota(jnp.int32, (size, width), 0) + first
    ).astype(F32) + 0.5
    loads[2].wait()
    for first in range(0, cycles, BLOCK):
        rows = pl.ds(first, BLOCK)
        radius = radius_of(first, BLOCK)
        inv_radius = 1.0 / radius
        for x in range(axial):
            values = [state[f, x, rows, :] for f in range(fields)]
            inverse = 1.0 / values[0]
            pressure = pressure_of(values, inverse)
            for f, part in enumerate(fluxes(values, 3, inverse, pressure)):
                g_turn[f, x, rows, :] = part
            for f, part in enumerate(fluxes(values, 2, inverse, pressure)):
                g_out[f, x, rows, :] = part * radius
            rate[2, x, rows, :] = (values[3] * values[3] * inverse + pressure) * inv_radius
            rate[3, x, rows, :] = -(values[2] * values[3] * inverse) * inv_radius

    edge_lane = lax.broadcasted_iota(jnp.int32, (cycles, LANES), 1)
    pack_right = jnp.zeros((cycles, LANES), F32)
    pack_left = jnp.zeros((cycles, LANES), F32)
    for p, (f, x) in enumerate(planes):
        mine = (edge_lane >> 1) == p
        ends = g_turn[f, x, :, pl.ds(width - LANES, LANES)]
        pack_right = jnp.where(mine, pltpu.roll(ends, 2 * p + 2, 1), pack_right)
        heads = g_turn[f, x, :, pl.ds(0, LANES)]
        pack_left = jnp.where(mine, pltpu.roll(heads, 2 * p, 1) if p else heads, pack_left)
    edge_right[...] = pack_right
    edge_left[...] = pack_left
    for copy in edges:
        copy.start()

    loads[5].wait()
    inv_radius = 1.0 / radius_of(0, cycles)
    angular = inv_radius * (1.0 / (12.0 * (2.0 * math.pi / total)))
    radial = inv_radius * (1.0 / 12.0)
    tail_row = lax.broadcasted_iota(jnp.int32, (8, width), 0)
    beyond = jnp.where(
        tail_row < 2, (tail_row.astype(F32) + (cycles + 0.5)) * (1.0 / (cycles - 0.5)), 0.0
    )
    for f, x in planes:
        g = g_turn[f, x]
        turn_term = 8.0 * (pltpu.roll(g, width - 1, 1) - pltpu.roll(g, 1, 1)) - (
            pltpu.roll(g, width - 2, 1) - pltpu.roll(g, 2, 1)
        )
        g = g_out[f, x]
        tall = cycles + 8
        g = jnp.concatenate([g, beyond * g[cycles - 1 :]], axis=0)
        out_term = (
            8.0 * (pltpu.roll(g, tall - 1, 0) - pltpu.roll(g, 1, 0))
            - (pltpu.roll(g, tall - 2, 0) - pltpu.roll(g, 2, 0))
        )[:cycles]
        change = -(turn_term * angular + out_term * radial)
        if f in (2, 3):
            change = change + rate[f, x]
        rate[f, x] = begun[f, x] + STEP_DT * change

    for copy in edges:
        copy.wait_recv()
    from_left = edge_from_left[...] - edge_right[...]
    from_right = edge_from_right[...] - edge_left[...]
    even = (edge_lane & 1) == 0
    scale = -STEP_DT * angular[:, :LANES]
    from_left = scale * jnp.where(
        even, from_left - 8.0 * pltpu.roll(from_left, LANES - 1, 1), from_left
    )
    from_right = scale * jnp.where(
        even, -from_right, 8.0 * pltpu.roll(from_right, 1, 1) - from_right
    )
    head, end = pl.ds(0, LANES), pl.ds((cells - 1) // LANES * LANES, LANES)
    end_lane = (cells - 2) % LANES
    ghost_row = lax.broadcasted_iota(jnp.int32, (8, width), 0)
    ghost_scale = -STEP_DT * radial[:8]
    for p, (f, x) in enumerate(planes):
        value = pltpu.roll(from_left, (LANES - 2 * p) % LANES, 1) if p else from_left
        rate[f, x, :, head] = rate[f, x, :, head] + jnp.where(edge_lane < 2, value, 0.0)
        value = pltpu.roll(from_right, (end_lane - 2 * p) % LANES, 1)
        mine = (edge_lane >= end_lane) & (edge_lane < end_lane + 2)
        rate[f, x, :, end] = rate[f, x, :, end] + jnp.where(mine, value, 0.0)
        tile = -ghost[f, x] if f in (2, 3) else ghost[f, x]
        inside = jnp.where(
            ghost_row == 0,
            pltpu.roll(tile, 7, 0) - 8.0 * tile,
            jnp.where(ghost_row == 1, pltpu.roll(tile, 1, 0), 0.0),
        )
        rate[f, x, pl.ds(0, 8), :] = rate[f, x, pl.ds(0, 8), :] + ghost_scale * inside

    def raw_flux(ref, x, rows):
        values = [ref[f, x, rows, :] for f in range(fields)]
        inverse = 1.0 / values[0]
        return fluxes(values, 1, inverse, pressure_of(values, inverse))

    for (begin, size), pair in zip(pieces, crossings):
        for copy in pair:
            copy.wait_recv()
        if begin == 0:
            sides = (low_left, low_right)
            outside = split(jnp.concatenate([ref[f, x] for ref in sides for f, x in planes], axis=0))
            inside = split(jnp.concatenate([ref[f, axial] for ref in sides for f in range(fields)], axis=0))
            half = upper(2 * len(planes) * TILE)
            head = jnp.where(half, from_basis(0, *outside), from_basis(1, *outside))
            last = jnp.where(half, from_basis(5, *outside), from_basis(4, *outside))
            second, third = from_basis(2, *inside), from_basis(3, *inside)
            for side, ref in enumerate((fx_left, fx_right)):
                for p, (f, x) in enumerate(planes):
                    row = (side * len(planes) + p) * TILE
                    ref[f, x, pl.ds(0, TILE), :] = head[row : row + TILE]
                    ref[f, x, pl.ds(2 * TILE, TILE), :] = swapped(last[row : row + TILE])
                    row = (side * fields + f) * TILE
                    early, late = second[row : row + TILE], third[row : row + TILE]
                    early, late = (early, swapped(late)) if x == 0 else (swapped(early), late)
                    ref[f, x, pl.ds(TILE, TILE), :] = jnp.where(upper(TILE), early, late)
        for first in range(begin, begin + size, 8):
            rows = pl.ds(first, 8)
            if begin in (0, inner):
                own, left, right = [
                    [raw_flux(ref, x, rows) for x in range(axial)] for ref in (state, fx_left, fx_right)
                ]
            else:
                own, left, right = [
                    [[ref[f, x, rows, :] for f in range(fields)] for x in range(axial)]
                    for ref in (fx_own, fx_left, fx_right)
                ]
            for f in range(fields):
                terms = (
                    8.0 * (own[1][f] - left[1][f]) - (right[0][f] - left[0][f]),
                    8.0 * (right[0][f] - own[0][f]) - (right[1][f] - left[1][f]),
                )
                for x, term in enumerate(terms):
                    out[f, x, rows, :] = rate[f, x, rows, :] - (STEP_DT / 12.0) * term

    for pair in crossings:
        for copy in pair:
            copy.wait_send()
    for group in moments:
        for copy in group:
            copy.wait_send()
    for copy in edges:
        copy.wait_send()


def shards(state, start, modes):
    fields, axial, cells, cycles = state.shape
    inner = modes.shape[0]
    cfg = dict(plan(cells, lax.axis_size("azim")), cells=cells)
    width, depth = cfg["width"], cfg["depth"]
    turned, begun = [
        jnp.concatenate([values.transpose(0, 1, 3, 2)] * (width // cells), axis=3)
        for values in (state, start)
    ]
    full = (fields, axial, cycles, width)
    columns = 2 * fields * axial * inner // CHUNKS
    hbm = pl.BlockSpec(memory_space=pltpu.HBM)
    vmem = pl.BlockSpec(memory_space=pltpu.VMEM)
    peers, pieces = len(cfg["ranks"]), len(pieces_of(inner, cycles))
    tables = [jnp.asarray(cfg[name]) for name in ("table", "bases")]
    operands = (turned, begun, modes.reshape(1, inner), *tables)
    step = pl.pallas_call(
        functools.partial(kernel, cfg),
        out_shape=jax.ShapeDtypeStruct(full, F32),
        in_specs=[hbm] * 5,
        out_specs=vmem,
        scratch_shapes=[
            pltpu.VMEM(full, F32),
            pltpu.VMEM(full, F32),
            pltpu.VMEM((1, inner), jnp.int32),
            *[pltpu.VMEM(table.shape, BF16) for table in tables],
            pltpu.VMEM((inner, width), F32),
            pltpu.VMEM((inner, width), F32),
            pltpu.VMEM((CHUNKS, columns, width), BF16),
            pltpu.VMEM((CHUNKS, columns, width), BF16),
            pltpu.VMEM((CHUNKS, columns, width), F32),
            pltpu.VMEM((CHUNKS, depth, columns), F32),
            pltpu.VMEM((CHUNKS, depth, columns), F32),
        ]
        + [pltpu.VMEM(full, F32)] * 6
        + [pltpu.VMEM((fields, axial + 1, TILE, width), F32)] * 3
        + [pltpu.VMEM((cycles, LANES), F32)] * 4
        + [
            pltpu.VMEM((fields, axial, 8, width), F32),
            pltpu.SemaphoreType.DMA((6,)),
            pltpu.SemaphoreType.DMA((CHUNKS, peers)),
            pltpu.SemaphoreType.DMA((CHUNKS, peers)),
            pltpu.SemaphoreType.DMA((2, pieces)),
            pltpu.SemaphoreType.DMA((2, pieces)),
            pltpu.SemaphoreType.DMA((3,)),
            pltpu.SemaphoreType.DMA((3,)),
        ],
        compiler_params=pltpu.CompilerParams(
            collective_id=0, has_side_effects=True, vmem_limit_bytes=48 * 1024 * 1024
        ),
        name="jet_section",
    )(*[pltpu.with_memory_space_constraint(operand, pltpu.HBM) for operand in operands])
    return step[..., :cells].transpose(0, 1, 3, 2)


def solution(mesh):
    in_specs = (P(None, "axial", "azim", None), P(None, "axial", "azim", None), P())
    out_specs = P(None, "axial", "azim", None)
    return jax.shard_map(shards, mesh=mesh, in_specs=in_specs, out_specs=out_specs, check_vma=False)
```

```python
import functools
import math

import jax
import jax.numpy as jnp
import numpy as np
from jax import lax
from jax.experimental import pallas as pl
from jax.experimental.pallas import tpu as pltpu
from jax.sharding import PartitionSpec as P

STEP_DT = 0.05
LANES = 128
CHUNKS = 2
BLOCK = 16
MSTEP = 8
TILE = 8
GROUP = 4
PACKED = 6
CUT = 1e-6
LEVELS = 3
FLOOR = 1e-9
F32 = jnp.float32
BF16 = jnp.bfloat16
MESH = pl.DeviceIdType.MESH


def split_np(values):
    high = values.astype(np.float32).astype(jnp.bfloat16)
    low = (values - high.astype(np.float64)).astype(np.float32).astype(jnp.bfloat16)
    return high, low


def round_up(value, multiple):
    return -(-value // multiple) * multiple


@functools.lru_cache(None)
def plan(cells, count):
    total = cells * count
    width = round_up(cells, LANES)
    where = np.arange(cells)

    def coupling(offset):
        distance = offset * cells + where[:, None] - where[None, :]
        sine = np.sin(np.pi * distance / total)
        return np.where(distance == 0, 0.0, 1.0 / (total * np.where(distance == 0, 1.0, sine)))

    def wide(rows):
        return np.concatenate([rows] * (width // cells), axis=1)

    def padded(rows):
        return np.pad(rows, ((0, 0), (0, width - cells)))

    local = np.zeros((width, width))
    local[:cells] = wide(coupling(0).T)
    starts, ranks, outgoing, incoming = [], [], [], []
    for offset in range(1, count):
        left, values, right = np.linalg.svd(coupling(offset))
        rank = round_up(max(int(np.sum(values > FLOOR)), 1), 8)
        starts.append(sum(ranks))
        ranks.append(rank)
        outgoing.append(padded(right[:rank]))
        incoming.append(wide((left[:, :rank] * values[:rank]).T))
    depth = sum(ranks)
    out_high, out_low = split_np(np.concatenate(outgoing))
    in_high, in_low = split_np(np.concatenate(incoming))
    stacked = round_up(3 * depth, LANES)
    blank = np.zeros((stacked - 3 * depth, width), jnp.bfloat16)
    table = np.concatenate([*split_np(local), out_high, out_low, in_high, in_high, in_low, blank])

    def band(group):
        bound = min(2 * MSTEP * GROUP * (group + 1), total // 2)
        waves = np.arange(1, bound)
        phase = 2 * np.pi * ((where[:, None] * waves) % total) / total
        scale = np.sqrt(2.0 / total)
        columns = [np.full((cells, 1), 1.0 / np.sqrt(total)), scale * np.cos(phase), scale * np.sin(phase)]
        left, values, _ = np.linalg.svd(np.concatenate(columns, axis=1))
        return left, np.append(values, np.zeros(cells + 1 - len(values)))

    blocks = [None] * PACKED
    for low in range(PACKED // 2):
        high = PACKED - 1 - low
        (first, first_values), (second, second_values) = band(low), band(high)
        sizes = range(max(width - cells, 0), min(cells, width) + 1)
        size = min(sizes, key=lambda n: max(first_values[n], second_values[width - n]))
        assert max(first_values[size], second_values[width - size]) < CUT
        blocks[low] = np.zeros((width, width))
        blocks[low][:cells, :size] = first[:, :size]
        blocks[high] = np.zeros((width, width))
        blocks[high][:cells, size:] = second[:, : width - size]
    halves = [split_np(block) for block in blocks]
    bases = np.concatenate([pair[part] for part in range(2) for pair in halves])
    return dict(
        width=width, depth=depth, stacked=stacked, starts=starts, ranks=ranks, table=table, bases=bases
    )


def pieces_of(inner, cycles):
    span = inner // CHUNKS
    half = span // 2
    packed = PACKED * GROUP
    pieces = [(inner, cycles - inner), (packed, span - packed), (0, packed)]
    pieces += [(c * span, span) for c in range(1, CHUNKS - 1)]
    return pieces + [(inner - span, half), (inner - half, half // 2), (inner - half // 2, half // 2)]


def split(values):
    high = values.astype(BF16)
    return high, (values - high.astype(F32)).astype(BF16)


def mm(a, b):
    return jnp.dot(a, b, preferred_element_type=F32)


def mm_lanes(a, b):
    return lax.dot_general(a, b, (((1,), (1,)), ((), ())), preferred_element_type=F32)


def pressure_of(values, inverse):
    kinetic = (values[1] * values[1] + values[2] * values[2] + values[3] * values[3]) * inverse
    return 0.4 * (values[4] - 0.5 * kinetic)


def fluxes(values, direction, inverse, pressure):
    velocity = values[direction] * inverse
    parts = [
        values[direction],
        values[1] * velocity,
        values[2] * velocity,
        values[3] * velocity,
        (values[4] + pressure) * velocity,
    ]
    parts[direction] = parts[direction] + pressure
    return parts


def turns(steps, total):
    quarter = total // 2
    quadrant = (steps + quarter // 2) // quarter
    angle = (steps - quadrant * quarter).astype(F32) * (math.pi / total)
    square = angle * angle
    sine = angle + angle * square * (
        -1.0 / 6 + square * (1.0 / 120 + square * (-1.0 / 5040 + square * (1.0 / 362880)))
    )
    cosine = 1.0 + square * (
        -0.5
        + square * (1.0 / 24 + square * (-1.0 / 720 + square * (1.0 / 40320 - square * (1.0 / 3628800))))
    )
    odd = (quadrant & 1) == 1
    first, second = jnp.where(odd, cosine, sine), jnp.where(odd, sine, cosine)
    return (
        jnp.where((quadrant & 2) == 2, -first, first),
        jnp.where(((quadrant + 1) & 2) == 2, -second, second),
    )


def kernel(
    cfg,
    state_hbm, start_hbm, modes_hbm, table_hbm, bases_hbm, out,
    state, begun, modes, table, bases, cosines, sines,
    x_high, x_low, near, mom_own, mom_in,
    fx_own, fx_left, fx_right, g_turn, g_out, rate, low_own, low_left, low_right,
    edge_right, edge_left, edge_from_left, edge_from_right, ghost,
    load_sem, mom_send, mom_recv, fx_send, fx_recv, edge_send, edge_recv, answered,
):
    fields, axial, cycles, width = state.shape
    cells, inner = cfg["cells"], modes.shape[1]
    depth, stacked = cfg["depth"], cfg["stacked"]
    starts, ranks = cfg["starts"], cfg["ranks"]
    count, ring = lax.axis_size("azim"), lax.axis_size("axial")
    d, a = lax.axis_index("azim"), lax.axis_index("axial")
    total = cells * count
    planes = [(f, x) for f in range(fields) for x in range(axial)]
    span = inner // CHUNKS

    def z_at(offset):
        return {"azim": lax.rem(d + offset, count)}

    x_right = {"axial": lax.rem(a + 1, ring)}
    x_left = {"axial": lax.rem(a + ring - 1, ring)}

    def remote(src, dst, send, recv, device):
        return pltpu.make_async_remote_copy(
            src_ref=src, dst_ref=dst, send_sem=send, recv_sem=recv,
            device_id=device, device_id_type=MESH,
        )

    outer_rows, inner_rows = pl.ds(inner, cycles - inner), pl.ds(0, inner)
    barrier = pltpu.get_barrier_semaphore()
    level = jnp.minimum(d, LEVELS - 1)
    level_mates = jnp.where(level == LEVELS - 1, count - LEVELS, 0)
    azim_peers = [z_at(offset) for offset in range(1, count)]
    peer_levels = [jnp.minimum(device["azim"], LEVELS - 1) for device in azim_peers]
    is_earlier = [peer_level < level for peer_level in peer_levels]
    is_later = [peer_level > level for peer_level in peer_levels]

    def greet(device, semaphore=barrier):
        pl.semaphore_signal(semaphore, inc=1, device_id=device, device_id_type=MESH)

    for device in (x_right, x_left):
        greet(device)
    for device, earlier in zip(azim_peers, is_earlier):
        pl.when(jnp.logical_not(earlier))(functools.partial(greet, device))
    loads = [
        pltpu.make_async_copy(modes_hbm, modes, load_sem.at[0]),
        pltpu.make_async_copy(
            state_hbm.at[:, :, inner_rows], state.at[:, :, inner_rows], load_sem.at[1]
        ),
        pltpu.make_async_copy(
            state_hbm.at[:, :, outer_rows], state.at[:, :, outer_rows], load_sem.at[2]
        ),
        pltpu.make_async_copy(table_hbm, table, load_sem.at[3]),
        pltpu.make_async_copy(bases_hbm, bases, load_sem.at[4]),
        pltpu.make_async_copy(start_hbm, begun, load_sem.at[5]),
    ]
    for copy in loads:
        copy.start()

    moments = [
        [
            remote(
                mom_own.at[c, pl.ds(starts[k], ranks[k])], mom_in.at[c, pl.ds(starts[k], ranks[k])],
                mom_send.at[c, k], mom_recv.at[c, k], z_at(k + 1),
            )
            for k in range(len(ranks))
        ]
        for c in range(CHUNKS)
    ]
    pieces = pieces_of(inner, cycles)
    crossings = []
    for k, (first, size) in enumerate(pieces):
        rows = pl.ds(first, size)
        source = (state_hbm if first == inner else fx_own).at[:, :, rows]
        targets = fx_left.at[:, :, rows], fx_right.at[:, :, rows]
        if first == 0:
            source, targets = low_own, (low_left, low_right)
        crossings.append(
            [
                remote(source, target, fx_send.at[side, k], fx_recv.at[side, k], device)
                for side, (target, device) in enumerate(zip(targets, (x_right, x_left)))
            ]
        )
    edges = [
        remote(edge_right, edge_from_left, edge_send.at[0], edge_recv.at[0], z_at(1)),
        remote(edge_left, edge_from_right, edge_send.at[1], edge_recv.at[1], z_at(count - 1)),
        remote(
            g_out.at[:, :, pl.ds(0, 8)], ghost, edge_send.at[2], edge_recv.at[2], z_at(count // 2)
        ),
    ]

    pl.semaphore_wait(barrier, 2 + level + level_mates)
    for copy in crossings[0]:
        copy.start()
    for device, earlier in zip(azim_peers, is_earlier):
        pl.when(earlier)(functools.partial(greet, device, answered))

    loads[0].wait()
    kept = jnp.broadcast_to(modes[...], (inner, inner)).astype(F32)
    same = lax.broadcasted_iota(jnp.int32, (inner, inner), 0) == lax.broadcasted_iota(
        jnp.int32, (inner, inner), 1
    )
    odd_count = 2.0 * jnp.sum(jnp.where(same, kept, 0.0), axis=1, keepdims=True) - 1.0
    share = odd_count * (1.0 / total)
    lane = lax.broadcasted_iota(jnp.int32, (inner, width), 1)
    place = (lax.rem(lane, cells) + d * cells).astype(F32)
    steps = (odd_count * place).astype(jnp.int32) & (2 * total - 1)
    sine, cosine = turns(steps, total)
    sines[...] = sine
    cosines[...] = cosine

    def axial_flux(values, x, rows):
        inverse = 1.0 / values[0]
        for f, part in enumerate(fluxes(values, 1, inverse, pressure_of(values, inverse))):
            fx_own[f, x, rows, :] = part

    loads[1].wait()
    loads[3].wait()
    out_table = table[pl.ds(2 * width, 2 * depth), :]
    for c in range(CHUNKS):
        rows = pl.ds(c * span, span)
        for p, (f, x) in enumerate(planes):
            value = state[f, x, rows, :]
            for part, wave in enumerate((cosines, sines)):
                high, low = split(value * wave[rows, :])
                slot = pl.ds((2 * p + part) * span, span)
                x_high[c, slot, :] = high
                x_low[c, slot, :] = low
        sums = mm_lanes(out_table, x_high[c]) + mm_lanes(out_table, x_low[c])
        sums = sums[:depth] + sums[depth:]
        for k in range(len(ranks)):
            wrapped = (1 - 2 * ((d + k + 1) // count)).astype(F32)
            mom_own[c, pl.ds(starts[k], ranks[k]), :] = (
                sums[starts[k] : starts[k] + ranks[k]] * wrapped
            )
        if c == 0:
            for copy, later in zip(moments[c], is_later):
                pl.when(jnp.logical_not(later))(copy.start)

            @pl.when(level < LEVELS - 1)
            def _():
                pl.semaphore_wait(answered, count - 1 - level)

            for copy, later in zip(moments[c], is_later):
                pl.when(later)(copy.start)
        else:
            for copy in moments[c]:
                copy.start()

    local_high, local_low = table[pl.ds(0, width), :], table[pl.ds(width, width), :]
    for c in range(CHUNKS):
        near[c] = mm(x_high[c], local_high) + mm(x_low[c], local_high) + mm(x_high[c], local_low)

    ends = [
        (first + size, pair) for (first, size), pair in zip(pieces, crossings) if first not in (0, inner)
    ]

    def into_basis(group, high, low):
        rows, at = high.shape[0], lambda part: pl.ds((PACKED * part + group) * width, width)
        both = mm(jnp.concatenate([high, low], axis=0), bases[at(0), :])
        return both[:rows] + both[rows:] + mm(high, bases[at(1), :])

    def from_basis(group, high, low):
        rows, at = high.shape[0], lambda part: pl.ds((PACKED * part + group) * width, width)
        both = mm_lanes(jnp.concatenate([high, low], axis=0), bases[at(0), :])
        return both[:rows] + both[rows:] + mm_lanes(high, bases[at(1), :])

    def upper(rows):
        return (lax.broadcasted_iota(jnp.int32, (rows, width), 0) & GROUP) == 0

    def swapped(tile):
        return pltpu.roll(tile, GROUP, 0)

    in_table = table[pl.ds(2 * width + 2 * depth, stacked), :]
    for c in range(CHUNKS):
        for copy in moments[c]:
            copy.wait_recv()
        high = mom_in[c].astype(BF16).astype(F32)
        low = (mom_in[c] - high).astype(BF16).astype(F32)
        parts = [high, low, high]
        if stacked > 3 * depth:
            parts.append(jnp.zeros((stacked - 3 * depth, high.shape[1]), F32))
        stack = jnp.concatenate(parts, axis=0).T.astype(BF16)
        near[c] = near[c] + mm(stack, in_table)
        for first in reversed(range(0, span, BLOCK)) if c == 0 else range(0, span, BLOCK):
            rows = pl.ds(c * span + first, BLOCK)
            wave_sine, wave_cosine = sines[rows, :], cosines[rows, :]
            weight = share[c * span + first : c * span + first + BLOCK]
            for x in range(axial):
                values = []
                for f in range(fields):
                    slot = 2 * (f * axial + x) * span + first
                    kept_value = (
                        wave_sine * near[c, pl.ds(slot, BLOCK), :]
                        - wave_cosine * near[c, pl.ds(slot + span, BLOCK), :]
                        + weight * state[f, x, rows, :]
                    )
                    state[f, x, rows, :] = kept_value
                    values.append(kept_value)
                axial_flux(values, x, rows)
            for end, pair in ends:
                if 0 < end - (c * span + first) <= BLOCK:
                    for copy in pair:
                        copy.start()
        if c == 0:
            loads[4].wait()
            tiles = [
                [state[f, x, pl.ds(TILE * t, TILE), :] for f, x in planes] for t in range(PACKED * GROUP // TILE)
            ]
            first, middle, last = [split(jnp.concatenate(tile, axis=0)) for tile in tiles]
            middle_swapped, last_swapped = [
                split(jnp.concatenate([swapped(part) for part in tile], axis=0)) for tile in tiles[1:]
            ]
            outside = jnp.where(
                upper(len(planes) * TILE),
                into_basis(0, *first) + into_basis(5, *last_swapped),
                into_basis(1, *first) + into_basis(4, *last_swapped),
            )
            inside = into_basis(2, *middle) + into_basis(3, *middle_swapped)
            for p, (f, x) in enumerate(planes):
                low_own[f, x] = outside[p * TILE : (p + 1) * TILE]
            for f in range(fields):
                even, odd = [inside[p * TILE : (p + 1) * TILE] for p in (2 * f, 2 * f + 1)]
                low_own[f, axial] = jnp.where(upper(TILE), even, swapped(odd))
            for copy in crossings[2]:
                copy.start()

    radius_of = lambda first, size: (
        lax.broadcasted_iota(jnp.int32, (size, width), 0) + first
    ).astype(F32) + 0.5
    loads[2].wait()
    for first in range(0, cycles, BLOCK):
        rows = pl.ds(first, BLOCK)
        radius = radius_of(first, BLOCK)
        inv_radius = 1.0 / radius
        for x in range(axial):
            values = [state[f, x, rows, :] for f in range(fields)]
            inverse = 1.0 / values[0]
            pressure = pressure_of(values, inverse)
            for f, part in enumerate(fluxes(values, 3, inverse, pressure)):
                g_turn[f, x, rows, :] = part
            for f, part in enumerate(fluxes(values, 2, inverse, pressure)):
                g_out[f, x, rows, :] = part * radius
            rate[2, x, rows, :] = (values[3] * values[3] * inverse + pressure) * inv_radius
            rate[3, x, rows, :] = -(values[2] * values[3] * inverse) * inv_radius

    edge_lane = lax.broadcasted_iota(jnp.int32, (cycles, LANES), 1)
    pack_right = jnp.zeros((cycles, LANES), F32)
    pack_left = jnp.zeros((cycles, LANES), F32)
    for p, (f, x) in enumerate(planes):
        mine = (edge_lane >> 1) == p
        ends = g_turn[f, x, :, pl.ds(width - LANES, LANES)]
        pack_right = jnp.where(mine, pltpu.roll(ends, 2 * p + 2, 1), pack_right)
        heads = g_turn[f, x, :, pl.ds(0, LANES)]
        pack_left = jnp.where(mine, pltpu.roll(heads, 2 * p, 1) if p else heads, pack_left)
    edge_right[...] = pack_right
    edge_left[...] = pack_left
    for copy in edges:
        copy.start()

    loads[5].wait()
    inv_radius = 1.0 / radius_of(0, cycles)
    angular = inv_radius * (1.0 / (12.0 * (2.0 * math.pi / total)))
    radial = inv_radius * (1.0 / 12.0)
    tail_row = lax.broadcasted_iota(jnp.int32, (8, width), 0)
    beyond = jnp.where(
        tail_row < 2, (tail_row.astype(F32) + (cycles + 0.5)) * (1.0 / (cycles - 0.5)), 0.0
    )
    for f, x in planes:
        g = g_turn[f, x]
        turn_term = 8.0 * (pltpu.roll(g, width - 1, 1) - pltpu.roll(g, 1, 1)) - (
            pltpu.roll(g, width - 2, 1) - pltpu.roll(g, 2, 1)
        )
        g = g_out[f, x]
        tall = cycles + 8
        g = jnp.concatenate([g, beyond * g[cycles - 1 :]], axis=0)
        out_term = (
            8.0 * (pltpu.roll(g, tall - 1, 0) - pltpu.roll(g, 1, 0))
            - (pltpu.roll(g, tall - 2, 0) - pltpu.roll(g, 2, 0))
        )[:cycles]
        change = -(turn_term * angular + out_term * radial)
        if f in (2, 3):
            change = change + rate[f, x]
        rate[f, x] = begun[f, x] + STEP_DT * change

    for copy in edges:
        copy.wait_recv()
    from_left = edge_from_left[...] - edge_right[...]
    from_right = edge_from_right[...] - edge_left[...]
    even = (edge_lane & 1) == 0
    scale = -STEP_DT * angular[:, :LANES]
    from_left = scale * jnp.where(
        even, from_left - 8.0 * pltpu.roll(from_left, LANES - 1, 1), from_left
    )
    from_right = scale * jnp.where(
        even, -from_right, 8.0 * pltpu.roll(from_right, 1, 1) - from_right
    )
    head, end = pl.ds(0, LANES), pl.ds((cells - 1) // LANES * LANES, LANES)
    end_lane = (cells - 2) % LANES
    ghost_row = lax.broadcasted_iota(jnp.int32, (8, width), 0)
    ghost_scale = -STEP_DT * radial[:8]
    for p, (f, x) in enumerate(planes):
        value = pltpu.roll(from_left, (LANES - 2 * p) % LANES, 1) if p else from_left
        rate[f, x, :, head] = rate[f, x, :, head] + jnp.where(edge_lane < 2, value, 0.0)
        value = pltpu.roll(from_right, (end_lane - 2 * p) % LANES, 1)
        mine = (edge_lane >= end_lane) & (edge_lane < end_lane + 2)
        rate[f, x, :, end] = rate[f, x, :, end] + jnp.where(mine, value, 0.0)
        tile = -ghost[f, x] if f in (2, 3) else ghost[f, x]
        inside = jnp.where(
            ghost_row == 0,
            pltpu.roll(tile, 7, 0) - 8.0 * tile,
            jnp.where(ghost_row == 1, pltpu.roll(tile, 1, 0), 0.0),
        )
        rate[f, x, pl.ds(0, 8), :] = rate[f, x, pl.ds(0, 8), :] + ghost_scale * inside

    def raw_flux(ref, x, rows):
        values = [ref[f, x, rows, :] for f in range(fields)]
        inverse = 1.0 / values[0]
        return fluxes(values, 1, inverse, pressure_of(values, inverse))

    for (begin, size), pair in zip(pieces, crossings):
        for copy in pair:
            copy.wait_recv()
        if begin == 0:
            sides = (low_left, low_right)
            outside = split(jnp.concatenate([ref[f, x] for ref in sides for f, x in planes], axis=0))
            inside = split(jnp.concatenate([ref[f, axial] for ref in sides for f in range(fields)], axis=0))
            half = upper(2 * len(planes) * TILE)
            head = jnp.where(half, from_basis(0, *outside), from_basis(1, *outside))
            last = jnp.where(half, from_basis(5, *outside), from_basis(4, *outside))
            second, third = from_basis(2, *inside), from_basis(3, *inside)
            for side, ref in enumerate((fx_left, fx_right)):
                for p, (f, x) in enumerate(planes):
                    row = (side * len(planes) + p) * TILE
                    ref[f, x, pl.ds(0, TILE), :] = head[row : row + TILE]
                    ref[f, x, pl.ds(2 * TILE, TILE), :] = swapped(last[row : row + TILE])
                    row = (side * fields + f) * TILE
                    early, late = second[row : row + TILE], third[row : row + TILE]
                    early, late = (early, swapped(late)) if x == 0 else (swapped(early), late)
                    ref[f, x, pl.ds(TILE, TILE), :] = jnp.where(upper(TILE), early, late)
        for first in range(begin, begin + size, 8):
            rows = pl.ds(first, 8)
            if begin in (0, inner):
                own, left, right = [
                    [raw_flux(ref, x, rows) for x in range(axial)] for ref in (state, fx_left, fx_right)
                ]
            else:
                own, left, right = [
                    [[ref[f, x, rows, :] for f in range(fields)] for x in range(axial)]
                    for ref in (fx_own, fx_left, fx_right)
                ]
            for f in range(fields):
                terms = (
                    8.0 * (own[1][f] - left[1][f]) - (right[0][f] - left[0][f]),
                    8.0 * (right[0][f] - own[0][f]) - (right[1][f] - left[1][f]),
                )
                for x, term in enumerate(terms):
                    out[f, x, rows, :] = rate[f, x, rows, :] - (STEP_DT / 12.0) * term

    for pair in crossings:
        for copy in pair:
            copy.wait_send()
    for group in moments:
        for copy in group:
            copy.wait_send()
    for copy in edges:
        copy.wait_send()


def shards(state, start, modes):
    fields, axial, cells, cycles = state.shape
    inner = modes.shape[0]
    cfg = dict(plan(cells, lax.axis_size("azim")), cells=cells)
    width, depth = cfg["width"], cfg["depth"]
    turned, begun = [
        jnp.concatenate([values.transpose(0, 1, 3, 2)] * (width // cells), axis=3)
        for values in (state, start)
    ]
    full = (fields, axial, cycles, width)
    columns = 2 * fields * axial * inner // CHUNKS
    hbm = pl.BlockSpec(memory_space=pltpu.HBM)
    vmem = pl.BlockSpec(memory_space=pltpu.VMEM)
    peers, pieces = len(cfg["ranks"]), len(pieces_of(inner, cycles))
    tables = [jnp.asarray(cfg[name]) for name in ("table", "bases")]
    operands = (turned, begun, modes.reshape(1, inner), *tables)
    step = pl.pallas_call(
        functools.partial(kernel, cfg),
        out_shape=jax.ShapeDtypeStruct(full, F32),
        in_specs=[hbm] * 5,
        out_specs=vmem,
        scratch_shapes=[
            pltpu.VMEM(full, F32),
            pltpu.VMEM(full, F32),
            pltpu.VMEM((1, inner), jnp.int32),
            *[pltpu.VMEM(table.shape, BF16) for table in tables],
            pltpu.VMEM((inner, width), F32),
            pltpu.VMEM((inner, width), F32),
            pltpu.VMEM((CHUNKS, columns, width), BF16),
            pltpu.VMEM((CHUNKS, columns, width), BF16),
            pltpu.VMEM((CHUNKS, columns, width), F32),
            pltpu.VMEM((CHUNKS, depth, columns), F32),
            pltpu.VMEM((CHUNKS, depth, columns), F32),
        ]
        + [pltpu.VMEM(full, F32)] * 6
        + [pltpu.VMEM((fields, axial + 1, TILE, width), F32)] * 3
        + [pltpu.VMEM((cycles, LANES), F32)] * 4
        + [
            pltpu.VMEM((fields, axial, 8, width), F32),
            pltpu.SemaphoreType.DMA((6,)),
            pltpu.SemaphoreType.DMA((CHUNKS, peers)),
            pltpu.SemaphoreType.DMA((CHUNKS, peers)),
            pltpu.SemaphoreType.DMA((2, pieces)),
            pltpu.SemaphoreType.DMA((2, pieces)),
            pltpu.SemaphoreType.DMA((3,)),
            pltpu.SemaphoreType.DMA((3,)),
            pltpu.SemaphoreType.REGULAR,
        ],
        compiler_params=pltpu.CompilerParams(
            collective_id=0, has_side_effects=True, vmem_limit_bytes=48 * 1024 * 1024
        ),
        name="jet_section",
    )(*[pltpu.with_memory_space_constraint(operand, pltpu.HBM) for operand in operands])
    return step[..., :cells].transpose(0, 1, 3, 2)


def solution(mesh):
    in_specs = (P(None, "axial", "azim", None), P(None, "axial", "azim", None), P())
    out_specs = P(None, "axial", "azim", None)
    return jax.shard_map(shards, mesh=mesh, in_specs=in_specs, out_specs=out_specs, check_vma=False)
```

```python
import functools
import math

import jax
import jax.numpy as jnp
import numpy as np
from jax import lax
from jax.experimental import pallas as pl
from jax.experimental.pallas import tpu as pltpu
from jax.sharding import PartitionSpec as P

STEP_DT = 0.05
LANES = 128
CHUNKS = 2
BLOCK = 16
MSTEP = 8
TILE = 8
GROUP = 4
PACKED = 6
CUT = 1e-6
LEVELS = 3
FLOOR = 1e-9
F32 = jnp.float32
BF16 = jnp.bfloat16
MESH = pl.DeviceIdType.MESH


def split_np(values):
    high = values.astype(np.float32).astype(jnp.bfloat16)
    low = (values - high.astype(np.float64)).astype(np.float32).astype(jnp.bfloat16)
    return high, low


def round_up(value, multiple):
    return -(-value // multiple) * multiple


@functools.lru_cache(None)
def plan(cells, count):
    total = cells * count
    width = round_up(cells, LANES)
    where = np.arange(cells)

    def coupling(offset):
        distance = offset * cells + where[:, None] - where[None, :]
        sine = np.sin(np.pi * distance / total)
        return np.where(distance == 0, 0.0, 1.0 / (total * np.where(distance == 0, 1.0, sine)))

    def wide(rows):
        return np.concatenate([rows] * (width // cells), axis=1)

    def padded(rows):
        return np.pad(rows, ((0, 0), (0, width - cells)))

    local = np.zeros((width, width))
    local[:cells] = wide(coupling(0).T)
    starts, ranks, outgoing, incoming = [], [], [], []
    for offset in range(1, count):
        left, values, right = np.linalg.svd(coupling(offset))
        rank = round_up(max(int(np.sum(values > FLOOR)), 1), 8)
        starts.append(sum(ranks))
        ranks.append(rank)
        outgoing.append(padded(right[:rank]))
        incoming.append(wide((left[:, :rank] * values[:rank]).T))
    depth = sum(ranks)
    out_high, out_low = split_np(np.concatenate(outgoing))
    in_high, in_low = split_np(np.concatenate(incoming))
    stacked = round_up(3 * depth, LANES)
    blank = np.zeros((stacked - 3 * depth, width), jnp.bfloat16)
    table = np.concatenate([*split_np(local), out_high, out_low, in_high, in_high, in_low, blank])

    def band(group):
        bound = min(2 * MSTEP * GROUP * (group + 1), total // 2)
        waves = np.arange(1, bound)
        phase = 2 * np.pi * ((where[:, None] * waves) % total) / total
        scale = np.sqrt(2.0 / total)
        columns = [np.full((cells, 1), 1.0 / np.sqrt(total)), scale * np.cos(phase), scale * np.sin(phase)]
        left, values, _ = np.linalg.svd(np.concatenate(columns, axis=1))
        return left, np.append(values, np.zeros(cells + 1 - len(values)))

    blocks = [None] * PACKED
    for low in range(PACKED // 2):
        high = PACKED - 1 - low
        (first, first_values), (second, second_values) = band(low), band(high)
        sizes = range(max(width - cells, 0), min(cells, width) + 1)
        size = min(sizes, key=lambda n: max(first_values[n], second_values[width - n]))
        assert max(first_values[size], second_values[width - size]) < CUT
        blocks[low] = np.zeros((width, width))
        blocks[low][:cells, :size] = first[:, :size]
        blocks[high] = np.zeros((width, width))
        blocks[high][:cells, size:] = second[:, : width - size]
    halves = [split_np(block) for block in blocks]
    bases = np.concatenate([pair[part] for part in range(2) for pair in halves])
    return dict(
        width=width, depth=depth, stacked=stacked, starts=starts, ranks=ranks, table=table, bases=bases
    )


def pieces_of(inner, cycles):
    span = inner // CHUNKS
    packed = PACKED * GROUP
    pieces = [(inner, cycles - inner), (packed, span - packed), (0, packed)]
    pieces += [(c * span, span) for c in range(1, CHUNKS - 1)]
    return pieces + [(inner - span, span - TILE), (inner - TILE, TILE)]


def split(values):
    high = values.astype(BF16)
    return high, (values - high.astype(F32)).astype(BF16)


def mm(a, b):
    return jnp.dot(a, b, preferred_element_type=F32)


def mm_lanes(a, b):
    return lax.dot_general(a, b, (((1,), (1,)), ((), ())), preferred_element_type=F32)


def pressure_of(values, inverse):
    kinetic = (values[1] * values[1] + values[2] * values[2] + values[3] * values[3]) * inverse
    return 0.4 * (values[4] - 0.5 * kinetic)


def fluxes(values, direction, inverse, pressure):
    velocity = values[direction] * inverse
    parts = [
        values[direction],
        values[1] * velocity,
        values[2] * velocity,
        values[3] * velocity,
        (values[4] + pressure) * velocity,
    ]
    parts[direction] = parts[direction] + pressure
    return parts


def turns(steps, total):
    quarter = total // 2
    quadrant = (steps + quarter // 2) // quarter
    angle = (steps - quadrant * quarter).astype(F32) * (math.pi / total)
    square = angle * angle
    sine = angle + angle * square * (
        -1.0 / 6 + square * (1.0 / 120 + square * (-1.0 / 5040 + square * (1.0 / 362880)))
    )
    cosine = 1.0 + square * (
        -0.5
        + square * (1.0 / 24 + square * (-1.0 / 720 + square * (1.0 / 40320 - square * (1.0 / 3628800))))
    )
    odd = (quadrant & 1) == 1
    first, second = jnp.where(odd, cosine, sine), jnp.where(odd, sine, cosine)
    return (
        jnp.where((quadrant & 2) == 2, -first, first),
        jnp.where(((quadrant + 1) & 2) == 2, -second, second),
    )


def kernel(
    cfg,
    state_hbm, start_hbm, modes_hbm, table_hbm, bases_hbm, out,
    state, begun, modes, table, bases, cosines, sines,
    x_high, x_low, near, mom_own, mom_in,
    fx_own, fx_left, fx_right, g_turn, g_out, rate, low_own, low_left, low_right,
    edge_right, edge_left, edge_from_left, edge_from_right, ghost,
    load_sem, mom_send, mom_recv, fx_send, fx_recv, edge_send, edge_recv, answered,
):
    fields, axial, cycles, width = state.shape
    cells, inner = cfg["cells"], modes.shape[1]
    depth, stacked = cfg["depth"], cfg["stacked"]
    starts, ranks = cfg["starts"], cfg["ranks"]
    count, ring = lax.axis_size("azim"), lax.axis_size("axial")
    d, a = lax.axis_index("azim"), lax.axis_index("axial")
    total = cells * count
    planes = [(f, x) for f in range(fields) for x in range(axial)]
    span = inner // CHUNKS

    def z_at(offset):
        return {"azim": lax.rem(d + offset, count)}

    x_right = {"axial": lax.rem(a + 1, ring)}
    x_left = {"axial": lax.rem(a + ring - 1, ring)}

    def remote(src, dst, send, recv, device):
        return pltpu.make_async_remote_copy(
            src_ref=src, dst_ref=dst, send_sem=send, recv_sem=recv,
            device_id=device, device_id_type=MESH,
        )

    outer_rows, inner_rows = pl.ds(inner, cycles - inner), pl.ds(0, inner)
    barrier = pltpu.get_barrier_semaphore()
    level = jnp.minimum(d, LEVELS - 1)
    level_mates = jnp.where(level == LEVELS - 1, count - LEVELS, 0)
    azim_peers = [z_at(offset) for offset in range(1, count)]
    peer_levels = [jnp.minimum(device["azim"], LEVELS - 1) for device in azim_peers]
    is_earlier = [peer_level < level for peer_level in peer_levels]
    is_later = [peer_level > level for peer_level in peer_levels]

    def greet(device, semaphore=barrier):
        pl.semaphore_signal(semaphore, inc=1, device_id=device, device_id_type=MESH)

    for device in (x_right, x_left):
        greet(device)
    for device, earlier in zip(azim_peers, is_earlier):
        pl.when(jnp.logical_not(earlier))(functools.partial(greet, device))
    loads = [
        pltpu.make_async_copy(modes_hbm, modes, load_sem.at[0]),
        pltpu.make_async_copy(
            state_hbm.at[:, :, inner_rows], state.at[:, :, inner_rows], load_sem.at[1]
        ),
        pltpu.make_async_copy(
            state_hbm.at[:, :, outer_rows], state.at[:, :, outer_rows], load_sem.at[2]
        ),
        pltpu.make_async_copy(table_hbm, table, load_sem.at[3]),
        pltpu.make_async_copy(bases_hbm, bases, load_sem.at[4]),
        pltpu.make_async_copy(start_hbm, begun, load_sem.at[5]),
    ]
    for copy in loads:
        copy.start()

    moments = [
        [
            remote(
                mom_own.at[c, pl.ds(starts[k], ranks[k])], mom_in.at[c, pl.ds(starts[k], ranks[k])],
                mom_send.at[c, k], mom_recv.at[c, k], z_at(k + 1),
            )
            for k in range(len(ranks))
        ]
        for c in range(CHUNKS)
    ]
    pieces = pieces_of(inner, cycles)
    crossings = []
    for k, (first, size) in enumerate(pieces):
        rows = pl.ds(first, size)
        source = (state_hbm if first == inner else fx_own).at[:, :, rows]
        targets = fx_left.at[:, :, rows], fx_right.at[:, :, rows]
        if first == 0:
            source, targets = low_own, (low_left, low_right)
        crossings.append(
            [
                remote(source, target, fx_send.at[side, k], fx_recv.at[side, k], device)
                for side, (target, device) in enumerate(zip(targets, (x_right, x_left)))
            ]
        )
    edges = [
        remote(edge_right, edge_from_left, edge_send.at[0], edge_recv.at[0], z_at(1)),
        remote(edge_left, edge_from_right, edge_send.at[1], edge_recv.at[1], z_at(count - 1)),
        remote(
            g_out.at[:, :, pl.ds(0, 8)], ghost, edge_send.at[2], edge_recv.at[2], z_at(count // 2)
        ),
    ]

    pl.semaphore_wait(barrier, 2 + level + level_mates)
    for copy in crossings[0]:
        copy.start()
    for device, earlier in zip(azim_peers, is_earlier):
        pl.when(earlier)(functools.partial(greet, device, answered))

    loads[0].wait()
    kept = jnp.broadcast_to(modes[...], (inner, inner)).astype(F32)
    same = lax.broadcasted_iota(jnp.int32, (inner, inner), 0) == lax.broadcasted_iota(
        jnp.int32, (inner, inner), 1
    )
    odd_count = 2.0 * jnp.sum(jnp.where(same, kept, 0.0), axis=1, keepdims=True) - 1.0
    share = odd_count * (1.0 / total)
    lane = lax.broadcasted_iota(jnp.int32, (inner, width), 1)
    place = (lax.rem(lane, cells) + d * cells).astype(F32)
    steps = (odd_count * place).astype(jnp.int32) & (2 * total - 1)
    sine, cosine = turns(steps, total)
    sines[...] = sine
    cosines[...] = cosine

    def axial_flux(values, x, rows):
        inverse = 1.0 / values[0]
        for f, part in enumerate(fluxes(values, 1, inverse, pressure_of(values, inverse))):
            fx_own[f, x, rows, :] = part

    loads[1].wait()
    loads[3].wait()
    out_table = table[pl.ds(2 * width, 2 * depth), :]
    for c in range(CHUNKS):
        rows = pl.ds(c * span, span)
        for p, (f, x) in enumerate(planes):
            value = state[f, x, rows, :]
            for part, wave in enumerate((cosines, sines)):
                high, low = split(value * wave[rows, :])
                slot = pl.ds((2 * p + part) * span, span)
                x_high[c, slot, :] = high
                x_low[c, slot, :] = low
        sums = mm_lanes(out_table, x_high[c]) + mm_lanes(out_table, x_low[c])
        sums = sums[:depth] + sums[depth:]
        for k in range(len(ranks)):
            wrapped = (1 - 2 * ((d + k + 1) // count)).astype(F32)
            mom_own[c, pl.ds(starts[k], ranks[k]), :] = (
                sums[starts[k] : starts[k] + ranks[k]] * wrapped
            )
        if c == 0:
            for copy, later in zip(moments[c], is_later):
                pl.when(jnp.logical_not(later))(copy.start)

            @pl.when(level < LEVELS - 1)
            def _():
                pl.semaphore_wait(answered, count - 1 - level)

            for copy, later in zip(moments[c], is_later):
                pl.when(later)(copy.start)
        else:
            for copy in moments[c]:
                copy.start()

    local_high, local_low = table[pl.ds(0, width), :], table[pl.ds(width, width), :]
    for c in range(CHUNKS):
        near[c] = mm(x_high[c], local_high) + mm(x_low[c], local_high) + mm(x_high[c], local_low)

    ends = [
        (first + size, pair) for (first, size), pair in zip(pieces, crossings) if first not in (0, inner)
    ]

    def into_basis(group, high, low):
        rows, at = high.shape[0], lambda part: pl.ds((PACKED * part + group) * width, width)
        both = mm(jnp.concatenate([high, low], axis=0), bases[at(0), :])
        return both[:rows] + both[rows:] + mm(high, bases[at(1), :])

    def from_basis(group, high, low):
        rows, at = high.shape[0], lambda part: pl.ds((PACKED * part + group) * width, width)
        both = mm_lanes(jnp.concatenate([high, low], axis=0), bases[at(0), :])
        return both[:rows] + both[rows:] + mm_lanes(high, bases[at(1), :])

    def upper(rows):
        return (lax.broadcasted_iota(jnp.int32, (rows, width), 0) & GROUP) == 0

    def swapped(tile):
        return pltpu.roll(tile, GROUP, 0)

    in_table = table[pl.ds(2 * width + 2 * depth, stacked), :]
    for c in range(CHUNKS):
        for copy in moments[c]:
            copy.wait_recv()
        high = mom_in[c].astype(BF16).astype(F32)
        low = (mom_in[c] - high).astype(BF16).astype(F32)
        parts = [high, low, high]
        if stacked > 3 * depth:
            parts.append(jnp.zeros((stacked - 3 * depth, high.shape[1]), F32))
        stack = jnp.concatenate(parts, axis=0).T.astype(BF16)
        near[c] = near[c] + mm(stack, in_table)
        for first in reversed(range(0, span, BLOCK)) if c == 0 else range(0, span, BLOCK):
            rows = pl.ds(c * span + first, BLOCK)
            wave_sine, wave_cosine = sines[rows, :], cosines[rows, :]
            weight = share[c * span + first : c * span + first + BLOCK]
            for x in range(axial):
                values = []
                for f in range(fields):
                    slot = 2 * (f * axial + x) * span + first
                    kept_value = (
                        wave_sine * near[c, pl.ds(slot, BLOCK), :]
                        - wave_cosine * near[c, pl.ds(slot + span, BLOCK), :]
                        + weight * state[f, x, rows, :]
                    )
                    state[f, x, rows, :] = kept_value
                    values.append(kept_value)
                axial_flux(values, x, rows)
            for end, pair in ends:
                if 0 < end - (c * span + first) <= BLOCK:
                    for copy in pair:
                        copy.start()
        if c == 0:
            loads[4].wait()
            tiles = [
                [state[f, x, pl.ds(TILE * t, TILE), :] for f, x in planes] for t in range(PACKED * GROUP // TILE)
            ]
            first, middle, last = [split(jnp.concatenate(tile, axis=0)) for tile in tiles]
            middle_swapped, last_swapped = [
                split(jnp.concatenate([swapped(part) for part in tile], axis=0)) for tile in tiles[1:]
            ]
            outside = jnp.where(
                upper(len(planes) * TILE),
                into_basis(0, *first) + into_basis(5, *last_swapped),
                into_basis(1, *first) + into_basis(4, *last_swapped),
            )
            inside = into_basis(2, *middle) + into_basis(3, *middle_swapped)
            for p, (f, x) in enumerate(planes):
                low_own[f, x] = outside[p * TILE : (p + 1) * TILE]
            for f in range(fields):
                even, odd = [inside[p * TILE : (p + 1) * TILE] for p in (2 * f, 2 * f + 1)]
                low_own[f, axial] = jnp.where(upper(TILE), even, swapped(odd))
            for copy in crossings[2]:
                copy.start()

    radius_of = lambda first, size: (
        lax.broadcasted_iota(jnp.int32, (size, width), 0) + first
    ).astype(F32) + 0.5
    loads[2].wait()
    for first in range(0, cycles, BLOCK):
        rows = pl.ds(first, BLOCK)
        radius = radius_of(first, BLOCK)
        inv_radius = 1.0 / radius
        for x in range(axial):
            values = [state[f, x, rows, :] for f in range(fields)]
            inverse = 1.0 / values[0]
            pressure = pressure_of(values, inverse)
            for f, part in enumerate(fluxes(values, 3, inverse, pressure)):
                g_turn[f, x, rows, :] = part
            for f, part in enumerate(fluxes(values, 2, inverse, pressure)):
                g_out[f, x, rows, :] = part * radius
            rate[2, x, rows, :] = (values[3] * values[3] * inverse + pressure) * inv_radius
            rate[3, x, rows, :] = -(values[2] * values[3] * inverse) * inv_radius

    edge_lane = lax.broadcasted_iota(jnp.int32, (cycles, LANES), 1)
    pack_right = jnp.zeros((cycles, LANES), F32)
    pack_left = jnp.zeros((cycles, LANES), F32)
    for p, (f, x) in enumerate(planes):
        mine = (edge_lane >> 1) == p
        ends = g_turn[f, x, :, pl.ds(width - LANES, LANES)]
        pack_right = jnp.where(mine, pltpu.roll(ends, 2 * p + 2, 1), pack_right)
        heads = g_turn[f, x, :, pl.ds(0, LANES)]
        pack_left = jnp.where(mine, pltpu.roll(heads, 2 * p, 1) if p else heads, pack_left)
    edge_right[...] = pack_right
    edge_left[...] = pack_left
    for copy in edges:
        copy.start()

    loads[5].wait()
    inv_radius = 1.0 / radius_of(0, cycles)
    angular = inv_radius * (1.0 / (12.0 * (2.0 * math.pi / total)))
    radial = inv_radius * (1.0 / 12.0)
    tail_row = lax.broadcasted_iota(jnp.int32, (8, width), 0)
    beyond = jnp.where(
        tail_row < 2, (tail_row.astype(F32) + (cycles + 0.5)) * (1.0 / (cycles - 0.5)), 0.0
    )
    for f, x in planes:
        g = g_turn[f, x]
        turn_term = 8.0 * (pltpu.roll(g, width - 1, 1) - pltpu.roll(g, 1, 1)) - (
            pltpu.roll(g, width - 2, 1) - pltpu.roll(g, 2, 1)
        )
        g = g_out[f, x]
        tall = cycles + 8
        g = jnp.concatenate([g, beyond * g[cycles - 1 :]], axis=0)
        out_term = (
            8.0 * (pltpu.roll(g, tall - 1, 0) - pltpu.roll(g, 1, 0))
            - (pltpu.roll(g, tall - 2, 0) - pltpu.roll(g, 2, 0))
        )[:cycles]
        change = -(turn_term * angular + out_term * radial)
        if f in (2, 3):
            change = change + rate[f, x]
        rate[f, x] = begun[f, x] + STEP_DT * change

    for copy in edges:
        copy.wait_recv()
    from_left = edge_from_left[...] - edge_right[...]
    from_right = edge_from_right[...] - edge_left[...]
    even = (edge_lane & 1) == 0
    scale = -STEP_DT * angular[:, :LANES]
    from_left = scale * jnp.where(
        even, from_left - 8.0 * pltpu.roll(from_left, LANES - 1, 1), from_left
    )
    from_right = scale * jnp.where(
        even, -from_right, 8.0 * pltpu.roll(from_right, 1, 1) - from_right
    )
    head, end = pl.ds(0, LANES), pl.ds((cells - 1) // LANES * LANES, LANES)
    end_lane = (cells - 2) % LANES
    ghost_row = lax.broadcasted_iota(jnp.int32, (8, width), 0)
    ghost_scale = -STEP_DT * radial[:8]
    for p, (f, x) in enumerate(planes):
        value = pltpu.roll(from_left, (LANES - 2 * p) % LANES, 1) if p else from_left
        rate[f, x, :, head] = rate[f, x, :, head] + jnp.where(edge_lane < 2, value, 0.0)
        value = pltpu.roll(from_right, (end_lane - 2 * p) % LANES, 1)
        mine = (edge_lane >= end_lane) & (edge_lane < end_lane + 2)
        rate[f, x, :, end] = rate[f, x, :, end] + jnp.where(mine, value, 0.0)
        tile = -ghost[f, x] if f in (2, 3) else ghost[f, x]
        inside = jnp.where(
            ghost_row == 0,
            pltpu.roll(tile, 7, 0) - 8.0 * tile,
            jnp.where(ghost_row == 1, pltpu.roll(tile, 1, 0), 0.0),
        )
        rate[f, x, pl.ds(0, 8), :] = rate[f, x, pl.ds(0, 8), :] + ghost_scale * inside

    def raw_flux(ref, x, rows):
        values = [ref[f, x, rows, :] for f in range(fields)]
        inverse = 1.0 / values[0]
        return fluxes(values, 1, inverse, pressure_of(values, inverse))

    for (begin, size), pair in zip(pieces, crossings):
        for copy in pair:
            copy.wait_recv()
        if begin == 0:
            sides = (low_left, low_right)
            outside = split(jnp.concatenate([ref[f, x] for ref in sides for f, x in planes], axis=0))
            inside = split(jnp.concatenate([ref[f, axial] for ref in sides for f in range(fields)], axis=0))
            half = upper(2 * len(planes) * TILE)
            head = jnp.where(half, from_basis(0, *outside), from_basis(1, *outside))
            last = jnp.where(half, from_basis(5, *outside), from_basis(4, *outside))
            second, third = from_basis(2, *inside), from_basis(3, *inside)
            for side, ref in enumerate((fx_left, fx_right)):
                for p, (f, x) in enumerate(planes):
                    row = (side * len(planes) + p) * TILE
                    ref[f, x, pl.ds(0, TILE), :] = head[row : row + TILE]
                    ref[f, x, pl.ds(2 * TILE, TILE), :] = swapped(last[row : row + TILE])
                    row = (side * fields + f) * TILE
                    early, late = second[row : row + TILE], third[row : row + TILE]
                    early, late = (early, swapped(late)) if x == 0 else (swapped(early), late)
                    ref[f, x, pl.ds(TILE, TILE), :] = jnp.where(upper(TILE), early, late)
        for first in range(begin, begin + size, 8):
            rows = pl.ds(first, 8)
            if begin in (0, inner):
                own, left, right = [
                    [raw_flux(ref, x, rows) for x in range(axial)] for ref in (state, fx_left, fx_right)
                ]
            else:
                own, left, right = [
                    [[ref[f, x, rows, :] for f in range(fields)] for x in range(axial)]
                    for ref in (fx_own, fx_left, fx_right)
                ]
            for f in range(fields):
                terms = (
                    8.0 * (own[1][f] - left[1][f]) - (right[0][f] - left[0][f]),
                    8.0 * (right[0][f] - own[0][f]) - (right[1][f] - left[1][f]),
                )
                for x, term in enumerate(terms):
                    out[f, x, rows, :] = rate[f, x, rows, :] - (STEP_DT / 12.0) * term

    for pair in crossings:
        for copy in pair:
            copy.wait_send()
    for group in moments:
        for copy in group:
            copy.wait_send()
    for copy in edges:
        copy.wait_send()


def shards(state, start, modes):
    fields, axial, cells, cycles = state.shape
    inner = modes.shape[0]
    cfg = dict(plan(cells, lax.axis_size("azim")), cells=cells)
    width, depth = cfg["width"], cfg["depth"]
    turned, begun = [
        jnp.concatenate([values.transpose(0, 1, 3, 2)] * (width // cells), axis=3)
        for values in (state, start)
    ]
    full = (fields, axial, cycles, width)
    columns = 2 * fields * axial * inner // CHUNKS
    hbm = pl.BlockSpec(memory_space=pltpu.HBM)
    vmem = pl.BlockSpec(memory_space=pltpu.VMEM)
    peers, pieces = len(cfg["ranks"]), len(pieces_of(inner, cycles))
    tables = [jnp.asarray(cfg[name]) for name in ("table", "bases")]
    operands = (turned, begun, modes.reshape(1, inner), *tables)
    step = pl.pallas_call(
        functools.partial(kernel, cfg),
        out_shape=jax.ShapeDtypeStruct(full, F32),
        in_specs=[hbm] * 5,
        out_specs=vmem,
        scratch_shapes=[
            pltpu.VMEM(full, F32),
            pltpu.VMEM(full, F32),
            pltpu.VMEM((1, inner), jnp.int32),
            *[pltpu.VMEM(table.shape, BF16) for table in tables],
            pltpu.VMEM((inner, width), F32),
            pltpu.VMEM((inner, width), F32),
            pltpu.VMEM((CHUNKS, columns, width), BF16),
            pltpu.VMEM((CHUNKS, columns, width), BF16),
            pltpu.VMEM((CHUNKS, columns, width), F32),
            pltpu.VMEM((CHUNKS, depth, columns), F32),
            pltpu.VMEM((CHUNKS, depth, columns), F32),
        ]
        + [pltpu.VMEM(full, F32)] * 6
        + [pltpu.VMEM((fields, axial + 1, TILE, width), F32)] * 3
        + [pltpu.VMEM((cycles, LANES), F32)] * 4
        + [
            pltpu.VMEM((fields, axial, 8, width), F32),
            pltpu.SemaphoreType.DMA((6,)),
            pltpu.SemaphoreType.DMA((CHUNKS, peers)),
            pltpu.SemaphoreType.DMA((CHUNKS, peers)),
            pltpu.SemaphoreType.DMA((2, pieces)),
            pltpu.SemaphoreType.DMA((2, pieces)),
            pltpu.SemaphoreType.DMA((3,)),
            pltpu.SemaphoreType.DMA((3,)),
            pltpu.SemaphoreType.REGULAR,
        ],
        compiler_params=pltpu.CompilerParams(
            collective_id=0, has_side_effects=True, vmem_limit_bytes=48 * 1024 * 1024
        ),
        name="jet_section",
    )(*[pltpu.with_memory_space_constraint(operand, pltpu.HBM) for operand in operands])
    return step[..., :cells].transpose(0, 1, 3, 2)


def solution(mesh):
    in_specs = (P(None, "axial", "azim", None), P(None, "axial", "azim", None), P())
    out_specs = P(None, "axial", "azim", None)
    return jax.shard_map(shards, mesh=mesh, in_specs=in_specs, out_specs=out_specs, check_vma=False)
```

```python
import functools
import math

import jax
import jax.numpy as jnp
import numpy as np
from jax import lax
from jax.experimental import pallas as pl
from jax.experimental.pallas import tpu as pltpu
from jax.sharding import PartitionSpec as P

STEP_DT = 0.05
LANES = 128
CHUNKS = 2
BLOCK = 16
MSTEP = 8
TILE = 8
GROUP = 4
PACKED = 6
CUT = 1e-6
LEVELS = 3
FLOOR = 1e-9
F32 = jnp.float32
BF16 = jnp.bfloat16
MESH = pl.DeviceIdType.MESH


def split_np(values):
    high = values.astype(np.float32).astype(jnp.bfloat16)
    low = (values - high.astype(np.float64)).astype(np.float32).astype(jnp.bfloat16)
    return high, low


def round_up(value, multiple):
    return -(-value // multiple) * multiple


@functools.lru_cache(None)
def plan(cells, count):
    total = cells * count
    width = round_up(cells, LANES)
    where = np.arange(cells)

    def coupling(offset):
        distance = offset * cells + where[:, None] - where[None, :]
        sine = np.sin(np.pi * distance / total)
        return np.where(distance == 0, 0.0, 1.0 / (total * np.where(distance == 0, 1.0, sine)))

    def wide(rows):
        return np.concatenate([rows] * (width // cells), axis=1)

    def padded(rows):
        return np.pad(rows, ((0, 0), (0, width - cells)))

    local = np.zeros((width, width))
    local[:cells] = wide(coupling(0).T)
    starts, ranks, outgoing, incoming = [], [], [], []
    for offset in range(1, count):
        left, values, right = np.linalg.svd(coupling(offset))
        rank = round_up(max(int(np.sum(values > FLOOR)), 1), 8)
        starts.append(sum(ranks))
        ranks.append(rank)
        outgoing.append(padded(right[:rank]))
        incoming.append(wide((left[:, :rank] * values[:rank]).T))
    depth = sum(ranks)
    out_high, out_low = split_np(np.concatenate(outgoing))
    in_high, in_low = split_np(np.concatenate(incoming))
    stacked = round_up(3 * depth, LANES)
    blank = np.zeros((stacked - 3 * depth, width), jnp.bfloat16)
    table = np.concatenate([*split_np(local), out_high, out_low, in_high, in_high, in_low, blank])

    def band(group):
        bound = min(2 * MSTEP * GROUP * (group + 1), total // 2)
        waves = np.arange(1, bound)
        phase = 2 * np.pi * ((where[:, None] * waves) % total) / total
        scale = np.sqrt(2.0 / total)
        columns = [np.full((cells, 1), 1.0 / np.sqrt(total)), scale * np.cos(phase), scale * np.sin(phase)]
        left, values, _ = np.linalg.svd(np.concatenate(columns, axis=1))
        return left, np.append(values, np.zeros(cells + 1 - len(values)))

    blocks = [None] * PACKED
    for low in range(PACKED // 2):
        high = PACKED - 1 - low
        (first, first_values), (second, second_values) = band(low), band(high)
        sizes = range(max(width - cells, 0), min(cells, width) + 1)
        size = min(sizes, key=lambda n: max(first_values[n], second_values[width - n]))
        assert max(first_values[size], second_values[width - size]) < CUT
        blocks[low] = np.zeros((width, width))
        blocks[low][:cells, :size] = first[:, :size]
        blocks[high] = np.zeros((width, width))
        blocks[high][:cells, size:] = second[:, : width - size]
    halves = [split_np(block) for block in blocks]
    bases = np.concatenate([pair[part] for part in range(2) for pair in halves])
    return dict(
        width=width, depth=depth, stacked=stacked, starts=starts, ranks=ranks, table=table, bases=bases
    )


def pieces_of(inner, cycles):
    span = inner // CHUNKS
    packed = PACKED * GROUP
    pieces = [(inner, cycles - inner), (packed, span - packed), (0, packed)]
    pieces += [(c * span, span) for c in range(1, CHUNKS - 1)]
    return pieces + [(inner - span, span - TILE), (inner - TILE, TILE)]


def split(values):
    high = values.astype(BF16)
    return high, (values - high.astype(F32)).astype(BF16)


def mm(a, b):
    return jnp.dot(a, b, preferred_element_type=F32)


def mm_lanes(a, b):
    return lax.dot_general(a, b, (((1,), (1,)), ((), ())), preferred_element_type=F32)


def pressure_of(values, inverse):
    kinetic = (values[1] * values[1] + values[2] * values[2] + values[3] * values[3]) * inverse
    return 0.4 * (values[4] - 0.5 * kinetic)


def fluxes(values, direction, inverse, pressure):
    velocity = values[direction] * inverse
    parts = [
        values[direction],
        values[1] * velocity,
        values[2] * velocity,
        values[3] * velocity,
        (values[4] + pressure) * velocity,
    ]
    parts[direction] = parts[direction] + pressure
    return parts


def turns(steps, total):
    quarter = total // 2
    quadrant = (steps + quarter // 2) // quarter
    angle = (steps - quadrant * quarter).astype(F32) * (math.pi / total)
    square = angle * angle
    sine = angle + angle * square * (
        -1.0 / 6 + square * (1.0 / 120 + square * (-1.0 / 5040 + square * (1.0 / 362880)))
    )
    cosine = 1.0 + square * (
        -0.5
        + square * (1.0 / 24 + square * (-1.0 / 720 + square * (1.0 / 40320 - square * (1.0 / 3628800))))
    )
    odd = (quadrant & 1) == 1
    first, second = jnp.where(odd, cosine, sine), jnp.where(odd, sine, cosine)
    return (
        jnp.where((quadrant & 2) == 2, -first, first),
        jnp.where(((quadrant + 1) & 2) == 2, -second, second),
    )


def kernel(
    cfg,
    state_hbm, start_hbm, modes_hbm, table_hbm, bases_hbm, out,
    state, begun, modes, table, bases, cosines, sines,
    x_high, x_low, near, mom_own, mom_in,
    fx_own, fx_left, fx_right, g_turn, g_out, rate, low_own, low_left, low_right,
    edge_right, edge_left, edge_from_left, edge_from_right, ghost,
    load_sem, mom_send, mom_recv, fx_send, fx_recv, edge_send, edge_recv, answered,
):
    fields, axial, cycles, width = state.shape
    cells, inner = cfg["cells"], modes.shape[1]
    depth, stacked = cfg["depth"], cfg["stacked"]
    starts, ranks = cfg["starts"], cfg["ranks"]
    count, ring = lax.axis_size("azim"), lax.axis_size("axial")
    d, a = lax.axis_index("azim"), lax.axis_index("axial")
    total = cells * count
    planes = [(f, x) for f in range(fields) for x in range(axial)]
    span = inner // CHUNKS

    def z_at(offset):
        return {"azim": lax.rem(d + offset, count)}

    x_right = {"axial": lax.rem(a + 1, ring)}
    x_left = {"axial": lax.rem(a + ring - 1, ring)}

    def remote(src, dst, send, recv, device):
        return pltpu.make_async_remote_copy(
            src_ref=src, dst_ref=dst, send_sem=send, recv_sem=recv,
            device_id=device, device_id_type=MESH,
        )

    outer_rows, inner_rows = pl.ds(inner, cycles - inner), pl.ds(0, inner)
    barrier = pltpu.get_barrier_semaphore()
    level = jnp.minimum(d, LEVELS - 1)
    level_mates = jnp.where(level == LEVELS - 1, count - LEVELS, 0)
    azim_peers = [z_at(offset) for offset in range(1, count)]
    peer_levels = [jnp.minimum(device["azim"], LEVELS - 1) for device in azim_peers]
    is_earlier = [peer_level < level for peer_level in peer_levels]
    is_later = [peer_level > level for peer_level in peer_levels]

    def greet(device, semaphore=barrier):
        pl.semaphore_signal(semaphore, inc=1, device_id=device, device_id_type=MESH)

    for device in (x_right, x_left):
        greet(device)
    for device, earlier in zip(azim_peers, is_earlier):
        pl.when(jnp.logical_not(earlier))(functools.partial(greet, device))
    loads = [
        pltpu.make_async_copy(modes_hbm, modes, load_sem.at[0]),
        pltpu.make_async_copy(
            state_hbm.at[:, :, inner_rows], state.at[:, :, inner_rows], load_sem.at[1]
        ),
        pltpu.make_async_copy(
            state_hbm.at[:, :, outer_rows], state.at[:, :, outer_rows], load_sem.at[2]
        ),
        pltpu.make_async_copy(table_hbm, table, load_sem.at[3]),
        pltpu.make_async_copy(bases_hbm, bases, load_sem.at[4]),
        pltpu.make_async_copy(start_hbm, begun, load_sem.at[5]),
    ]
    for copy in loads:
        copy.start()

    moments = [
        [
            remote(
                mom_own.at[c, pl.ds(starts[k], ranks[k])], mom_in.at[c, pl.ds(starts[k], ranks[k])],
                mom_send.at[c, k], mom_recv.at[c, k], z_at(k + 1),
            )
            for k in range(len(ranks))
        ]
        for c in range(CHUNKS)
    ]
    pieces = pieces_of(inner, cycles)
    crossings = []
    for k, (first, size) in enumerate(pieces):
        rows = pl.ds(first, size)
        source = (state_hbm if first == inner else fx_own).at[:, :, rows]
        targets = fx_left.at[:, :, rows], fx_right.at[:, :, rows]
        if first == 0:
            source, targets = low_own, (low_left, low_right)
        crossings.append(
            [
                remote(source, target, fx_send.at[side, k], fx_recv.at[side, k], device)
                for side, (target, device) in enumerate(zip(targets, (x_right, x_left)))
            ]
        )
    edges = [
        remote(edge_right, edge_from_left, edge_send.at[0], edge_recv.at[0], z_at(1)),
        remote(edge_left, edge_from_right, edge_send.at[1], edge_recv.at[1], z_at(count - 1)),
        remote(
            g_out.at[:, :, pl.ds(0, 8)], ghost, edge_send.at[2], edge_recv.at[2], z_at(count // 2)
        ),
    ]

    pl.semaphore_wait(barrier, 2 + level + level_mates)
    last_core = lax.rem(a, 2) == 1
    pl.when(last_core)(crossings[0][0].start)
    pl.when(jnp.logical_not(last_core))(crossings[0][1].start)
    for device, earlier in zip(azim_peers, is_earlier):
        pl.when(earlier)(functools.partial(greet, device, answered))

    loads[0].wait()
    kept = jnp.broadcast_to(modes[...], (inner, inner)).astype(F32)
    same = lax.broadcasted_iota(jnp.int32, (inner, inner), 0) == lax.broadcasted_iota(
        jnp.int32, (inner, inner), 1
    )
    odd_count = 2.0 * jnp.sum(jnp.where(same, kept, 0.0), axis=1, keepdims=True) - 1.0
    share = odd_count * (1.0 / total)
    lane = lax.broadcasted_iota(jnp.int32, (inner, width), 1)
    place = (lax.rem(lane, cells) + d * cells).astype(F32)
    steps = (odd_count * place).astype(jnp.int32) & (2 * total - 1)
    sine, cosine = turns(steps, total)
    sines[...] = sine
    cosines[...] = cosine

    def axial_flux(values, x, rows):
        inverse = 1.0 / values[0]
        for f, part in enumerate(fluxes(values, 1, inverse, pressure_of(values, inverse))):
            fx_own[f, x, rows, :] = part

    loads[1].wait()
    loads[3].wait()
    out_table = table[pl.ds(2 * width, 2 * depth), :]
    for c in range(CHUNKS):
        rows = pl.ds(c * span, span)
        for p, (f, x) in enumerate(planes):
            value = state[f, x, rows, :]
            for part, wave in enumerate((cosines, sines)):
                high, low = split(value * wave[rows, :])
                slot = pl.ds((2 * p + part) * span, span)
                x_high[c, slot, :] = high
                x_low[c, slot, :] = low
        sums = mm_lanes(out_table, x_high[c]) + mm_lanes(out_table, x_low[c])
        sums = sums[:depth] + sums[depth:]
        for k in range(len(ranks)):
            wrapped = (1 - 2 * ((d + k + 1) // count)).astype(F32)
            mom_own[c, pl.ds(starts[k], ranks[k]), :] = (
                sums[starts[k] : starts[k] + ranks[k]] * wrapped
            )
        if c == 0:
            for copy, later in zip(moments[c], is_later):
                pl.when(jnp.logical_not(later))(copy.start)

            @pl.when(level < LEVELS - 1)
            def _():
                pl.semaphore_wait(answered, count - 1 - level)

            for copy, later in zip(moments[c], is_later):
                pl.when(later)(copy.start)
        else:
            for copy in moments[c]:
                copy.start()

    pl.when(last_core)(crossings[0][1].start)
    pl.when(jnp.logical_not(last_core))(crossings[0][0].start)
    local_high, local_low = table[pl.ds(0, width), :], table[pl.ds(width, width), :]
    for c in range(CHUNKS):
        near[c] = mm(x_high[c], local_high) + mm(x_low[c], local_high) + mm(x_high[c], local_low)

    ends = [
        (first + size, pair) for (first, size), pair in zip(pieces, crossings) if first not in (0, inner)
    ]

    def into_basis(group, high, low):
        rows, at = high.shape[0], lambda part: pl.ds((PACKED * part + group) * width, width)
        both = mm(jnp.concatenate([high, low], axis=0), bases[at(0), :])
        return both[:rows] + both[rows:] + mm(high, bases[at(1), :])

    def from_basis(group, high, low):
        rows, at = high.shape[0], lambda part: pl.ds((PACKED * part + group) * width, width)
        both = mm_lanes(jnp.concatenate([high, low], axis=0), bases[at(0), :])
        return both[:rows] + both[rows:] + mm_lanes(high, bases[at(1), :])

    def upper(rows):
        return (lax.broadcasted_iota(jnp.int32, (rows, width), 0) & GROUP) == 0

    def swapped(tile):
        return pltpu.roll(tile, GROUP, 0)

    in_table = table[pl.ds(2 * width + 2 * depth, stacked), :]
    for c in range(CHUNKS):
        for copy in moments[c]:
            copy.wait_recv()
        high = mom_in[c].astype(BF16).astype(F32)
        low = (mom_in[c] - high).astype(BF16).astype(F32)
        parts = [high, low, high]
        if stacked > 3 * depth:
            parts.append(jnp.zeros((stacked - 3 * depth, high.shape[1]), F32))
        stack = jnp.concatenate(parts, axis=0).T.astype(BF16)
        near[c] = near[c] + mm(stack, in_table)
        for first in reversed(range(0, span, BLOCK)) if c == 0 else range(0, span, BLOCK):
            rows = pl.ds(c * span + first, BLOCK)
            wave_sine, wave_cosine = sines[rows, :], cosines[rows, :]
            weight = share[c * span + first : c * span + first + BLOCK]
            for x in range(axial):
                values = []
                for f in range(fields):
                    slot = 2 * (f * axial + x) * span + first
                    kept_value = (
                        wave_sine * near[c, pl.ds(slot, BLOCK), :]
                        - wave_cosine * near[c, pl.ds(slot + span, BLOCK), :]
                        + weight * state[f, x, rows, :]
                    )
                    state[f, x, rows, :] = kept_value
                    values.append(kept_value)
                axial_flux(values, x, rows)
            for end, pair in ends:
                if 0 < end - (c * span + first) <= BLOCK:
                    for copy in pair:
                        copy.start()
        if c == 0:
            loads[4].wait()
            tiles = [
                [state[f, x, pl.ds(TILE * t, TILE), :] for f, x in planes] for t in range(PACKED * GROUP // TILE)
            ]
            first, middle, last = [split(jnp.concatenate(tile, axis=0)) for tile in tiles]
            middle_swapped, last_swapped = [
                split(jnp.concatenate([swapped(part) for part in tile], axis=0)) for tile in tiles[1:]
            ]
            outside = jnp.where(
                upper(len(planes) * TILE),
                into_basis(0, *first) + into_basis(5, *last_swapped),
                into_basis(1, *first) + into_basis(4, *last_swapped),
            )
            inside = into_basis(2, *middle) + into_basis(3, *middle_swapped)
            for p, (f, x) in enumerate(planes):
                low_own[f, x] = outside[p * TILE : (p + 1) * TILE]
            for f in range(fields):
                even, odd = [inside[p * TILE : (p + 1) * TILE] for p in (2 * f, 2 * f + 1)]
                low_own[f, axial] = jnp.where(upper(TILE), even, swapped(odd))
            for copy in crossings[2]:
                copy.start()

    radius_of = lambda first, size: (
        lax.broadcasted_iota(jnp.int32, (size, width), 0) + first
    ).astype(F32) + 0.5
    loads[2].wait()
    for first in range(0, cycles, BLOCK):
        rows = pl.ds(first, BLOCK)
        radius = radius_of(first, BLOCK)
        inv_radius = 1.0 / radius
        for x in range(axial):
            values = [state[f, x, rows, :] for f in range(fields)]
            inverse = 1.0 / values[0]
            pressure = pressure_of(values, inverse)
            for f, part in enumerate(fluxes(values, 3, inverse, pressure)):
                g_turn[f, x, rows, :] = part
            for f, part in enumerate(fluxes(values, 2, inverse, pressure)):
                g_out[f, x, rows, :] = part * radius
            rate[2, x, rows, :] = (values[3] * values[3] * inverse + pressure) * inv_radius
            rate[3, x, rows, :] = -(values[2] * values[3] * inverse) * inv_radius

    edge_lane = lax.broadcasted_iota(jnp.int32, (cycles, LANES), 1)
    pack_right = jnp.zeros((cycles, LANES), F32)
    pack_left = jnp.zeros((cycles, LANES), F32)
    for p, (f, x) in enumerate(planes):
        mine = (edge_lane >> 1) == p
        ends = g_turn[f, x, :, pl.ds(width - LANES, LANES)]
        pack_right = jnp.where(mine, pltpu.roll(ends, 2 * p + 2, 1), pack_right)
        heads = g_turn[f, x, :, pl.ds(0, LANES)]
        pack_left = jnp.where(mine, pltpu.roll(heads, 2 * p, 1) if p else heads, pack_left)
    edge_right[...] = pack_right
    edge_left[...] = pack_left
    for copy in edges:
        copy.start()

    loads[5].wait()
    inv_radius = 1.0 / radius_of(0, cycles)
    angular = inv_radius * (1.0 / (12.0 * (2.0 * math.pi / total)))
    radial = inv_radius * (1.0 / 12.0)
    tail_row = lax.broadcasted_iota(jnp.int32, (8, width), 0)
    beyond = jnp.where(
        tail_row < 2, (tail_row.astype(F32) + (cycles + 0.5)) * (1.0 / (cycles - 0.5)), 0.0
    )
    for f, x in planes:
        g = g_turn[f, x]
        turn_term = 8.0 * (pltpu.roll(g, width - 1, 1) - pltpu.roll(g, 1, 1)) - (
            pltpu.roll(g, width - 2, 1) - pltpu.roll(g, 2, 1)
        )
        g = g_out[f, x]
        tall = cycles + 8
        g = jnp.concatenate([g, beyond * g[cycles - 1 :]], axis=0)
        out_term = (
            8.0 * (pltpu.roll(g, tall - 1, 0) - pltpu.roll(g, 1, 0))
            - (pltpu.roll(g, tall - 2, 0) - pltpu.roll(g, 2, 0))
        )[:cycles]
        change = -(turn_term * angular + out_term * radial)
        if f in (2, 3):
            change = change + rate[f, x]
        rate[f, x] = begun[f, x] + STEP_DT * change

    for copy in edges:
        copy.wait_recv()
    from_left = edge_from_left[...] - edge_right[...]
    from_right = edge_from_right[...] - edge_left[...]
    even = (edge_lane & 1) == 0
    scale = -STEP_DT * angular[:, :LANES]
    from_left = scale * jnp.where(
        even, from_left - 8.0 * pltpu.roll(from_left, LANES - 1, 1), from_left
    )
    from_right = scale * jnp.where(
        even, -from_right, 8.0 * pltpu.roll(from_right, 1, 1) - from_right
    )
    head, end = pl.ds(0, LANES), pl.ds((cells - 1) // LANES * LANES, LANES)
    end_lane = (cells - 2) % LANES
    ghost_row = lax.broadcasted_iota(jnp.int32, (8, width), 0)
    ghost_scale = -STEP_DT * radial[:8]
    for p, (f, x) in enumerate(planes):
        value = pltpu.roll(from_left, (LANES - 2 * p) % LANES, 1) if p else from_left
        rate[f, x, :, head] = rate[f, x, :, head] + jnp.where(edge_lane < 2, value, 0.0)
        value = pltpu.roll(from_right, (end_lane - 2 * p) % LANES, 1)
        mine = (edge_lane >= end_lane) & (edge_lane < end_lane + 2)
        rate[f, x, :, end] = rate[f, x, :, end] + jnp.where(mine, value, 0.0)
        tile = -ghost[f, x] if f in (2, 3) else ghost[f, x]
        inside = jnp.where(
            ghost_row == 0,
            pltpu.roll(tile, 7, 0) - 8.0 * tile,
            jnp.where(ghost_row == 1, pltpu.roll(tile, 1, 0), 0.0),
        )
        rate[f, x, pl.ds(0, 8), :] = rate[f, x, pl.ds(0, 8), :] + ghost_scale * inside

    def raw_flux(ref, x, rows):
        values = [ref[f, x, rows, :] for f in range(fields)]
        inverse = 1.0 / values[0]
        return fluxes(values, 1, inverse, pressure_of(values, inverse))

    for (begin, size), pair in zip(pieces, crossings):
        for copy in pair:
            copy.wait_recv()
        if begin == 0:
            sides = (low_left, low_right)
            outside = split(jnp.concatenate([ref[f, x] for ref in sides for f, x in planes], axis=0))
            inside = split(jnp.concatenate([ref[f, axial] for ref in sides for f in range(fields)], axis=0))
            half = upper(2 * len(planes) * TILE)
            head = jnp.where(half, from_basis(0, *outside), from_basis(1, *outside))
            last = jnp.where(half, from_basis(5, *outside), from_basis(4, *outside))
            second, third = from_basis(2, *inside), from_basis(3, *inside)
            for side, ref in enumerate((fx_left, fx_right)):
                for p, (f, x) in enumerate(planes):
                    row = (side * len(planes) + p) * TILE
                    ref[f, x, pl.ds(0, TILE), :] = head[row : row + TILE]
                    ref[f, x, pl.ds(2 * TILE, TILE), :] = swapped(last[row : row + TILE])
                    row = (side * fields + f) * TILE
                    early, late = second[row : row + TILE], third[row : row + TILE]
                    early, late = (early, swapped(late)) if x == 0 else (swapped(early), late)
                    ref[f, x, pl.ds(TILE, TILE), :] = jnp.where(upper(TILE), early, late)
        for first in range(begin, begin + size, 8):
            rows = pl.ds(first, 8)
            if begin in (0, inner):
                own, left, right = [
                    [raw_flux(ref, x, rows) for x in range(axial)] for ref in (state, fx_left, fx_right)
                ]
            else:
                own, left, right = [
                    [[ref[f, x, rows, :] for f in range(fields)] for x in range(axial)]
                    for ref in (fx_own, fx_left, fx_right)
                ]
            for f in range(fields):
                terms = (
                    8.0 * (own[1][f] - left[1][f]) - (right[0][f] - left[0][f]),
                    8.0 * (right[0][f] - own[0][f]) - (right[1][f] - left[1][f]),
                )
                for x, term in enumerate(terms):
                    out[f, x, rows, :] = rate[f, x, rows, :] - (STEP_DT / 12.0) * term

    for pair in crossings:
        for copy in pair:
            copy.wait_send()
    for group in moments:
        for copy in group:
            copy.wait_send()
    for copy in edges:
        copy.wait_send()


def shards(state, start, modes):
    fields, axial, cells, cycles = state.shape
    inner = modes.shape[0]
    cfg = dict(plan(cells, lax.axis_size("azim")), cells=cells)
    width, depth = cfg["width"], cfg["depth"]
    turned, begun = [
        jnp.concatenate([values.transpose(0, 1, 3, 2)] * (width // cells), axis=3)
        for values in (state, start)
    ]
    full = (fields, axial, cycles, width)
    columns = 2 * fields * axial * inner // CHUNKS
    hbm = pl.BlockSpec(memory_space=pltpu.HBM)
    vmem = pl.BlockSpec(memory_space=pltpu.VMEM)
    peers, pieces = len(cfg["ranks"]), len(pieces_of(inner, cycles))
    tables = [jnp.asarray(cfg[name]) for name in ("table", "bases")]
    operands = (turned, begun, modes.reshape(1, inner), *tables)
    step = pl.pallas_call(
        functools.partial(kernel, cfg),
        out_shape=jax.ShapeDtypeStruct(full, F32),
        in_specs=[hbm] * 5,
        out_specs=vmem,
        scratch_shapes=[
            pltpu.VMEM(full, F32),
            pltpu.VMEM(full, F32),
            pltpu.VMEM((1, inner), jnp.int32),
            *[pltpu.VMEM(table.shape, BF16) for table in tables],
            pltpu.VMEM((inner, width), F32),
            pltpu.VMEM((inner, width), F32),
            pltpu.VMEM((CHUNKS, columns, width), BF16),
            pltpu.VMEM((CHUNKS, columns, width), BF16),
            pltpu.VMEM((CHUNKS, columns, width), F32),
            pltpu.VMEM((CHUNKS, depth, columns), F32),
            pltpu.VMEM((CHUNKS, depth, columns), F32),
        ]
        + [pltpu.VMEM(full, F32)] * 6
        + [pltpu.VMEM((fields, axial + 1, TILE, width), F32)] * 3
        + [pltpu.VMEM((cycles, LANES), F32)] * 4
        + [
            pltpu.VMEM((fields, axial, 8, width), F32),
            pltpu.SemaphoreType.DMA((6,)),
            pltpu.SemaphoreType.DMA((CHUNKS, peers)),
            pltpu.SemaphoreType.DMA((CHUNKS, peers)),
            pltpu.SemaphoreType.DMA((2, pieces)),
            pltpu.SemaphoreType.DMA((2, pieces)),
            pltpu.SemaphoreType.DMA((3,)),
            pltpu.SemaphoreType.DMA((3,)),
            pltpu.SemaphoreType.REGULAR,
        ],
        compiler_params=pltpu.CompilerParams(
            collective_id=0, has_side_effects=True, vmem_limit_bytes=48 * 1024 * 1024
        ),
        name="jet_section",
    )(*[pltpu.with_memory_space_constraint(operand, pltpu.HBM) for operand in operands])
    return step[..., :cells].transpose(0, 1, 3, 2)


def solution(mesh):
    in_specs = (P(None, "axial", "azim", None), P(None, "axial", "azim", None), P())
    out_specs = P(None, "axial", "azim", None)
    return jax.shard_map(shards, mesh=mesh, in_specs=in_specs, out_specs=out_specs, check_vma=False)
```

```python
import functools
import math

import jax
import jax.numpy as jnp
import numpy as np
from jax import lax
from jax.experimental import pallas as pl
from jax.experimental.pallas import tpu as pltpu
from jax.sharding import PartitionSpec as P

STEP_DT = 0.05
LANES = 128
CHUNKS = 2
BLOCK = 16
MSTEP = 8
TILE = 8
GROUP = 4
PACKED = 6
CUT = 1e-6
LEVELS = 3
FLOOR = 1e-9
F32 = jnp.float32
BF16 = jnp.bfloat16
MESH = pl.DeviceIdType.MESH


def split_np(values):
    high = values.astype(np.float32).astype(jnp.bfloat16)
    low = (values - high.astype(np.float64)).astype(np.float32).astype(jnp.bfloat16)
    return high, low


def round_up(value, multiple):
    return -(-value // multiple) * multiple


@functools.lru_cache(None)
def plan(cells, count):
    total = cells * count
    width = round_up(cells, LANES)
    where = np.arange(cells)

    def coupling(offset):
        distance = offset * cells + where[:, None] - where[None, :]
        sine = np.sin(np.pi * distance / total)
        return np.where(distance == 0, 0.0, 1.0 / (total * np.where(distance == 0, 1.0, sine)))

    def wide(rows):
        return np.concatenate([rows] * (width // cells), axis=1)

    def padded(rows):
        return np.pad(rows, ((0, 0), (0, width - cells)))

    local = np.zeros((width, width))
    local[:cells] = wide(coupling(0).T)
    starts, ranks, outgoing, incoming = [], [], [], []
    for offset in range(1, count):
        left, values, right = np.linalg.svd(coupling(offset))
        rank = round_up(max(int(np.sum(values > FLOOR)), 1), 8)
        starts.append(sum(ranks))
        ranks.append(rank)
        outgoing.append(padded(right[:rank]))
        incoming.append(wide((left[:, :rank] * values[:rank]).T))
    depth = sum(ranks)
    out_high, out_low = split_np(np.concatenate(outgoing))
    in_high, in_low = split_np(np.concatenate(incoming))
    stacked = round_up(3 * depth, LANES)
    blank = np.zeros((stacked - 3 * depth, width), jnp.bfloat16)
    table = np.concatenate([*split_np(local), out_high, out_low, in_high, in_high, in_low, blank])

    def band(group):
        bound = min(2 * MSTEP * GROUP * (group + 1), total // 2)
        waves = np.arange(1, bound)
        phase = 2 * np.pi * ((where[:, None] * waves) % total) / total
        scale = np.sqrt(2.0 / total)
        columns = [np.full((cells, 1), 1.0 / np.sqrt(total)), scale * np.cos(phase), scale * np.sin(phase)]
        left, values, _ = np.linalg.svd(np.concatenate(columns, axis=1))
        return left, np.append(values, np.zeros(cells + 1 - len(values)))

    blocks = [None] * PACKED
    for low in range(PACKED // 2):
        high = PACKED - 1 - low
        (first, first_values), (second, second_values) = band(low), band(high)
        sizes = range(max(width - cells, 0), min(cells, width) + 1)
        size = min(sizes, key=lambda n: max(first_values[n], second_values[width - n]))
        assert max(first_values[size], second_values[width - size]) < CUT
        blocks[low] = np.zeros((width, width))
        blocks[low][:cells, :size] = first[:, :size]
        blocks[high] = np.zeros((width, width))
        blocks[high][:cells, size:] = second[:, : width - size]
    halves = [split_np(block) for block in blocks]
    bases = np.concatenate([pair[part] for part in range(2) for pair in halves])
    return dict(
        width=width, depth=depth, stacked=stacked, starts=starts, ranks=ranks, table=table, bases=bases
    )


def pieces_of(inner, cycles):
    span = inner // CHUNKS
    packed = PACKED * GROUP
    pieces = [(inner, cycles - inner), (packed, span - packed), (0, packed)]
    pieces += [(c * span, span) for c in range(1, CHUNKS - 1)]
    return pieces + [(inner - span, span - 2 * TILE), (inner - 2 * TILE, 2 * TILE)]


def split(values):
    high = values.astype(BF16)
    return high, (values - high.astype(F32)).astype(BF16)


def mm(a, b):
    return jnp.dot(a, b, preferred_element_type=F32)


def mm_lanes(a, b):
    return lax.dot_general(a, b, (((1,), (1,)), ((), ())), preferred_element_type=F32)


def pressure_of(values, inverse):
    kinetic = (values[1] * values[1] + values[2] * values[2] + values[3] * values[3]) * inverse
    return 0.4 * (values[4] - 0.5 * kinetic)


def fluxes(values, direction, inverse, pressure):
    velocity = values[direction] * inverse
    parts = [
        values[direction],
        values[1] * velocity,
        values[2] * velocity,
        values[3] * velocity,
        (values[4] + pressure) * velocity,
    ]
    parts[direction] = parts[direction] + pressure
    return parts


def turns(steps, total):
    quarter = total // 2
    quadrant = (steps + quarter // 2) // quarter
    angle = (steps - quadrant * quarter).astype(F32) * (math.pi / total)
    square = angle * angle
    sine = angle + angle * square * (
        -1.0 / 6 + square * (1.0 / 120 + square * (-1.0 / 5040 + square * (1.0 / 362880)))
    )
    cosine = 1.0 + square * (
        -0.5
        + square * (1.0 / 24 + square * (-1.0 / 720 + square * (1.0 / 40320 - square * (1.0 / 3628800))))
    )
    odd = (quadrant & 1) == 1
    first, second = jnp.where(odd, cosine, sine), jnp.where(odd, sine, cosine)
    return (
        jnp.where((quadrant & 2) == 2, -first, first),
        jnp.where(((quadrant + 1) & 2) == 2, -second, second),
    )


def kernel(
    cfg,
    state_hbm, start_hbm, modes_hbm, table_hbm, bases_hbm, out,
    state, begun, modes, table, bases, cosines, sines,
    x_high, x_low, near, mom_own, mom_in,
    fx_own, fx_left, fx_right, g_turn, g_out, rate, low_own, low_left, low_right,
    edge_right, edge_left, edge_from_left, edge_from_right, ghost,
    load_sem, mom_send, mom_recv, fx_send, fx_recv, edge_send, edge_recv, answered,
):
    fields, axial, cycles, width = state.shape
    cells, inner = cfg["cells"], modes.shape[1]
    depth, stacked = cfg["depth"], cfg["stacked"]
    starts, ranks = cfg["starts"], cfg["ranks"]
    count, ring = lax.axis_size("azim"), lax.axis_size("axial")
    d, a = lax.axis_index("azim"), lax.axis_index("axial")
    total = cells * count
    planes = [(f, x) for f in range(fields) for x in range(axial)]
    span = inner // CHUNKS

    def z_at(offset):
        return {"azim": lax.rem(d + offset, count)}

    x_right = {"axial": lax.rem(a + 1, ring)}
    x_left = {"axial": lax.rem(a + ring - 1, ring)}

    def remote(src, dst, send, recv, device):
        return pltpu.make_async_remote_copy(
            src_ref=src, dst_ref=dst, send_sem=send, recv_sem=recv,
            device_id=device, device_id_type=MESH,
        )

    outer_rows, inner_rows = pl.ds(inner, cycles - inner), pl.ds(0, inner)
    barrier = pltpu.get_barrier_semaphore()
    level = jnp.minimum(d, LEVELS - 1)
    level_mates = jnp.where(level == LEVELS - 1, count - LEVELS, 0)
    azim_peers = [z_at(offset) for offset in range(1, count)]
    peer_levels = [jnp.minimum(device["azim"], LEVELS - 1) for device in azim_peers]
    is_earlier = [peer_level < level for peer_level in peer_levels]
    is_later = [peer_level > level for peer_level in peer_levels]

    def greet(device, semaphore=barrier):
        pl.semaphore_signal(semaphore, inc=1, device_id=device, device_id_type=MESH)

    for device in (x_right, x_left):
        greet(device)
    for device, earlier in zip(azim_peers, is_earlier):
        pl.when(jnp.logical_not(earlier))(functools.partial(greet, device))
    loads = [
        pltpu.make_async_copy(modes_hbm, modes, load_sem.at[0]),
        pltpu.make_async_copy(
            state_hbm.at[:, :, inner_rows], state.at[:, :, inner_rows], load_sem.at[1]
        ),
        pltpu.make_async_copy(
            state_hbm.at[:, :, outer_rows], state.at[:, :, outer_rows], load_sem.at[2]
        ),
        pltpu.make_async_copy(table_hbm, table, load_sem.at[3]),
        pltpu.make_async_copy(bases_hbm, bases, load_sem.at[4]),
        pltpu.make_async_copy(start_hbm, begun, load_sem.at[5]),
    ]
    for copy in loads:
        copy.start()

    moments = [
        [
            remote(
                mom_own.at[c, pl.ds(starts[k], ranks[k])], mom_in.at[c, pl.ds(starts[k], ranks[k])],
                mom_send.at[c, k], mom_recv.at[c, k], z_at(k + 1),
            )
            for k in range(len(ranks))
        ]
        for c in range(CHUNKS)
    ]
    pieces = pieces_of(inner, cycles)
    crossings = []
    for k, (first, size) in enumerate(pieces):
        rows = pl.ds(first, size)
        source = (state_hbm if first == inner else fx_own).at[:, :, rows]
        targets = fx_left.at[:, :, rows], fx_right.at[:, :, rows]
        if first == 0:
            source, targets = low_own, (low_left, low_right)
        crossings.append(
            [
                remote(source, target, fx_send.at[side, k], fx_recv.at[side, k], device)
                for side, (target, device) in enumerate(zip(targets, (x_right, x_left)))
            ]
        )
    edges = [
        remote(edge_right, edge_from_left, edge_send.at[0], edge_recv.at[0], z_at(1)),
        remote(edge_left, edge_from_right, edge_send.at[1], edge_recv.at[1], z_at(count - 1)),
        remote(
            g_out.at[:, :, pl.ds(0, 8)], ghost, edge_send.at[2], edge_recv.at[2], z_at(count // 2)
        ),
    ]

    pl.semaphore_wait(barrier, 2 + level + level_mates)
    for copy in crossings[0]:
        copy.start()
    for device, earlier in zip(azim_peers, is_earlier):
        pl.when(earlier)(functools.partial(greet, device, answered))

    loads[0].wait()
    kept = jnp.broadcast_to(modes[...], (inner, inner)).astype(F32)
    same = lax.broadcasted_iota(jnp.int32, (inner, inner), 0) == lax.broadcasted_iota(
        jnp.int32, (inner, inner), 1
    )
    odd_count = 2.0 * jnp.sum(jnp.where(same, kept, 0.0), axis=1, keepdims=True) - 1.0
    share = odd_count * (1.0 / total)
    lane = lax.broadcasted_iota(jnp.int32, (inner, width), 1)
    place = (lax.rem(lane, cells) + d * cells).astype(F32)
    steps = (odd_count * place).astype(jnp.int32) & (2 * total - 1)
    sine, cosine = turns(steps, total)
    sines[...] = sine
    cosines[...] = cosine

    def axial_flux(values, x, rows):
        inverse = 1.0 / values[0]
        for f, part in enumerate(fluxes(values, 1, inverse, pressure_of(values, inverse))):
            fx_own[f, x, rows, :] = part

    loads[1].wait()
    loads[3].wait()
    out_table = table[pl.ds(2 * width, 2 * depth), :]
    for c in range(CHUNKS):
        rows = pl.ds(c * span, span)
        for p, (f, x) in enumerate(planes):
            value = state[f, x, rows, :]
            for part, wave in enumerate((cosines, sines)):
                high, low = split(value * wave[rows, :])
                slot = pl.ds((2 * p + part) * span, span)
                x_high[c, slot, :] = high
                x_low[c, slot, :] = low
        sums = mm_lanes(out_table, x_high[c]) + mm_lanes(out_table, x_low[c])
        sums = sums[:depth] + sums[depth:]
        for k in range(len(ranks)):
            wrapped = (1 - 2 * ((d + k + 1) // count)).astype(F32)
            mom_own[c, pl.ds(starts[k], ranks[k]), :] = (
                sums[starts[k] : starts[k] + ranks[k]] * wrapped
            )
        if c == 0:
            for copy, later in zip(moments[c], is_later):
                pl.when(jnp.logical_not(later))(copy.start)

            @pl.when(level < LEVELS - 1)
            def _():
                pl.semaphore_wait(answered, count - 1 - level)

            for copy, later in zip(moments[c], is_later):
                pl.when(later)(copy.start)
        else:
            for copy in moments[c]:
                copy.start()

    local_high, local_low = table[pl.ds(0, width), :], table[pl.ds(width, width), :]
    for c in range(CHUNKS):
        near[c] = mm(x_high[c], local_high) + mm(x_low[c], local_high) + mm(x_high[c], local_low)

    ends = [
        (first + size, pair) for (first, size), pair in zip(pieces, crossings) if first not in (0, inner)
    ]

    def into_basis(group, high, low):
        rows, at = high.shape[0], lambda part: pl.ds((PACKED * part + group) * width, width)
        both = mm(jnp.concatenate([high, low], axis=0), bases[at(0), :])
        return both[:rows] + both[rows:] + mm(high, bases[at(1), :])

    def from_basis(group, high, low):
        rows, at = high.shape[0], lambda part: pl.ds((PACKED * part + group) * width, width)
        both = mm_lanes(jnp.concatenate([high, low], axis=0), bases[at(0), :])
        return both[:rows] + both[rows:] + mm_lanes(high, bases[at(1), :])

    def upper(rows):
        return (lax.broadcasted_iota(jnp.int32, (rows, width), 0) & GROUP) == 0

    def swapped(tile):
        return pltpu.roll(tile, GROUP, 0)

    in_table = table[pl.ds(2 * width + 2 * depth, stacked), :]
    for c in range(CHUNKS):
        for copy in moments[c]:
            copy.wait_recv()
        high = mom_in[c].astype(BF16).astype(F32)
        low = (mom_in[c] - high).astype(BF16).astype(F32)
        parts = [high, low, high]
        if stacked > 3 * depth:
            parts.append(jnp.zeros((stacked - 3 * depth, high.shape[1]), F32))
        stack = jnp.concatenate(parts, axis=0).T.astype(BF16)
        near[c] = near[c] + mm(stack, in_table)
        for first in reversed(range(0, span, BLOCK)) if c == 0 else range(0, span, BLOCK):
            rows = pl.ds(c * span + first, BLOCK)
            wave_sine, wave_cosine = sines[rows, :], cosines[rows, :]
            weight = share[c * span + first : c * span + first + BLOCK]
            for x in range(axial):
                values = []
                for f in range(fields):
                    slot = 2 * (f * axial + x) * span + first
                    kept_value = (
                        wave_sine * near[c, pl.ds(slot, BLOCK), :]
                        - wave_cosine * near[c, pl.ds(slot + span, BLOCK), :]
                        + weight * state[f, x, rows, :]
                    )
                    state[f, x, rows, :] = kept_value
                    values.append(kept_value)
                axial_flux(values, x, rows)
            for end, pair in ends:
                if 0 < end - (c * span + first) <= BLOCK:
                    pair[1].start()
                    if end < inner:
                        pair[0].start()
        if c == 0:
            loads[4].wait()
            tiles = [
                [state[f, x, pl.ds(TILE * t, TILE), :] for f, x in planes] for t in range(PACKED * GROUP // TILE)
            ]
            first, middle, last = [split(jnp.concatenate(tile, axis=0)) for tile in tiles]
            middle_swapped, last_swapped = [
                split(jnp.concatenate([swapped(part) for part in tile], axis=0)) for tile in tiles[1:]
            ]
            outside = jnp.where(
                upper(len(planes) * TILE),
                into_basis(0, *first) + into_basis(5, *last_swapped),
                into_basis(1, *first) + into_basis(4, *last_swapped),
            )
            inside = into_basis(2, *middle) + into_basis(3, *middle_swapped)
            for p, (f, x) in enumerate(planes):
                low_own[f, x] = outside[p * TILE : (p + 1) * TILE]
            for f in range(fields):
                even, odd = [inside[p * TILE : (p + 1) * TILE] for p in (2 * f, 2 * f + 1)]
                low_own[f, axial] = jnp.where(upper(TILE), even, swapped(odd))
            for copy in crossings[2]:
                copy.start()

    radius_of = lambda first, size: (
        lax.broadcasted_iota(jnp.int32, (size, width), 0) + first
    ).astype(F32) + 0.5
    loads[2].wait()
    for first in range(0, cycles, BLOCK):
        rows = pl.ds(first, BLOCK)
        radius = radius_of(first, BLOCK)
        inv_radius = 1.0 / radius
        for x in range(axial):
            values = [state[f, x, rows, :] for f in range(fields)]
            inverse = 1.0 / values[0]
            pressure = pressure_of(values, inverse)
            for f, part in enumerate(fluxes(values, 3, inverse, pressure)):
                g_turn[f, x, rows, :] = part
            for f, part in enumerate(fluxes(values, 2, inverse, pressure)):
                g_out[f, x, rows, :] = part * radius
            rate[2, x, rows, :] = (values[3] * values[3] * inverse + pressure) * inv_radius
            rate[3, x, rows, :] = -(values[2] * values[3] * inverse) * inv_radius

    edge_lane = lax.broadcasted_iota(jnp.int32, (cycles, LANES), 1)
    pack_right = jnp.zeros((cycles, LANES), F32)
    pack_left = jnp.zeros((cycles, LANES), F32)
    for p, (f, x) in enumerate(planes):
        mine = (edge_lane >> 1) == p
        ends = g_turn[f, x, :, pl.ds(width - LANES, LANES)]
        pack_right = jnp.where(mine, pltpu.roll(ends, 2 * p + 2, 1), pack_right)
        heads = g_turn[f, x, :, pl.ds(0, LANES)]
        pack_left = jnp.where(mine, pltpu.roll(heads, 2 * p, 1) if p else heads, pack_left)
    edge_right[...] = pack_right
    edge_left[...] = pack_left
    for copy in edges:
        copy.start()

    loads[5].wait()
    inv_radius = 1.0 / radius_of(0, cycles)
    angular = inv_radius * (1.0 / (12.0 * (2.0 * math.pi / total)))
    radial = inv_radius * (1.0 / 12.0)
    tail_row = lax.broadcasted_iota(jnp.int32, (8, width), 0)
    beyond = jnp.where(
        tail_row < 2, (tail_row.astype(F32) + (cycles + 0.5)) * (1.0 / (cycles - 0.5)), 0.0
    )
    for f, x in planes:
        g = g_turn[f, x]
        turn_term = 8.0 * (pltpu.roll(g, width - 1, 1) - pltpu.roll(g, 1, 1)) - (
            pltpu.roll(g, width - 2, 1) - pltpu.roll(g, 2, 1)
        )
        g = g_out[f, x]
        tall = cycles + 8
        g = jnp.concatenate([g, beyond * g[cycles - 1 :]], axis=0)
        out_term = (
            8.0 * (pltpu.roll(g, tall - 1, 0) - pltpu.roll(g, 1, 0))
            - (pltpu.roll(g, tall - 2, 0) - pltpu.roll(g, 2, 0))
        )[:cycles]
        change = -(turn_term * angular + out_term * radial)
        if f in (2, 3):
            change = change + rate[f, x]
        rate[f, x] = begun[f, x] + STEP_DT * change

    for copy in edges:
        copy.wait_recv()
    from_left = edge_from_left[...] - edge_right[...]
    from_right = edge_from_right[...] - edge_left[...]
    even = (edge_lane & 1) == 0
    scale = -STEP_DT * angular[:, :LANES]
    from_left = scale * jnp.where(
        even, from_left - 8.0 * pltpu.roll(from_left, LANES - 1, 1), from_left
    )
    from_right = scale * jnp.where(
        even, -from_right, 8.0 * pltpu.roll(from_right, 1, 1) - from_right
    )
    head, end = pl.ds(0, LANES), pl.ds((cells - 1) // LANES * LANES, LANES)
    end_lane = (cells - 2) % LANES
    ghost_row = lax.broadcasted_iota(jnp.int32, (8, width), 0)
    ghost_scale = -STEP_DT * radial[:8]
    for p, (f, x) in enumerate(planes):
        value = pltpu.roll(from_left, (LANES - 2 * p) % LANES, 1) if p else from_left
        rate[f, x, :, head] = rate[f, x, :, head] + jnp.where(edge_lane < 2, value, 0.0)
        value = pltpu.roll(from_right, (end_lane - 2 * p) % LANES, 1)
        mine = (edge_lane >= end_lane) & (edge_lane < end_lane + 2)
        rate[f, x, :, end] = rate[f, x, :, end] + jnp.where(mine, value, 0.0)
        tile = -ghost[f, x] if f in (2, 3) else ghost[f, x]
        inside = jnp.where(
            ghost_row == 0,
            pltpu.roll(tile, 7, 0) - 8.0 * tile,
            jnp.where(ghost_row == 1, pltpu.roll(tile, 1, 0), 0.0),
        )
        rate[f, x, pl.ds(0, 8), :] = rate[f, x, pl.ds(0, 8), :] + ghost_scale * inside

    crossings[-1][0].start()

    def raw_flux(ref, x, rows):
        values = [ref[f, x, rows, :] for f in range(fields)]
        inverse = 1.0 / values[0]
        return fluxes(values, 1, inverse, pressure_of(values, inverse))

    for (begin, size), pair in zip(pieces, crossings):
        for copy in pair:
            copy.wait_recv()
        if begin == 0:
            sides = (low_left, low_right)
            outside = split(jnp.concatenate([ref[f, x] for ref in sides for f, x in planes], axis=0))
            inside = split(jnp.concatenate([ref[f, axial] for ref in sides for f in range(fields)], axis=0))
            half = upper(2 * len(planes) * TILE)
            head = jnp.where(half, from_basis(0, *outside), from_basis(1, *outside))
            last = jnp.where(half, from_basis(5, *outside), from_basis(4, *outside))
            second, third = from_basis(2, *inside), from_basis(3, *inside)
            for side, ref in enumerate((fx_left, fx_right)):
                for p, (f, x) in enumerate(planes):
                    row = (side * len(planes) + p) * TILE
                    ref[f, x, pl.ds(0, TILE), :] = head[row : row + TILE]
                    ref[f, x, pl.ds(2 * TILE, TILE), :] = swapped(last[row : row + TILE])
                    row = (side * fields + f) * TILE
                    early, late = second[row : row + TILE], third[row : row + TILE]
                    early, late = (early, swapped(late)) if x == 0 else (swapped(early), late)
                    ref[f, x, pl.ds(TILE, TILE), :] = jnp.where(upper(TILE), early, late)
        for first in range(begin, begin + size, 8):
            rows = pl.ds(first, 8)
            if begin in (0, inner):
                own, left, right = [
                    [raw_flux(ref, x, rows) for x in range(axial)] for ref in (state, fx_left, fx_right)
                ]
            else:
                own, left, right = [
                    [[ref[f, x, rows, :] for f in range(fields)] for x in range(axial)]
                    for ref in (fx_own, fx_left, fx_right)
                ]
            for f in range(fields):
                terms = (
                    8.0 * (own[1][f] - left[1][f]) - (right[0][f] - left[0][f]),
                    8.0 * (right[0][f] - own[0][f]) - (right[1][f] - left[1][f]),
                )
                for x, term in enumerate(terms):
                    out[f, x, rows, :] = rate[f, x, rows, :] - (STEP_DT / 12.0) * term

    for pair in crossings:
        for copy in pair:
            copy.wait_send()
    for group in moments:
        for copy in group:
            copy.wait_send()
    for copy in edges:
        copy.wait_send()


def shards(state, start, modes):
    fields, axial, cells, cycles = state.shape
    inner = modes.shape[0]
    cfg = dict(plan(cells, lax.axis_size("azim")), cells=cells)
    width, depth = cfg["width"], cfg["depth"]
    turned, begun = [
        jnp.concatenate([values.transpose(0, 1, 3, 2)] * (width // cells), axis=3)
        for values in (state, start)
    ]
    full = (fields, axial, cycles, width)
    columns = 2 * fields * axial * inner // CHUNKS
    hbm = pl.BlockSpec(memory_space=pltpu.HBM)
    vmem = pl.BlockSpec(memory_space=pltpu.VMEM)
    peers, pieces = len(cfg["ranks"]), len(pieces_of(inner, cycles))
    tables = [jnp.asarray(cfg[name]) for name in ("table", "bases")]
    operands = (turned, begun, modes.reshape(1, inner), *tables)
    step = pl.pallas_call(
        functools.partial(kernel, cfg),
        out_shape=jax.ShapeDtypeStruct(full, F32),
        in_specs=[hbm] * 5,
        out_specs=vmem,
        scratch_shapes=[
            pltpu.VMEM(full, F32),
            pltpu.VMEM(full, F32),
            pltpu.VMEM((1, inner), jnp.int32),
            *[pltpu.VMEM(table.shape, BF16) for table in tables],
            pltpu.VMEM((inner, width), F32),
            pltpu.VMEM((inner, width), F32),
            pltpu.VMEM((CHUNKS, columns, width), BF16),
            pltpu.VMEM((CHUNKS, columns, width), BF16),
            pltpu.VMEM((CHUNKS, columns, width), F32),
            pltpu.VMEM((CHUNKS, depth, columns), F32),
            pltpu.VMEM((CHUNKS, depth, columns), F32),
        ]
        + [pltpu.VMEM(full, F32)] * 6
        + [pltpu.VMEM((fields, axial + 1, TILE, width), F32)] * 3
        + [pltpu.VMEM((cycles, LANES), F32)] * 4
        + [
            pltpu.VMEM((fields, axial, 8, width), F32),
            pltpu.SemaphoreType.DMA((6,)),
            pltpu.SemaphoreType.DMA((CHUNKS, peers)),
            pltpu.SemaphoreType.DMA((CHUNKS, peers)),
            pltpu.SemaphoreType.DMA((2, pieces)),
            pltpu.SemaphoreType.DMA((2, pieces)),
            pltpu.SemaphoreType.DMA((3,)),
            pltpu.SemaphoreType.DMA((3,)),
            pltpu.SemaphoreType.REGULAR,
        ],
        compiler_params=pltpu.CompilerParams(
            collective_id=0, has_side_effects=True, vmem_limit_bytes=48 * 1024 * 1024
        ),
        name="jet_section",
    )(*[pltpu.with_memory_space_constraint(operand, pltpu.HBM) for operand in operands])
    return step[..., :cells].transpose(0, 1, 3, 2)


def solution(mesh):
    in_specs = (P(None, "axial", "azim", None), P(None, "axial", "azim", None), P())
    out_specs = P(None, "axial", "azim", None)
    return jax.shard_map(shards, mesh=mesh, in_specs=in_specs, out_specs=out_specs, check_vma=False)
```
